32 devices in a mesh: mem: 2 (over x), hid: 4 (over z), tok: 4 (over y, core).
Axes of the slice: x: 2, y: 2, z: 4, core: 2. Of those that a mesh axis runs over, the one named last changes fastest.
Arguments:
- inputs: bfloat16 [256, 12288], P(('mem', 'hid'), 'tok'), may hold values from -6 to 6
- cotangent: bfloat16 [256, 12288], P(('mem', 'hid'), 'tok'), may hold values from -1.1953125 to 1.1953125
- blocks: float32 [2, 4, 4, 144, 128, 128], P(None, None, 'hid', ('mem', 'tok')), may hold values from -0.15625 to 0.15625
- first_moment: float32 [2, 4, 4, 144, 128, 128], P(None, None, 'hid', ('mem', 'tok')), may hold values from -18 to 18
- second_moment: float32 [2, 4, 4, 144, 128, 128], P(None, None, 'hid', ('mem', 'tok')), may hold values from 4 to 100
- places: int32 [2, 4, 4, 144], P(None, 'tok', 'hid'), may hold values from 0 to 1151, as said below
- kept_counts: int32 [2, 4, 4], P(None, None, 'hid'), may hold values from 18 to 144, as said below
Outputs:
- layer_out: bfloat16 [256, 12288], P(('mem', 'hid'), 'tok')
- grad_in: bfloat16 [256, 12288], P(('mem', 'hid'), 'tok')
- new_blocks: float32 [2, 4, 4, 144, 128, 128], P(None, None, 'hid', ('mem', 'tok'))
- new_first: float32 [2, 4, 4, 144, 128, 128], P(None, None, 'hid', ('mem', 'tok'))
- new_second: float32 [2, 4, 4, 144, 128, 128], P(None, None, 'hid', ('mem', 'tok'))
The draws below stay inside these ranges and needn't reach their ends.
Inputs may be any that keep to these rules, and one draw needn't show every extreme that they name: Within each matrix and cell the 144 places are distinct. `kept_counts`: in every draw some cell of each matrix has all 144 slots live.
All inputs are finite; a program needn't handle non-finite values.
Results may differ from the reference program's by a relative error of at most 0.0015.
The reference program's roundings to bfloat16 on the way count: a program that leaves them out, or rounds other values in their place, can miss the bound.
Values may be sent and summed in bfloat16 or wider, within the bound.
No kernel may reach another device: no remote copies, remote signals or barrier semaphores. Data moves between devices by JAX's collectives and lax.ppermute only.
A program may use at most 128 MiB of HBM per device.

```python
import math
import jax
import jax.numpy as jnp
from jax import lax

D = 12288
FFW = 24576
BLK = 128
TOK_DEV = 128
STEP = 10
TOKENS = 256
CELL = 1152
SLOTS = 144
N_HID = 4
N_TOK = 4


def draw_places(key, part):
    cell_keys = jax.random.split(key, 2 * N_TOK * N_HID)

    def first_places(cell_key):
        return jax.random.permutation(cell_key, CELL)[:SLOTS]
    shuffled = jax.vmap(first_places)(cell_keys)
    return shuffled.reshape(2, N_TOK, N_HID, SLOTS).astype(jnp.int32)


def draw_kept_counts(key, part):
    lowest = max(SLOTS // 8, 1)
    counts = jax.random.randint(jax.random.fold_in(key, 11), (2, N_TOK * N_HID), lowest, SLOTS + 1)
    full_cell = jax.random.randint(jax.random.fold_in(key, 17), (2,), 0, N_TOK * N_HID)
    is_full = jnp.arange(N_TOK * N_HID)[None, :] == full_cell[:, None]
    counts = jnp.where(is_full, SLOTS, counts)
    return counts.reshape(2, N_TOK, N_HID).astype(jnp.int32)


def shard_levels(rng, dims, pieces, smallest, top_value):
    loudness = 1.0
    for dim, shards_of in pieces:
        steps = jax.random.uniform(jax.random.fold_in(jax.random.fold_in(rng, 6), dim), (shards_of,), jnp.float32, smallest / len(pieces), top_value / len(pieces))
        loudness = loudness * jnp.repeat(jnp.exp(steps), dims[dim] // shards_of).reshape((-1,) + (1,) * (len(dims) - 1 - dim))
    return loudness


def normal_values(own_key, extent, width, most, cuts=(), kind=jnp.bfloat16):
    result = width * jax.random.normal(own_key, extent, jnp.float32)
    if cuts:
        result = result * shard_levels(own_key, extent, cuts, -0.22, 0.18)
    return jnp.clip(result, -most, most).astype(kind)


def setup_inputs(seed: int = 0) -> dict:
    seeds = jax.random.split(jax.random.key(seed), 8)
    return {
        "inputs": normal_values(seeds[0], (TOKENS, D), 1.0, 6.0, ((0, 8), (1, 4))),
        "cotangent": normal_values(seeds[1], (TOKENS, D), 0.2, 1.1953125, ((0, 8), (1, 4))),
        "blocks": normal_values(seeds[2], (2, N_TOK, N_HID, SLOTS, BLK, BLK), (D // 8) ** -0.5, 0.15625, ((2, 4), (3, 8)), jnp.float32),
        "first_moment": normal_values(seeds[3], (2, N_TOK, N_HID, SLOTS, BLK, BLK), 3.0, 18.0, ((2, 4), (3, 8)), jnp.float32),
        "second_moment": jnp.clip(jnp.exp(math.log(100.0) - 3.218876 * jax.random.uniform(seeds[4], (2, N_TOK, N_HID, SLOTS, BLK, BLK), jnp.float32) ** shard_levels(seeds[4], (2, N_TOK, N_HID, SLOTS, BLK, BLK), ((2, 4), (3, 8)), -0.2, 0.2)), 4.0, 100.0),
        "places": draw_places(jax.random.fold_in(seeds[7], 71), 0),
        "kept_counts": draw_kept_counts(jax.random.fold_in(seeds[7], 71), 0),
    }


GELU_ROOT = 0.7978845608028654
GELU_CUBIC = 0.044715
BETA_FIRST = 0.9
BETA_SECOND = 0.95
LEARN_RATE = 0.001
WEIGHT_DECAY = 0.1
ADAM_EPSILON = 1e-08

def activate(values):
    tangent = jnp.tanh(GELU_ROOT * (values + GELU_CUBIC * values * values * values))
    return 0.5 * values * (1.0 + tangent)

def gelu_slope(values):
    tangent = jnp.tanh(GELU_ROOT * (values + GELU_CUBIC * values * values * values))
    return 0.5 * (1.0 + tangent) + 0.5 * values * (1.0 - tangent * tangent) * GELU_ROOT * (1.0 + 3.0 * GELU_CUBIC * values * values)

def select(matrix, slot_index, groups):
    return jnp.take(matrix.reshape(matrix.shape[0], groups, -1), slot_index, axis=1)

def spread(values, slot_index, groups, live_mask):
    masked = values * live_mask[None, :, None]
    placed = jnp.zeros((values.shape[0], groups, values.shape[2]), values.dtype).at[:, slot_index].add(masked)
    return placed.reshape(values.shape[0], -1)

def group_sum(left_rows, right_rows):
    left_rows = left_rows.reshape(TOKENS // TOK_DEV, TOK_DEV, left_rows.shape[1], left_rows.shape[2])
    right_rows = right_rows.reshape(TOKENS // TOK_DEV, TOK_DEV, right_rows.shape[1], right_rows.shape[2])
    grouped = jnp.einsum('gnsi,gnsj->gsij', left_rows, right_rows, precision=lax.Precision.HIGHEST)
    return lax.optimization_barrier(grouped.astype(jnp.bfloat16)).astype(jnp.float32).sum(axis=0)

def adam_step(weight, moment, variance, gradient, live_mask):
    new_moment = BETA_FIRST * moment + (1.0 - BETA_FIRST) * gradient
    new_variance = BETA_SECOND * variance + (1.0 - BETA_SECOND) * gradient * gradient
    scaled = new_moment / (1.0 - BETA_FIRST ** STEP) / (jnp.sqrt(new_variance / (1.0 - BETA_SECOND ** STEP)) + ADAM_EPSILON)
    new_weight = weight - LEARN_RATE * (scaled + WEIGHT_DECAY * weight)
    return (jnp.where(live_mask, new_weight, weight), jnp.where(live_mask, new_moment, moment), jnp.where(live_mask, new_variance, variance))

def reference(inputs, cotangent, blocks, first_moment, second_moment, places, kept_counts):
    block_size = blocks.shape[-1]
    width_blocks = D // (block_size * N_TOK)
    hidden_blocks = FFW // (block_size * N_HID)
    width_span = width_blocks * block_size
    hidden_span = hidden_blocks * block_size
    highest = lax.Precision.HIGHEST
    weights = lax.optimization_barrier(blocks.astype(jnp.bfloat16)).astype(jnp.float32)
    token_rows = inputs.astype(jnp.float32)
    grad_rows = cotangent.astype(jnp.float32)
    slot_ids = jnp.arange(SLOTS, dtype=jnp.int32)

    def cell_parts(matrix, tok_index, hid_index):
        place_ids = places[matrix, tok_index, hid_index].astype(jnp.int32)
        live_mask = (slot_ids < kept_counts[matrix, tok_index, hid_index]).astype(jnp.float32)
        return (place_ids % width_blocks, place_ids // width_blocks, live_mask)
    preact = jnp.zeros((TOKENS, FFW), jnp.float32)
    for tok_index in range(N_TOK):
        token_part = token_rows[:, tok_index * width_span:(tok_index + 1) * width_span]
        for hid_index in range(N_HID):
            width_index, hidden_index, live_mask = cell_parts(0, tok_index, hid_index)
            product = jnp.einsum('nsi,sij->nsj', select(token_part, width_index, width_blocks), weights[0, tok_index, hid_index], precision=highest)
            cell_part = spread(product, hidden_index, hidden_blocks, live_mask)
            preact = preact.at[:, hid_index * hidden_span:(hid_index + 1) * hidden_span].add(cell_part)
    hidden = lax.optimization_barrier(activate(preact).astype(jnp.bfloat16)).astype(jnp.float32)
    layer_out = jnp.zeros((TOKENS, D), jnp.float32)
    hidden_grad = jnp.zeros((TOKENS, FFW), jnp.float32)
    for tok_index in range(N_TOK):
        grad_part = grad_rows[:, tok_index * width_span:(tok_index + 1) * width_span]
        for hid_index in range(N_HID):
            hidden_part = hidden[:, hid_index * hidden_span:(hid_index + 1) * hidden_span]
            width_index, hidden_index, live_mask = cell_parts(1, tok_index, hid_index)
            forward = jnp.einsum('nsi,sij->nsj', select(hidden_part, hidden_index, hidden_blocks), weights[1, tok_index, hid_index], precision=highest)
            layer_out = layer_out.at[:, tok_index * width_span:(tok_index + 1) * width_span].add(spread(forward, width_index, width_blocks, live_mask))
            backward = jnp.einsum('nsj,sij->nsi', select(grad_part, width_index, width_blocks), weights[1, tok_index, hid_index], precision=highest)
            hidden_grad = hidden_grad.at[:, hid_index * hidden_span:(hid_index + 1) * hidden_span].add(spread(backward, hidden_index, hidden_blocks, live_mask))
    pre_grad = lax.optimization_barrier((hidden_grad * gelu_slope(preact)).astype(jnp.bfloat16)).astype(jnp.float32)
    grad_in = jnp.zeros((TOKENS, D), jnp.float32)
    weight_rows, first_rows, second_rows = ([], [], [])
    for matrix in range(2):
        weight_rows.append([])
        first_rows.append([])
        second_rows.append([])
    for tok_index in range(N_TOK):
        token_part = token_rows[:, tok_index * width_span:(tok_index + 1) * width_span]
        grad_part = grad_rows[:, tok_index * width_span:(tok_index + 1) * width_span]
        cell_lists = [([], [], []), ([], [], [])]
        for hid_index in range(N_HID):
            hidden_part = hidden[:, hid_index * hidden_span:(hid_index + 1) * hidden_span]
            pre_part = pre_grad[:, hid_index * hidden_span:(hid_index + 1) * hidden_span]
            width_index, hidden_index, live_mask = cell_parts(0, tok_index, hid_index)
            pre_cols = select(pre_part, hidden_index, hidden_blocks)
            backward = jnp.einsum('nsj,sij->nsi', pre_cols, weights[0, tok_index, hid_index], precision=highest)
            grad_in = grad_in.at[:, tok_index * width_span:(tok_index + 1) * width_span].add(spread(backward, width_index, width_blocks, live_mask))
            first_grad = group_sum(select(token_part, width_index, width_blocks), pre_cols)
            updated = adam_step(blocks[0, tok_index, hid_index], first_moment[0, tok_index, hid_index], second_moment[0, tok_index, hid_index], first_grad, live_mask[:, None, None] > 0.5)
            for member in range(3):
                cell_lists[0][member].append(updated[member])
            width_index, hidden_index, live_mask = cell_parts(1, tok_index, hid_index)
            second_grad = group_sum(select(hidden_part, hidden_index, hidden_blocks), select(grad_part, width_index, width_blocks))
            updated = adam_step(blocks[1, tok_index, hid_index], first_moment[1, tok_index, hid_index], second_moment[1, tok_index, hid_index], second_grad, live_mask[:, None, None] > 0.5)
            for member in range(3):
                cell_lists[1][member].append(updated[member])
        for matrix in range(2):
            weight_rows[matrix].append(jnp.stack(cell_lists[matrix][0]))
            first_rows[matrix].append(jnp.stack(cell_lists[matrix][1]))
            second_rows[matrix].append(jnp.stack(cell_lists[matrix][2]))
    new_blocks = jnp.stack([jnp.stack(weight_rows[matrix]) for matrix in range(2)])
    new_first = jnp.stack([jnp.stack(first_rows[matrix]) for matrix in range(2)])
    new_second = jnp.stack([jnp.stack(second_rows[matrix]) for matrix in range(2)])
    return (layer_out.astype(jnp.bfloat16), grad_in.astype(jnp.bfloat16), new_blocks, new_first, new_second)
```

```python
import functools

import jax
import jax.numpy as jnp
from jax import lax
from jax.experimental import pallas as pl
from jax.experimental.pallas import tpu as pltpu
from jax.sharding import PartitionSpec as P

FFW = 24576
STEP = 10


GELU_ROOT = 0.7978845608028654
GELU_CUBIC = 0.044715
BETA_FIRST = 0.9
BETA_SECOND = 0.95
LEARN_RATE = 0.001
WEIGHT_DECAY = 0.1
ADAM_EPSILON = 1e-08
VMEM_BYTES = 56 * 2**20
UNROLL = 4


def activate(values):
    tangent = jnp.tanh(GELU_ROOT * (values + GELU_CUBIC * values * values * values))
    return 0.5 * values * (1.0 + tangent)


def gelu_slope(values):
    tangent = jnp.tanh(GELU_ROOT * (values + GELU_CUBIC * values * values * values))
    return 0.5 * (1.0 + tangent) + 0.5 * values * (1.0 - tangent * tangent) * GELU_ROOT * (
        1.0 + 3.0 * GELU_CUBIC * values * values
    )


def adam_step(weight, moment, variance, gradient):
    new_moment = BETA_FIRST * moment + (1.0 - BETA_FIRST) * gradient
    new_variance = BETA_SECOND * variance + (1.0 - BETA_SECOND) * gradient * gradient
    scaled = (
        new_moment
        / (1.0 - BETA_FIRST**STEP)
        / (jnp.sqrt(new_variance / (1.0 - BETA_SECOND**STEP)) + ADAM_EPSILON)
    )
    new_weight = weight - LEARN_RATE * (scaled + WEIGHT_DECAY * weight)
    return new_weight, new_moment, new_variance


def dot(left, right, left_dim, right_dim):
    return lax.dot_general(
        left, right, (((left_dim,), (right_dim,)), ((), ())), preferred_element_type=jnp.float32
    )


def lanes(index, size):
    return pl.ds(pl.multiple_of(index * size, size), size)


def live_range(kept_ref, matrix, local_slots):
    first = lax.axis_index("mem") * local_slots
    count = jnp.clip(kept_ref[matrix, lax.axis_index("tok")] - first, 0, local_slots)
    return first, count


def over_slots(count, body):
    groups = count // UNROLL

    def run(group, carry):
        body([group * UNROLL + lane for lane in range(UNROLL)])
        return carry

    lax.fori_loop(0, groups, run, 0)

    def single(slot, carry):
        body([slot])
        return carry

    lax.fori_loop(groups * UNROLL, count, single, 0)


def relative(tok_count):
    tok = lax.axis_index("tok")
    return (tok % 2) * (tok_count // 2) + tok // 2


def forward_kernel(
    matrix, transposed, width_blocks, tok_count, hid_count, mem_count, kept_ref, place_ref, *refs
):
    own_refs, (weight_ref, row_ref, keep_ref, send_ref) = refs[:mem_count], refs[mem_count:]
    half = keep_ref.shape[1]
    size = weight_ref.shape[-1]
    rows = own_refs[0].shape[0]
    step = rows // hid_count
    part = rows // tok_count
    turn = relative(tok_count)
    for group in range(mem_count):
        for block in range(hid_count):
            start = block * step
            spot = ((start // part) ^ turn) * part + start % part + group * rows
            row_ref[pl.ds(pl.multiple_of(spot, step), step), :] = own_refs[group][
                start : start + step, :
            ]
    keep_ref[...] = jnp.zeros(keep_ref.shape, jnp.float32)
    send_ref[...] = jnp.zeros(send_ref.shape, jnp.float32)
    first, count = live_range(kept_ref, matrix, weight_ref.shape[0])

    def body(slots):
        found = []
        for slot in slots:
            place = place_ref[matrix, first + slot]
            left = row_ref[:, lanes(place % width_blocks, size)]
            product = dot(left, weight_ref[slot], 1, 1 if transposed else 0)
            found.append((lanes(place // width_blocks, size), product))
        for spot, product in found:
            for group in range(mem_count):
                start = group * rows
                keep_ref[group, :, spot] += product[start : start + half]
                send_ref[group, :, spot] += product[start + half : start + rows]

    over_slots(count, body)


def backward_kernel(
    matrix, transposed, width_blocks, mem_count, kept_ref, place_ref, own_ref, pair_ref, weight_ref, *out_refs
):
    size = weight_ref.shape[-1]
    half = own_ref.shape[1]
    for out_ref in out_refs:
        out_ref[...] = jnp.zeros(out_ref.shape, jnp.float32)
    first, count = live_range(kept_ref, matrix, weight_ref.shape[0])

    def body(slots):
        found = []
        for slot in slots:
            place = place_ref[matrix, first + slot]
            spot = lanes(place // width_blocks, size)
            pieces = []
            for group in range(mem_count):
                pieces += [own_ref[group, :, spot], pair_ref[group, :, spot]]
            product = dot(
                jnp.concatenate(pieces, axis=0), weight_ref[slot], 1, 1 if transposed else 0
            )
            found.append((lanes(place % width_blocks, size), product))
        for spot, product in found:
            for group, out_ref in enumerate(out_refs):
                out_ref[:, spot] += product[group * 2 * half : (group + 1) * 2 * half]

    over_slots(count, body)


def gradient_kernel(
    matrix, width_blocks, mem_count, kept_ref, place_ref, row_ref, own_ref, pair_ref, out_ref
):
    size = out_ref.shape[-1]
    rows = row_ref.shape[0] // mem_count
    first, count = live_range(kept_ref, matrix, out_ref.shape[0])

    def body(slots):
        for slot in slots:
            place = place_ref[matrix, first + slot]
            hidden = lanes(place // width_blocks, size)
            width = lanes(place % width_blocks, size)
            total = None
            for group in range(mem_count):
                wide = row_ref[group * rows : (group + 1) * rows, width]
                deep = jnp.concatenate(
                    [own_ref[group, :, hidden], pair_ref[group, :, hidden]], axis=0
                )
                left, right = (wide, deep) if matrix == 0 else (deep, wide)
                term = dot(left, right, 0, 0).astype(jnp.bfloat16).astype(jnp.float32)
                total = term if total is None else total + term
            out_ref[slot] = total

    over_slots(count, body)

    def clear(slot, carry):
        out_ref[slot] = jnp.zeros(out_ref.shape[1:], jnp.float32)
        return carry

    lax.fori_loop(count, out_ref.shape[0], clear, 0)


def adam_kernel(matrix, tok_count, kept_ref, grad_ref, weight_ref, moment_ref, variance_ref, *refs):
    out_refs = refs[-3:]
    cell = pl.program_id(0)
    owned = weight_ref.shape[3]
    first = (lax.axis_index("mem") * tok_count + lax.axis_index("tok")) * owned
    count = jnp.clip(kept_ref[matrix, cell] - first, 0, owned)

    def update(slot, carry):
        at = (0, 0, 0, slot)
        fresh = adam_step(weight_ref[at], moment_ref[at], variance_ref[at], grad_ref[0, slot])
        for out_ref, value in zip(out_refs, fresh):
            out_ref[at] = value
        return carry

    lax.fori_loop(0, count, update, 0)

    def keep(slot, carry):
        at = (0, 0, 0, slot)
        for out_ref, value_ref in zip(out_refs, (weight_ref, moment_ref, variance_ref)):
            out_ref[at] = value_ref[at]
        return carry

    lax.fori_loop(count, owned, keep, 0)


SCALARS = pl.BlockSpec(memory_space=pltpu.SMEM)
WHOLE = pl.BlockSpec(memory_space=pltpu.VMEM)
ANYWHERE = pl.BlockSpec(memory_space=pl.ANY)


def call(kernel, name, outs, scalars, arrays, flops):
    moved = sum(a.size * a.dtype.itemsize for a in arrays)
    moved += sum(math_size(o) for o in outs)
    return pl.pallas_call(
        kernel,
        out_shape=outs,
        in_specs=[SCALARS] * len(scalars) + [WHOLE] * len(arrays),
        out_specs=[WHOLE] * len(outs),
        compiler_params=pltpu.CompilerParams(vmem_limit_bytes=VMEM_BYTES),
        cost_estimate=pl.CostEstimate(flops=flops, bytes_accessed=moved, transcendentals=0),
        name=name,
    )(*scalars, *arrays)


def math_size(shape):
    total = shape.dtype.itemsize
    for dim in shape.shape:
        total *= dim
    return total


def on_device(inputs, cotangent, blocks, first_moment, second_moment, places, kept_counts):
    mem_count = lax.axis_size("mem")
    tok_count = lax.axis_size("tok")
    hid_count = lax.axis_size("hid")
    block_size = blocks.shape[-1]
    owned_slots = blocks.shape[3]
    local_slots = owned_slots * tok_count
    width_blocks = inputs.shape[1] // block_size
    hidden_span = FFW // hid_count
    rows = inputs.shape[0] * hid_count
    other = tok_count // 2
    half = rows // 2
    part = rows // tok_count
    kept = kept_counts[:, :, 0]
    place_ids = places[:, 0, 0]
    scalars = (kept, place_ids)
    f32, bf16 = jnp.float32, jnp.bfloat16

    def shift_hid(array, shift):
        return lax.ppermute(array, "hid", [(i, (i + shift) % hid_count) for i in range(hid_count)])

    def shift_mem(array, shift):
        return lax.ppermute(array, "mem", [(i, (i + shift) % mem_count) for i in range(mem_count)])

    def pair(array):
        return lax.ppermute(array, "tok", [(i, i ^ 1) for i in range(tok_count)])

    def across(array, mem_shift, tok_shift):
        table = []
        for m in range(mem_count):
            for t in range(tok_count):
                to = ((m - mem_shift) % mem_count) * tok_count + (t ^ (2 * tok_shift))
                table.append((m * tok_count + t, to))
        return lax.ppermute(array, ("mem", "tok"), table)

    peers = [(j, b) for j in range(mem_count) for b in range(other)][1:]

    def gather_rows(array):
        pieces = [array] + [shift_hid(array, k) for k in range(1, hid_count)]
        near = jnp.concatenate(pieces, axis=0)
        return [near] + [shift_mem(near, j) for j in range(1, mem_count)]

    def gather_weights(matrix):
        narrow = blocks[matrix, :, 0].astype(bf16)
        moved = lax.all_to_all(narrow, "tok", split_axis=0, concat_axis=0, tiled=True)
        return moved.reshape(local_slots, block_size, block_size)

    def forward(matrix, transposed, row_groups, weights):
        kernel = functools.partial(
            forward_kernel, matrix, transposed, width_blocks, tok_count, hid_count, mem_count
        )
        width = row_groups[0].shape[1]
        outs = [
            jax.ShapeDtypeStruct((mem_count * rows, width), bf16),
            jax.ShapeDtypeStruct((mem_count, half, hidden_span), f32),
            jax.ShapeDtypeStruct((mem_count, half, hidden_span), f32),
        ]
        flops = 2 * mem_count * rows * local_slots * block_size * block_size
        return call(kernel, f"forward_{matrix}", outs, scalars, [*row_groups, weights], flops)

    def reduce_plane(keep, send):
        total = (keep + pair(send)).reshape(mem_count, other, part, hidden_span)
        result = total[0, 0]
        for j, b in peers:
            result = result + across(total[j, b], j, b)
        return result

    def gather_plane(piece):
        found = {(0, 0): piece}
        for j, b in peers:
            found[(-j) % mem_count, b] = across(piece, j, b)
        near = jnp.concatenate(
            [found[j, b] for j in range(mem_count) for b in range(other)], axis=0
        ).reshape(mem_count, half, hidden_span)
        return near, pair(near)

    def backward(matrix, transposed, near, far, weights):
        kernel = functools.partial(backward_kernel, matrix, transposed, width_blocks, mem_count)
        outs = [jax.ShapeDtypeStruct((rows, width_blocks * block_size), f32)] * mem_count
        flops = 2 * mem_count * rows * local_slots * block_size * block_size
        return call(kernel, f"backward_{matrix}", outs, scalars, [near, far, weights], flops)

    turn = relative(tok_count)
    step = inputs.shape[0]

    def reduce_rows(groups):
        total = groups[0]
        for j in range(1, mem_count):
            total = total + shift_mem(groups[j], -j)
        result = None
        for k in range(hid_count):
            start = k * step
            spot = ((start // part) ^ turn) * part + start % part
            piece = lax.dynamic_slice_in_dim(total, spot, step, 0)
            if k:
                piece = shift_hid(piece, -k)
            result = piece if result is None else result + piece
        return result.astype(bf16)

    def gradient(matrix, row_values, near, far):
        kernel = functools.partial(gradient_kernel, matrix, width_blocks, mem_count)
        outs = [jax.ShapeDtypeStruct((local_slots, block_size, block_size), f32)]
        flops = 2 * mem_count * rows * local_slots * block_size * block_size
        (found,) = call(
            kernel, f"gradient_{matrix}", outs, scalars, [row_values, near, far], flops
        )
        sendable = found.reshape(tok_count, owned_slots, block_size, block_size)
        return lax.all_to_all(sendable, "tok", split_axis=0, concat_axis=0, tiled=True)

    def update(matrix, grads, held):
        state_spec = pl.BlockSpec(
            (1, 1, 1, owned_slots, block_size, block_size), lambda i: (matrix, i, 0, 0, 0, 0)
        )
        grad_spec = pl.BlockSpec((1, owned_slots, block_size, block_size), lambda i: (i, 0, 0, 0))
        state = (blocks, first_moment, second_moment)
        return pl.pallas_call(
            functools.partial(adam_kernel, matrix, tok_count),
            grid=(tok_count,),
            out_shape=[jax.ShapeDtypeStruct(s.shape, f32) for s in state],
            in_specs=[SCALARS, grad_spec] + [state_spec] * 3 + [ANYWHERE] * len(held),
            out_specs=[state_spec] * 3,
            input_output_aliases={5 + i: i for i in range(len(held))},
            compiler_params=pltpu.CompilerParams(vmem_limit_bytes=VMEM_BYTES),
            cost_estimate=pl.CostEstimate(
                flops=grads.size * 12, bytes_accessed=grads.size * 28, transcendentals=grads.size
            ),
            name=f"update_{matrix}",
        )(kept, grads, *state, *held)

    input_groups = gather_rows(inputs)
    weights_first = gather_weights(0)
    cotangent_groups = gather_rows(cotangent)
    weights_second = gather_weights(1)
    token_rows, *pre_part = forward(0, False, input_groups, weights_first)
    preact = reduce_plane(*pre_part)
    grad_rows, *back_part = forward(1, True, cotangent_groups, weights_second)
    hidden = gather_plane(activate(preact).astype(bf16))
    hidden_grad = reduce_plane(*back_part)
    pre_grad = gather_plane((hidden_grad * gelu_slope(preact)).astype(bf16))
    layer_out = reduce_rows(backward(1, False, *hidden, weights_second))
    second_grad = gradient(1, grad_rows, *hidden)
    grad_in = reduce_rows(backward(0, True, *pre_grad, weights_first))
    first_grad = gradient(0, token_rows, *pre_grad)
    held = update(1, second_grad, ())
    return (layer_out, grad_in, *update(0, first_grad, held))


def solution(mesh):
    return jax.shard_map(
        on_device,
        mesh=mesh,
        in_specs=(
            P(("mem", "hid"), "tok"),
            P(("mem", "hid"), "tok"),
            P(None, None, "hid", ("mem", "tok"), None, None),
            P(None, None, "hid", ("mem", "tok"), None, None),
            P(None, None, "hid", ("mem", "tok"), None, None),
            P(None, "tok", "hid", None),
            P(None, None, "hid"),
        ),
        out_specs=(
            P(("mem", "hid"), "tok"),
            P(("mem", "hid"), "tok"),
            P(None, None, "hid", ("mem", "tok"), None, None),
            P(None, None, "hid", ("mem", "tok"), None, None),
            P(None, None, "hid", ("mem", "tok"), None, None),
        ),
        check_vma=False,
    )
```

```python
import functools

import jax
import jax.numpy as jnp
from jax import lax
from jax.experimental import pallas as pl
from jax.experimental.pallas import tpu as pltpu
from jax.sharding import PartitionSpec as P


FFW = 24576
STEP = 10


GELU_ROOT = 0.7978845608028654
GELU_CUBIC = 0.044715
BETA_FIRST = 0.9
BETA_SECOND = 0.95
LEARN_RATE = 0.001
WEIGHT_DECAY = 0.1
ADAM_EPSILON = 1e-08
VMEM_BYTES = 56 * 2**20
UNROLL = 4
CHUNKS = 2


def activate(values):
    tangent = jnp.tanh(GELU_ROOT * (values + GELU_CUBIC * values * values * values))
    return 0.5 * values * (1.0 + tangent)


def gelu_slope(values):
    tangent = jnp.tanh(GELU_ROOT * (values + GELU_CUBIC * values * values * values))
    return 0.5 * (1.0 + tangent) + 0.5 * values * (1.0 - tangent * tangent) * GELU_ROOT * (
        1.0 + 3.0 * GELU_CUBIC * values * values
    )


def adam_step(weight, moment, variance, gradient):
    new_moment = BETA_FIRST * moment + (1.0 - BETA_FIRST) * gradient
    new_variance = BETA_SECOND * variance + (1.0 - BETA_SECOND) * gradient * gradient
    scaled = (
        new_moment
        / (1.0 - BETA_FIRST**STEP)
        / (jnp.sqrt(new_variance / (1.0 - BETA_SECOND**STEP)) + ADAM_EPSILON)
    )
    new_weight = weight - LEARN_RATE * (scaled + WEIGHT_DECAY * weight)
    return new_weight, new_moment, new_variance


def dot(left, right, left_dim, right_dim):
    return lax.dot_general(
        left, right, (((left_dim,), (right_dim,)), ((), ())), preferred_element_type=jnp.float32
    )


def lanes(index, size):
    return pl.ds(pl.multiple_of(index * size, size), size)


def live_range(kept_ref, matrix, local_slots):
    first = lax.axis_index("mem") * local_slots
    count = jnp.clip(kept_ref[matrix, lax.axis_index("tok")] - first, 0, local_slots)
    return first, count


def over_slots(count, body):
    groups = count // UNROLL

    def run(group, carry):
        body([group * UNROLL + lane for lane in range(UNROLL)])
        return carry

    lax.fori_loop(0, groups, run, 0)

    def single(slot, carry):
        body([slot])
        return carry

    lax.fori_loop(groups * UNROLL, count, single, 0)


def relative(tok_count):
    tok = lax.axis_index("tok")
    return (tok % 2) * (tok_count // 2) + tok // 2


def forward_kernel(
    matrix, transposed, width_blocks, tok_count, hid_count, mem_count, kept_ref, place_ref, *refs
):
    own_refs, (weight_ref, row_ref, keep_ref, send_ref) = refs[:mem_count], refs[mem_count:]
    half = keep_ref.shape[1]
    size = weight_ref.shape[-1]
    rows = own_refs[0].shape[0]
    step = rows // hid_count
    part = rows // tok_count
    turn = relative(tok_count)
    for group in range(mem_count):
        for block in range(hid_count):
            start = block * step
            spot = ((start // part) ^ turn) * part + start % part + group * rows
            row_ref[pl.ds(pl.multiple_of(spot, step), step), :] = own_refs[group][
                start : start + step, :
            ]
    keep_ref[...] = jnp.zeros(keep_ref.shape, jnp.float32)
    send_ref[...] = jnp.zeros(send_ref.shape, jnp.float32)
    first, count = live_range(kept_ref, matrix, weight_ref.shape[0])

    def body(slots):
        found = []
        for slot in slots:
            place = place_ref[matrix, first + slot]
            left = row_ref[:, lanes(place % width_blocks, size)]
            product = dot(left, weight_ref[slot], 1, 1 if transposed else 0)
            found.append((lanes(place // width_blocks, size), product))
        for spot, product in found:
            for group in range(mem_count):
                start = group * rows
                keep_ref[group, :, spot] += product[start : start + half]
                send_ref[group, :, spot] += product[start + half : start + rows]

    over_slots(count, body)


def backward_kernel(
    matrix,
    transposed,
    width_blocks,
    mem_count,
    kept_ref,
    place_ref,
    own_ref,
    pair_ref,
    weight_ref,
    *refs,
):
    out_refs, total_ref = refs[:-1], refs[-1]
    size = weight_ref.shape[-1]
    half = own_ref.shape[1]
    total_ref[...] = jnp.zeros(total_ref.shape, jnp.float32)
    first, count = live_range(kept_ref, matrix, weight_ref.shape[0])

    def body(slots):
        found = []
        for slot in slots:
            place = place_ref[matrix, first + slot]
            spot = lanes(place // width_blocks, size)
            pieces = []
            for group in range(mem_count):
                pieces += [own_ref[group, :, spot], pair_ref[group, :, spot]]
            product = dot(
                jnp.concatenate(pieces, axis=0), weight_ref[slot], 1, 1 if transposed else 0
            )
            found.append((lanes(place % width_blocks, size), product))
        for spot, product in found:
            total_ref[:, spot] += product

    over_slots(count, body)
    for index, out_ref in enumerate(out_refs):
        chunk, group = index // mem_count, index % mem_count
        span = out_ref.shape[1]
        out_ref[...] = total_ref[
            group * 2 * half : (group + 1) * 2 * half, chunk * span : (chunk + 1) * span
        ]


def owner_count(kept_ref, matrix, cell, owner, owned):
    first = (lax.axis_index("mem") * lax.axis_size("tok") + owner) * owned
    return first, jnp.clip(kept_ref[matrix, cell] - first, 0, owned)


def gradient_kernel(matrix, width_blocks, mem_count, hid_count, kept_ref, place_ref, far_place_ref, *refs):
    row_ref, own_ref, pair_ref = refs[:3]
    late_refs = refs[3 : 3 + hid_count]
    keep_ref, send_ref, late_ref = refs[3 + hid_count :]
    cells, owned, size = keep_ref.shape[:3]
    tok_count = lax.axis_size("tok")
    tok = lax.axis_index("tok")
    rows = row_ref.shape[0] // mem_count
    part = rows // tok_count
    step = rows // hid_count
    turn = relative(tok_count)
    for block, source in enumerate(late_refs):
        start = block * step
        spot = ((start // part) ^ turn) * part + start % part
        for group in range(mem_count):
            late_ref[pl.ds(pl.multiple_of(spot + group * rows, step), step), :] = source[matrix, group]

    for cell in range(cells):
        places, values = ((place_ref, row_ref), (far_place_ref, late_ref))[cell]
        for side, out_ref in enumerate((keep_ref, send_ref)):
            first, count = owner_count(kept_ref, matrix, tok ^ (2 * cell), tok ^ side, owned)

            def body(slots):
                for slot in slots:
                    place = places[matrix, first + slot]
                    hidden = lanes(place // width_blocks, size)
                    width = lanes(place % width_blocks, size)
                    total = None
                    for group in range(mem_count):
                        wide = values[group * rows : (group + 1) * rows, width]
                        deep = jnp.concatenate(
                            [own_ref[group, :, hidden], pair_ref[group, :, hidden]], axis=0
                        )
                        left, right = (wide, deep) if matrix == 0 else (deep, wide)
                        term = dot(left, right, 0, 0).astype(jnp.bfloat16).astype(jnp.float32)
                        total = term if total is None else total + term
                    out_ref[cell, slot] = total

            over_slots(count, body)

            def clear(slot, carry):
                out_ref[cell, slot] = jnp.zeros((size, size), jnp.float32)
                return carry

            lax.fori_loop(count, owned, clear, 0)


def update_kernel(matrix, kept_ref, keep_ref, swap_ref, weight_ref, moment_ref, variance_ref, *refs):
    out_refs = refs[-3:]
    turn = pl.program_id(0)
    tok = lax.axis_index("tok")
    owned = weight_ref.shape[3]
    _, count = owner_count(kept_ref, matrix, tok ^ turn, tok, owned)

    def update_from(grad_ref):
        def update(slot, carry):
            at = (0, 0, 0, slot)
            fresh = adam_step(weight_ref[at], moment_ref[at], variance_ref[at], grad_ref[0, slot])
            for out_ref, value in zip(out_refs, fresh):
                out_ref[at] = value
            return carry

        lax.fori_loop(0, count, update, 0)

    pl.when(turn % 2 == 0)(functools.partial(update_from, keep_ref))
    pl.when(turn % 2 == 1)(functools.partial(update_from, swap_ref))

    def keep(slot, carry):
        at = (0, 0, 0, slot)
        for out_ref, value_ref in zip(out_refs, (weight_ref, moment_ref, variance_ref)):
            out_ref[at] = value_ref[at]
        return carry

    lax.fori_loop(count, owned, keep, 0)


def join_kernel(keep_ref, swap_ref, *out_refs):
    groups = keep_ref.shape[0]
    part = out_refs[0].shape[0]
    for index, out_ref in enumerate(out_refs):
        group, start = index % groups, index // groups * part
        out_ref[...] = keep_ref[group, start : start + part] + swap_ref[group, start : start + part]


def total_of(refs):
    total = refs[0][...]
    for ref in refs[1:]:
        total = total + ref[...]
    return total


def activate_kernel(*refs):
    *part_refs, hidden_ref, preact_ref = refs
    preact = total_of(part_refs)
    preact_ref[...] = preact
    hidden_ref[...] = activate(preact).astype(jnp.bfloat16)


def slope_kernel(*refs):
    *part_refs, preact_ref, out_ref = refs
    out_ref[...] = (total_of(part_refs) * gelu_slope(preact_ref[...])).astype(jnp.bfloat16)


def narrow_kernel(block_ref, out_ref):
    out_ref[...] = block_ref[0, :, 0].astype(jnp.bfloat16)


SCALARS = pl.BlockSpec(memory_space=pltpu.SMEM)
WHOLE = pl.BlockSpec(memory_space=pltpu.VMEM)
ANYWHERE = pl.BlockSpec(memory_space=pl.ANY)


def call(kernel, outs, scalars, arrays, flops, scratch=()):
    moved = sum(a.size * a.dtype.itemsize for a in arrays)
    moved += sum(math_size(o) for o in outs)
    return pl.pallas_call(
        kernel,
        out_shape=outs,
        in_specs=[SCALARS] * len(scalars) + [WHOLE] * len(arrays),
        out_specs=[WHOLE] * len(outs),
        scratch_shapes=scratch,
        compiler_params=pltpu.CompilerParams(vmem_limit_bytes=VMEM_BYTES),
        cost_estimate=pl.CostEstimate(flops=flops, bytes_accessed=moved, transcendentals=0),
    )(*scalars, *arrays)


def math_size(shape):
    total = shape.dtype.itemsize
    for dim in shape.shape:
        total *= dim
    return total


def on_device(inputs, cotangent, blocks, first_moment, second_moment, places, kept_counts):
    mem_count = lax.axis_size("mem")
    tok_count = lax.axis_size("tok")
    hid_count = lax.axis_size("hid")
    block_size = blocks.shape[-1]
    owned_slots = blocks.shape[3]
    local_slots = owned_slots * tok_count
    width_blocks = inputs.shape[1] // block_size
    hidden_span = FFW // hid_count
    rows = inputs.shape[0] * hid_count
    other = tok_count // 2
    half = rows // 2
    part = rows // tok_count
    chunks = CHUNKS
    kept = kept_counts[:, :, 0]
    place_ids = places[:, 0, 0]
    scalars = (kept, place_ids)
    f32, bf16 = jnp.float32, jnp.bfloat16

    def shift_hid(array, shift):
        return lax.ppermute(array, "hid", [(i, (i + shift) % hid_count) for i in range(hid_count)])

    def shift_mem(array, shift):
        return lax.ppermute(array, "mem", [(i, (i + shift) % mem_count) for i in range(mem_count)])

    def flip_tok(array, bit):
        return lax.ppermute(array, "tok", [(i, i ^ bit) for i in range(tok_count)])

    def across(array, mem_shift, tok_shift):
        table = []
        for m in range(mem_count):
            for t in range(tok_count):
                to = ((m - mem_shift) % mem_count) * tok_count + (t ^ (2 * tok_shift))
                table.append((m * tok_count + t, to))
        return lax.ppermute(array, ("mem", "tok"), table)

    peers = [(j, b) for j in range(mem_count) for b in range(other)][1:]

    def gather_rows(array):
        pieces = [array] + [shift_hid(array, k) for k in range(1, hid_count)]
        near = jnp.concatenate(pieces, axis=0)
        return [near] + [shift_mem(near, j) for j in range(1, mem_count)]

    def gather_late():
        both = flip_tok(jnp.stack([inputs, cotangent]), 2)
        found = [both] + [shift_mem(both, j) for j in range(1, mem_count)]
        moved = jnp.stack(found, axis=1)
        return [moved] + [shift_hid(moved, k) for k in range(1, hid_count)]

    def gather_weights(matrix):
        shape = (tok_count, owned_slots, block_size, block_size)
        narrow = pl.pallas_call(
            narrow_kernel,
            grid=(tok_count,),
            out_shape=jax.ShapeDtypeStruct(shape, bf16),
            in_specs=[
                pl.BlockSpec((1, 1, 1) + blocks.shape[3:], lambda i: (matrix, i, 0, 0, 0, 0))
            ],
            out_specs=pl.BlockSpec((1,) + shape[1:], lambda i: (i, 0, 0, 0)),
            compiler_params=pltpu.CompilerParams(vmem_limit_bytes=VMEM_BYTES),
        )(blocks)
        moved = lax.all_to_all(narrow, "tok", split_axis=0, concat_axis=0, tiled=True)
        return moved.reshape(local_slots, block_size, block_size)

    def forward(matrix, transposed, row_groups, weights):
        kernel = functools.partial(
            forward_kernel, matrix, transposed, width_blocks, tok_count, hid_count, mem_count
        )
        width = row_groups[0].shape[1]
        outs = [
            jax.ShapeDtypeStruct((mem_count * rows, width), bf16),
            jax.ShapeDtypeStruct((mem_count, half, hidden_span), f32),
            jax.ShapeDtypeStruct((mem_count, half, hidden_span), f32),
        ]
        flops = 2 * mem_count * rows * local_slots * block_size * block_size
        return call(kernel, outs, scalars, [*row_groups, weights], flops)

    def over_columns(kernel, outs, arrays, steps):
        def spec(shape):
            lead = len(shape) - 1
            return pl.BlockSpec(
                tuple(shape[:-1]) + (shape[-1] // steps,), lambda i: (0,) * lead + (i,)
            )

        return pl.pallas_call(
            kernel,
            grid=(steps,),
            out_shape=outs,
            in_specs=[spec(a.shape) for a in arrays],
            out_specs=[spec(o.shape) for o in outs],
            compiler_params=pltpu.CompilerParams(vmem_limit_bytes=VMEM_BYTES),
            cost_estimate=pl.CostEstimate(
                flops=sum(o.size for o in outs) * 4,
                bytes_accessed=sum(a.size * a.dtype.itemsize for a in (*arrays, *outs)),
                transcendentals=0,
            ),
        )(*arrays)

    def reduce_plane(keep, send):
        outs = [jax.ShapeDtypeStruct((part, hidden_span), f32)] * (mem_count * other)
        swap = flip_tok(send, 1)
        found = over_columns(join_kernel, outs, [keep, swap], 4)
        terms = [found[0]]
        for j, b in peers:
            terms.append(across(found[b * mem_count + j], j, b))
        return terms

    def gather_plane(piece):
        found = {(0, 0): piece}
        for j, b in peers:
            found[(-j) % mem_count, b] = across(piece, j, b)
        near = jnp.concatenate(
            [found[j, b] for j in range(mem_count) for b in range(other)], axis=0
        ).reshape(mem_count, half, hidden_span)
        return near, flip_tok(near, 1)

    def backward(matrix, transposed, near, far, weights):
        kernel = functools.partial(backward_kernel, matrix, transposed, width_blocks, mem_count)
        span = inputs.shape[1] // chunks
        outs = [jax.ShapeDtypeStruct((rows, span), f32)] * (mem_count * chunks)
        flops = 2 * mem_count * rows * local_slots * block_size * block_size
        scratch = [pltpu.VMEM((mem_count * rows, inputs.shape[1]), f32)]
        return call(kernel, outs, scalars, [near, far, weights], flops, scratch)

    turn = relative(tok_count)
    step = inputs.shape[0]

    def reduce_rows(found):
        results = []
        for chunk in range(chunks):
            groups = found[chunk * mem_count : (chunk + 1) * mem_count]
            total = groups[0]
            for j in range(1, mem_count):
                total = total + shift_mem(groups[j], -j)
            result = None
            for k in range(hid_count):
                start = k * step
                spot = ((start // part) ^ turn) * part + start % part
                piece = lax.dynamic_slice_in_dim(total, spot, step, 0)
                if k:
                    piece = shift_hid(piece, -k)
                result = piece if result is None else result + piece
            results.append(result.astype(bf16))
        return jnp.concatenate(results, axis=1)

    def gradient(matrix, row_values, near, far, late):
        kernel = functools.partial(gradient_kernel, matrix, width_blocks, mem_count, hid_count)
        outs = [
            jax.ShapeDtypeStruct((other, owned_slots, block_size, block_size), f32),
            jax.ShapeDtypeStruct((other, owned_slots, block_size, block_size), f32),
        ]
        flops = 2 * mem_count * rows * local_slots * block_size * block_size
        keep, send = call(
            kernel,
            outs,
            (kept, place_ids, far_place_ids),
            [row_values, near, far, *late],
            flops,
            [pltpu.VMEM(row_values.shape, bf16)],
        )
        return keep, flip_tok(send, 1)

    def update(matrix, grads, held):
        state_shape = (1, 1, 1, owned_slots, block_size, block_size)
        state_spec = pl.BlockSpec(state_shape, lambda i: (matrix, lax.axis_index("tok") ^ i, 0, 0, 0, 0))
        grad_spec = pl.BlockSpec((1, owned_slots, block_size, block_size), lambda i: (i // 2, 0, 0, 0))
        state = (blocks, first_moment, second_moment)
        size = local_slots * block_size * block_size
        return pl.pallas_call(
            functools.partial(update_kernel, matrix),
            grid=(tok_count,),
            out_shape=[jax.ShapeDtypeStruct(s.shape, f32) for s in state],
            in_specs=[SCALARS, grad_spec, grad_spec] + [state_spec] * 3 + [ANYWHERE] * len(held),
            out_specs=[state_spec] * 3,
            input_output_aliases={6 + i: i for i in range(len(held))},
            compiler_params=pltpu.CompilerParams(vmem_limit_bytes=VMEM_BYTES),
            cost_estimate=pl.CostEstimate(
                flops=size * 12, bytes_accessed=size * 28, transcendentals=size
            ),
        )(kept, *grads, *state, *held)

    far_place_ids = flip_tok(place_ids, 2)
    input_groups = gather_rows(inputs)
    weights_first = gather_weights(0)
    cotangent_groups = gather_rows(cotangent)
    weights_second = gather_weights(1)
    late = gather_late()
    token_rows, *pre_part = forward(0, False, input_groups, weights_first)
    pre_terms = reduce_plane(*pre_part)
    grad_rows, *back_part = forward(1, True, cotangent_groups, weights_second)
    back_terms = reduce_plane(*back_part)
    piece = (part, hidden_span)
    outs = [jax.ShapeDtypeStruct(piece, bf16), jax.ShapeDtypeStruct(piece, f32)]
    hidden_piece, preact = over_columns(activate_kernel, outs, pre_terms, 2)
    hidden = gather_plane(hidden_piece)
    (grad_piece,) = over_columns(slope_kernel, outs[:1], [*back_terms, preact], 2)
    pre_grad = gather_plane(grad_piece)
    layer_out = reduce_rows(backward(1, False, *hidden, weights_second))
    grad_in = reduce_rows(backward(0, True, *pre_grad, weights_first))
    second_grad = gradient(1, grad_rows, *hidden, late)
    first_grad = gradient(0, token_rows, *pre_grad, late)
    held = update(1, second_grad, ())
    return (layer_out, grad_in, *update(0, first_grad, held))


def solution(mesh):
    return jax.shard_map(
        on_device,
        mesh=mesh,
        in_specs=(
            P(("mem", "hid"), "tok"),
            P(("mem", "hid"), "tok"),
            P(None, None, "hid", ("mem", "tok"), None, None),
            P(None, None, "hid", ("mem", "tok"), None, None),
            P(None, None, "hid", ("mem", "tok"), None, None),
            P(None, "tok", "hid", None),
            P(None, None, "hid"),
        ),
        out_specs=(
            P(("mem", "hid"), "tok"),
            P(("mem", "hid"), "tok"),
            P(None, None, "hid", ("mem", "tok"), None, None),
            P(None, None, "hid", ("mem", "tok"), None, None),
            P(None, None, "hid", ("mem", "tok"), None, None),
        ),
        check_vma=False,
    )
```

```python
import functools

import jax
import jax.numpy as jnp
from jax import lax
from jax.experimental import pallas as pl
from jax.experimental.pallas import tpu as pltpu
from jax.sharding import PartitionSpec as P


FFW = 24576
STEP = 10


GELU_ROOT = 0.7978845608028654
GELU_CUBIC = 0.044715
BETA_FIRST = 0.9
BETA_SECOND = 0.95
LEARN_RATE = 0.001
WEIGHT_DECAY = 0.1
ADAM_EPSILON = 1e-08
VMEM_BYTES = 56 * 2**20
UNROLL = 4
CHUNKS = 2
MEM, HID, TOK = "mem", "hid", "tok"


def activate(values):
    tangent = jnp.tanh(GELU_ROOT * (values + GELU_CUBIC * values * values * values))
    return 0.5 * values * (1.0 + tangent)


def gelu_slope(values):
    tangent = jnp.tanh(GELU_ROOT * (values + GELU_CUBIC * values * values * values))
    return 0.5 * (1.0 + tangent) + 0.5 * values * (1.0 - tangent * tangent) * GELU_ROOT * (
        1.0 + 3.0 * GELU_CUBIC * values * values
    )


def adam_step(weight, moment, variance, gradient):
    new_moment = BETA_FIRST * moment + (1.0 - BETA_FIRST) * gradient
    new_variance = BETA_SECOND * variance + (1.0 - BETA_SECOND) * gradient * gradient
    scaled = (
        new_moment
        / (1.0 - BETA_FIRST**STEP)
        / (jnp.sqrt(new_variance / (1.0 - BETA_SECOND**STEP)) + ADAM_EPSILON)
    )
    new_weight = weight - LEARN_RATE * (scaled + WEIGHT_DECAY * weight)
    return new_weight, new_moment, new_variance


def dot(left, right, left_dim, right_dim):
    return lax.dot_general(
        left, right, (((left_dim,), (right_dim,)), ((), ())), preferred_element_type=jnp.float32
    )


def lanes(index, size):
    return pl.ds(pl.multiple_of(index * size, size), size)


def owner_count(kept_ref, matrix, cell, owner, owned):
    first = (lax.axis_index(MEM) * lax.axis_size(TOK) + owner) * owned
    return first, jnp.clip(kept_ref[matrix, cell] - first, 0, owned)


def over_slots(count, body):
    groups = count // UNROLL

    def run(group, carry):
        body([group * UNROLL + lane for lane in range(UNROLL)])
        return carry

    lax.fori_loop(0, groups, run, 0)

    def single(slot, carry):
        body([slot])
        return carry

    lax.fori_loop(groups * UNROLL, count, single, 0)


def over_owners(matrix, kept_ref, weight_refs, body):
    tok = lax.axis_index(TOK)
    for turn, weight_ref in enumerate(weight_refs):
        owned = weight_ref.shape[0]
        first, count = owner_count(kept_ref, matrix, tok, tok ^ turn, owned)
        over_slots(count, functools.partial(body, weight_ref, first))


def relative(tok_count):
    tok = lax.axis_index(TOK)
    return (tok % 2) * (tok_count // 2) + tok // 2


def forward_kernel(
    matrix, transposed, width_blocks, tok_count, hid_count, mem_count, kept_ref, place_ref, *refs
):
    own_refs, weight_refs, (row_ref, keep_ref, send_ref) = (
        refs[:mem_count],
        refs[mem_count:-3],
        refs[-3:],
    )
    half = keep_ref.shape[1]
    _, size = weight_refs[0].shape[:2]
    rows = own_refs[0].shape[0]
    step = rows // hid_count
    part = rows // tok_count
    turn = relative(tok_count)
    for group in range(mem_count):
        for block in range(hid_count):
            start = block * step
            spot = ((start // part) ^ turn) * part + start % part + group * rows
            row_ref[pl.ds(pl.multiple_of(spot, step), step), :] = own_refs[group][
                start : start + step, :
            ]
    keep_ref[...] = jnp.zeros(keep_ref.shape, jnp.float32)
    send_ref[...] = jnp.zeros(send_ref.shape, jnp.float32)

    def body(weight_ref, first, slots):
        found = []
        for slot in slots:
            place = place_ref[matrix, first + slot]
            left = row_ref[:, lanes(place % width_blocks, size)]
            product = dot(left, weight_ref[slot], 1, 1 if transposed else 0)
            found.append((lanes(place // width_blocks, size), product))
        for spot, product in found:
            for group in range(mem_count):
                start = group * rows
                keep_ref[group, :, spot] += product[start : start + half]
                send_ref[group, :, spot] += product[start + half : start + rows]

    over_owners(matrix, kept_ref, weight_refs, body)


def backward_kernel(
    matrix, transposed, width_blocks, mem_count, kept_ref, place_ref, own_ref, pair_ref, *refs
):
    tok_count = lax.axis_size(TOK)
    weight_refs, out_refs, total_ref = refs[:tok_count], refs[tok_count:-1], refs[-1]
    size = weight_refs[0].shape[-1]
    half = own_ref.shape[1]
    total_ref[...] = jnp.zeros(total_ref.shape, jnp.float32)

    def body(weight_ref, first, slots):
        found = []
        for slot in slots:
            place = place_ref[matrix, first + slot]
            spot = lanes(place // width_blocks, size)
            pieces = []
            for group in range(mem_count):
                pieces += [own_ref[group, :, spot], pair_ref[group, :, spot]]
            product = dot(
                jnp.concatenate(pieces, axis=0), weight_ref[slot], 1, 1 if transposed else 0
            )
            found.append((lanes(place % width_blocks, size), product))
        for spot, product in found:
            total_ref[:, spot] += product

    over_owners(matrix, kept_ref, weight_refs, body)
    for index, out_ref in enumerate(out_refs):
        chunk, group = index // mem_count, index % mem_count
        span = out_ref.shape[1]
        out_ref[...] = total_ref[
            group * 2 * half : (group + 1) * 2 * half, chunk * span : (chunk + 1) * span
        ]


def gradient_kernel(matrix, width_blocks, mem_count, hid_count, kept_ref, place_ref, far_place_ref, *refs):
    row_ref, own_ref, pair_ref = refs[:3]
    late_refs = refs[3 : 3 + hid_count]
    keep_ref, send_ref, late_ref = refs[3 + hid_count :]
    cells, owned, size = keep_ref.shape[:3]
    tok_count = lax.axis_size(TOK)
    tok = lax.axis_index(TOK)
    rows = row_ref.shape[0] // mem_count
    part = rows // tok_count
    step = rows // hid_count
    turn = relative(tok_count)
    for block, source in enumerate(late_refs):
        start = block * step
        spot = ((start // part) ^ turn) * part + start % part
        for group in range(mem_count):
            late_ref[pl.ds(pl.multiple_of(spot + group * rows, step), step), :] = source[matrix, group]

    for cell in range(cells):
        places, values = ((place_ref, row_ref), (far_place_ref, late_ref))[cell]
        for side, out_ref in enumerate((keep_ref, send_ref)):
            first, count = owner_count(kept_ref, matrix, tok ^ (2 * cell), tok ^ side, owned)

            def body(slots):
                for slot in slots:
                    place = places[matrix, first + slot]
                    hidden = lanes(place // width_blocks, size)
                    width = lanes(place % width_blocks, size)
                    total = None
                    for group in range(mem_count):
                        wide = values[group * rows : (group + 1) * rows, width]
                        deep = jnp.concatenate(
                            [own_ref[group, :, hidden], pair_ref[group, :, hidden]], axis=0
                        )
                        left, right = (wide, deep) if matrix == 0 else (deep, wide)
                        term = dot(left, right, 0, 0).astype(jnp.bfloat16).astype(jnp.float32)
                        total = term if total is None else total + term
                    out_ref[cell, slot] = total

            over_slots(count, body)

            def clear(slot, carry):
                out_ref[cell, slot] = jnp.zeros((size, size), jnp.float32)
                return carry

            lax.fori_loop(count, owned, clear, 0)


def update_kernel(matrix, kept_ref, keep_ref, swap_ref, weight_ref, moment_ref, variance_ref, *refs):
    out_refs = refs[-3:]
    turn = pl.program_id(0)
    tok = lax.axis_index(TOK)
    owned = weight_ref.shape[3]
    _, count = owner_count(kept_ref, matrix, tok ^ turn, tok, owned)

    def update_from(grad_ref):
        def update(slot, carry):
            at = (0, 0, 0, slot)
            fresh = adam_step(weight_ref[at], moment_ref[at], variance_ref[at], grad_ref[0, slot])
            for out_ref, value in zip(out_refs, fresh):
                out_ref[at] = value
            return carry

        lax.fori_loop(0, count, update, 0)

    pl.when(turn % 2 == 0)(functools.partial(update_from, keep_ref))
    pl.when(turn % 2 == 1)(functools.partial(update_from, swap_ref))

    def keep(slot, carry):
        at = (0, 0, 0, slot)
        for out_ref, value_ref in zip(out_refs, (weight_ref, moment_ref, variance_ref)):
            out_ref[at] = value_ref[at]
        return carry

    lax.fori_loop(count, owned, keep, 0)


def join_kernel(keep_ref, swap_ref, *out_refs):
    groups = keep_ref.shape[0]
    part = out_refs[0].shape[0]
    for index, out_ref in enumerate(out_refs):
        group, start = index % groups, index // groups * part
        out_ref[...] = keep_ref[group, start : start + part] + swap_ref[group, start : start + part]


def total_of(refs):
    total = refs[0][...]
    for ref in refs[1:]:
        total = total + ref[...]
    return total


def activate_kernel(*refs):
    *part_refs, hidden_ref, preact_ref = refs
    preact = total_of(part_refs)
    preact_ref[...] = preact
    hidden_ref[...] = activate(preact).astype(jnp.bfloat16)


def slope_kernel(*refs):
    *part_refs, preact_ref, out_ref = refs
    out_ref[...] = (total_of(part_refs) * gelu_slope(preact_ref[...])).astype(jnp.bfloat16)


def narrow_kernel(block_ref, *out_refs):
    for turn, out_ref in enumerate(out_refs):

        @pl.when(pl.program_id(0) == turn)
        def _():
            out_ref[...] = block_ref[0, 0, 0].astype(jnp.bfloat16)


SCALARS = pl.BlockSpec(memory_space=pltpu.SMEM)
WHOLE = pl.BlockSpec(memory_space=pltpu.VMEM)
ANYWHERE = pl.BlockSpec(memory_space=pl.ANY)


def call(kernel, outs, scalars, arrays, flops, scratch=()):
    moved = sum(a.size * a.dtype.itemsize for a in arrays)
    moved += sum(math_size(o) for o in outs)
    return pl.pallas_call(
        kernel,
        out_shape=outs,
        in_specs=[SCALARS] * len(scalars) + [WHOLE] * len(arrays),
        out_specs=[WHOLE] * len(outs),
        scratch_shapes=scratch,
        compiler_params=pltpu.CompilerParams(vmem_limit_bytes=VMEM_BYTES),
        cost_estimate=pl.CostEstimate(flops=flops, bytes_accessed=moved, transcendentals=0),
    )(*scalars, *arrays)


def math_size(shape):
    total = shape.dtype.itemsize
    for dim in shape.shape:
        total *= dim
    return total


def on_device(inputs, cotangent, blocks, first_moment, second_moment, places, kept_counts):
    mem_count = lax.axis_size(MEM)
    tok_count = lax.axis_size(TOK)
    hid_count = lax.axis_size(HID)
    block_size = blocks.shape[-1]
    owned_slots = blocks.shape[3]
    local_slots = owned_slots * tok_count
    width_blocks = inputs.shape[1] // block_size
    hidden_span = FFW // hid_count
    rows = inputs.shape[0] * hid_count
    other = tok_count // 2
    half = rows // 2
    part = rows // tok_count
    chunks = CHUNKS
    kept = kept_counts[:, :, 0]
    place_ids = places[:, 0, 0]
    scalars = (kept, place_ids)
    f32, bf16 = jnp.float32, jnp.bfloat16

    def shift_hid(array, shift):
        return lax.ppermute(array, HID, [(i, (i + shift) % hid_count) for i in range(hid_count)])

    def shift_mem(array, shift):
        return lax.ppermute(array, MEM, [(i, (i + shift) % mem_count) for i in range(mem_count)])

    def flip_tok(array, bit):
        return lax.ppermute(array, TOK, [(i, i ^ bit) for i in range(tok_count)])

    def across(array, mem_shift, tok_shift):
        table = []
        for m in range(mem_count):
            for t in range(tok_count):
                to = ((m - mem_shift) % mem_count) * tok_count + (t ^ (2 * tok_shift))
                table.append((m * tok_count + t, to))
        return lax.ppermute(array, (MEM, TOK), table)

    peers = [(j, b) for j in range(mem_count) for b in range(other)][1:]

    def gather_rows(array):
        pieces = [array] + [shift_hid(array, k) for k in range(1, hid_count)]
        near = jnp.concatenate(pieces, axis=0)
        return [near] + [shift_mem(near, j) for j in range(1, mem_count)]

    def gather_late():
        both = flip_tok(jnp.stack([inputs, cotangent]), 2)
        found = [both] + [shift_mem(both, j) for j in range(1, mem_count)]
        moved = jnp.stack(found, axis=1)
        return [moved] + [shift_hid(moved, k) for k in range(1, hid_count)]

    def gather_weights(matrix):
        shape = (owned_slots, block_size, block_size)
        narrow = pl.pallas_call(
            narrow_kernel,
            grid=(tok_count,),
            out_shape=[jax.ShapeDtypeStruct(shape, bf16)] * tok_count,
            in_specs=[
                pl.BlockSpec(
                    (1, 1, 1) + blocks.shape[3:],
                    lambda i: (matrix, lax.axis_index(TOK) ^ i, 0, 0, 0, 0),
                )
            ],
            out_specs=[pl.BlockSpec(shape, lambda i: (0, 0, 0))] * tok_count,
            compiler_params=pltpu.CompilerParams(vmem_limit_bytes=VMEM_BYTES),
        )(blocks)
        moved = [flip_tok(narrow[r], r) for r in range(1, tok_count)]
        return [narrow[0], *moved]

    def forward(matrix, transposed, row_groups, weights):
        kernel = functools.partial(
            forward_kernel, matrix, transposed, width_blocks, tok_count, hid_count, mem_count
        )
        width = row_groups[0].shape[1]
        outs = [
            jax.ShapeDtypeStruct((mem_count * rows, width), bf16),
            jax.ShapeDtypeStruct((mem_count, half, hidden_span), f32),
            jax.ShapeDtypeStruct((mem_count, half, hidden_span), f32),
        ]
        flops = 2 * mem_count * rows * local_slots * block_size * block_size
        return call(kernel, outs, scalars, [*row_groups, *weights], flops)

    def over_columns(kernel, outs, arrays, steps):
        def spec(shape):
            lead = len(shape) - 1
            return pl.BlockSpec(
                tuple(shape[:-1]) + (shape[-1] // steps,), lambda i: (0,) * lead + (i,)
            )

        return pl.pallas_call(
            kernel,
            grid=(steps,),
            out_shape=outs,
            in_specs=[spec(a.shape) for a in arrays],
            out_specs=[spec(o.shape) for o in outs],
            compiler_params=pltpu.CompilerParams(vmem_limit_bytes=VMEM_BYTES),
            cost_estimate=pl.CostEstimate(
                flops=sum(o.size for o in outs) * 4,
                bytes_accessed=sum(a.size * a.dtype.itemsize for a in (*arrays, *outs)),
                transcendentals=0,
            ),
        )(*arrays)

    def reduce_plane(keep, send):
        outs = [jax.ShapeDtypeStruct((part, hidden_span), f32)] * (mem_count * other)
        swap = flip_tok(send, 1)
        found = over_columns(join_kernel, outs, [keep, swap], 4)
        terms = [found[0]]
        for j, b in peers:
            terms.append(across(found[b * mem_count + j], j, b))
        return terms

    def gather_plane(piece):
        found = {(0, 0): piece}
        for j, b in peers:
            found[(-j) % mem_count, b] = across(piece, j, b)
        near = jnp.concatenate(
            [found[j, b] for j in range(mem_count) for b in range(other)], axis=0
        ).reshape(mem_count, half, hidden_span)
        return near, flip_tok(near, 1)

    def backward(matrix, transposed, near, far, weights):
        kernel = functools.partial(backward_kernel, matrix, transposed, width_blocks, mem_count)
        span = inputs.shape[1] // chunks
        outs = [jax.ShapeDtypeStruct((rows, span), f32)] * (mem_count * chunks)
        flops = 2 * mem_count * rows * local_slots * block_size * block_size
        scratch = [pltpu.VMEM((mem_count * rows, inputs.shape[1]), f32)]
        return call(kernel, outs, scalars, [near, far, *weights], flops, scratch)

    turn = relative(tok_count)
    step = inputs.shape[0]

    def reduce_rows(found):
        results = []
        for chunk in range(chunks):
            groups = found[chunk * mem_count : (chunk + 1) * mem_count]
            total = groups[0]
            for j in range(1, mem_count):
                total = total + shift_mem(groups[j], -j)
            result = None
            for k in range(hid_count):
                start = k * step
                spot = ((start // part) ^ turn) * part + start % part
                piece = lax.dynamic_slice_in_dim(total, spot, step, 0)
                if k:
                    piece = shift_hid(piece, -k)
                result = piece if result is None else result + piece
            results.append(result.astype(bf16))
        return jnp.concatenate(results, axis=1)

    def gradient(matrix, row_values, near, far, late):
        kernel = functools.partial(gradient_kernel, matrix, width_blocks, mem_count, hid_count)
        outs = [
            jax.ShapeDtypeStruct((other, owned_slots, block_size, block_size), f32),
            jax.ShapeDtypeStruct((other, owned_slots, block_size, block_size), f32),
        ]
        flops = 2 * mem_count * rows * local_slots * block_size * block_size
        keep, send = call(
            kernel,
            outs,
            (kept, place_ids, far_place_ids),
            [row_values, near, far, *late],
            flops,
            [pltpu.VMEM(row_values.shape, bf16)],
        )
        return keep, flip_tok(send, 1)

    def update(matrix, grads, held):
        state_shape = (1, 1, 1, owned_slots, block_size, block_size)
        state_spec = pl.BlockSpec(state_shape, lambda i: (matrix, lax.axis_index(TOK) ^ i, 0, 0, 0, 0))
        grad_spec = pl.BlockSpec((1, owned_slots, block_size, block_size), lambda i: (i // 2, 0, 0, 0))
        state = (blocks, first_moment, second_moment)
        size = local_slots * block_size * block_size
        return pl.pallas_call(
            functools.partial(update_kernel, matrix),
            grid=(tok_count,),
            out_shape=[jax.ShapeDtypeStruct(s.shape, f32) for s in state],
            in_specs=[SCALARS, grad_spec, grad_spec] + [state_spec] * 3 + [ANYWHERE] * len(held),
            out_specs=[state_spec] * 3,
            input_output_aliases={6 + i: i for i in range(len(held))},
            compiler_params=pltpu.CompilerParams(vmem_limit_bytes=VMEM_BYTES),
            cost_estimate=pl.CostEstimate(
                flops=size * 12, bytes_accessed=size * 28, transcendentals=size
            ),
        )(kept, *grads, *state, *held)

    far_place_ids = flip_tok(place_ids, 2)
    input_groups = gather_rows(inputs)
    weights_first = gather_weights(0)
    cotangent_groups = gather_rows(cotangent)
    weights_second = gather_weights(1)
    late = gather_late()
    token_rows, *pre_part = forward(0, False, input_groups, weights_first)
    pre_terms = reduce_plane(*pre_part)
    grad_rows, *back_part = forward(1, True, cotangent_groups, weights_second)
    back_terms = reduce_plane(*back_part)
    piece = (part, hidden_span)
    outs = [jax.ShapeDtypeStruct(piece, bf16), jax.ShapeDtypeStruct(piece, f32)]
    hidden_piece, preact = over_columns(activate_kernel, outs, pre_terms, 2)
    hidden = gather_plane(hidden_piece)
    (grad_piece,) = over_columns(slope_kernel, outs[:1], [*back_terms, preact], 2)
    pre_grad = gather_plane(grad_piece)
    layer_out = reduce_rows(backward(1, False, *hidden, weights_second))
    grad_in = reduce_rows(backward(0, True, *pre_grad, weights_first))
    second_grad = gradient(1, grad_rows, *hidden, late)
    first_grad = gradient(0, token_rows, *pre_grad, late)
    held = update(1, second_grad, ())
    return (layer_out, grad_in, *update(0, first_grad, held))


def solution(mesh):
    return jax.shard_map(
        on_device,
        mesh=mesh,
        in_specs=(
            P((MEM, HID), TOK),
            P((MEM, HID), TOK),
            P(None, None, HID, (MEM, TOK), None, None),
            P(None, None, HID, (MEM, TOK), None, None),
            P(None, None, HID, (MEM, TOK), None, None),
            P(None, TOK, HID, None),
            P(None, None, HID),
        ),
        out_specs=(
            P((MEM, HID), TOK),
            P((MEM, HID), TOK),
            P(None, None, HID, (MEM, TOK), None, None),
            P(None, None, HID, (MEM, TOK), None, None),
            P(None, None, HID, (MEM, TOK), None, None),
        ),
        check_vma=False,
    )
```

```python
import functools
import math

import jax
import jax.numpy as jnp
from jax import lax
from jax.experimental import pallas as pl
from jax.experimental.pallas import tpu as pltpu
from jax.sharding import PartitionSpec as P


FFW = 24576
STEP = 10


GELU_ROOT = 0.7978845608028654
GELU_CUBIC = 0.044715
BETA_FIRST = 0.9
BETA_SECOND = 0.95
LEARN_RATE = 0.001
WEIGHT_DECAY = 0.1
ADAM_EPSILON = 1e-08
VMEM_SPARE = 3 * 2**19
UNROLL = 4
CHUNKS = 2
MEM, HID, TOK = "mem", "hid", "tok"


def activate(values):
    tangent = jnp.tanh(GELU_ROOT * (values + GELU_CUBIC * values * values * values))
    return 0.5 * values * (1.0 + tangent)


def gelu_slope(values):
    tangent = jnp.tanh(GELU_ROOT * (values + GELU_CUBIC * values * values * values))
    return 0.5 * (1.0 + tangent) + 0.5 * values * (1.0 - tangent * tangent) * GELU_ROOT * (
        1.0 + 3.0 * GELU_CUBIC * values * values
    )


def adam_step(weight, moment, variance, gradient):
    new_moment = BETA_FIRST * moment + (1.0 - BETA_FIRST) * gradient
    new_variance = BETA_SECOND * variance + (1.0 - BETA_SECOND) * gradient * gradient
    scaled = (
        new_moment
        / (1.0 - BETA_FIRST**STEP)
        / (jnp.sqrt(new_variance / (1.0 - BETA_SECOND**STEP)) + ADAM_EPSILON)
    )
    new_weight = weight - LEARN_RATE * (scaled + WEIGHT_DECAY * weight)
    return new_weight, new_moment, new_variance


def dot(left, right, left_dim, right_dim):
    return lax.dot_general(
        left, right, (((left_dim,), (right_dim,)), ((), ())), preferred_element_type=jnp.float32
    )


def lanes(index, size):
    return pl.ds(pl.multiple_of(index * size, size), size)


def owner_count(kept_ref, matrix, cell, owner, owned):
    first = (lax.axis_index(MEM) * lax.axis_size(TOK) + owner) * owned
    return first, jnp.clip(kept_ref[matrix, cell] - first, 0, owned)


def over_slots(count, body):
    groups = count // UNROLL

    def run(group, carry):
        body([group * UNROLL + lane for lane in range(UNROLL)])
        return carry

    lax.fori_loop(0, groups, run, 0)

    def single(slot, carry):
        body([slot])
        return carry

    lax.fori_loop(groups * UNROLL, count, single, 0)


def over_owners(matrix, kept_ref, weight_refs, body):
    tok = lax.axis_index(TOK)
    for turn, weight_ref in enumerate(weight_refs):
        owned = weight_ref.shape[0]
        first, count = owner_count(kept_ref, matrix, tok, tok ^ turn, owned)
        over_slots(count, functools.partial(body, weight_ref, first))


def relative(tok_count):
    tok = lax.axis_index(TOK)
    return (tok % 2) * (tok_count // 2) + tok // 2


def forward_kernel(
    matrix, transposed, width_blocks, tok_count, hid_count, mem_count, kept_ref, place_ref, *refs
):
    own_refs, weight_refs, (row_ref, keep_ref, send_ref) = (
        refs[:mem_count],
        refs[mem_count:-3],
        refs[-3:],
    )
    half = keep_ref.shape[1]
    _, size = weight_refs[0].shape[:2]
    rows = own_refs[0].shape[0]
    step = rows // hid_count
    part = rows // tok_count
    turn = relative(tok_count)
    for group in range(mem_count):
        for block in range(hid_count):
            start = block * step
            spot = ((start // part) ^ turn) * part + start % part + group * rows
            row_ref[pl.ds(pl.multiple_of(spot, step), step), :] = own_refs[group][
                start : start + step, :
            ]
    keep_ref[...] = jnp.zeros(keep_ref.shape, jnp.float32)
    send_ref[...] = jnp.zeros(send_ref.shape, jnp.float32)

    def body(weight_ref, first, slots):
        found = []
        for slot in slots:
            place = place_ref[matrix, first + slot]
            left = row_ref[:, lanes(place % width_blocks, size)]
            product = dot(left, weight_ref[slot], 1, 1 if transposed else 0)
            found.append((lanes(place // width_blocks, size), product))
        for spot, product in found:
            for group in range(mem_count):
                start = group * rows
                keep_ref[group, :, spot] += product[start : start + half]
                send_ref[group, :, spot] += product[start + half : start + rows]

    over_owners(matrix, kept_ref, weight_refs, body)


def backward_kernel(
    matrix, transposed, width_blocks, mem_count, kept_ref, place_ref, own_ref, pair_ref, *refs
):
    tok_count = lax.axis_size(TOK)
    weight_refs, out_refs, total_ref = refs[:tok_count], refs[tok_count:-1], refs[-1]
    size = weight_refs[0].shape[-1]
    half = own_ref.shape[1]
    total_ref[...] = jnp.zeros(total_ref.shape, jnp.float32)

    def body(weight_ref, first, slots):
        found = []
        for slot in slots:
            place = place_ref[matrix, first + slot]
            spot = lanes(place // width_blocks, size)
            pieces = []
            for group in range(mem_count):
                pieces += [own_ref[group, :, spot], pair_ref[group, :, spot]]
            product = dot(
                jnp.concatenate(pieces, axis=0), weight_ref[slot], 1, 1 if transposed else 0
            )
            found.append((lanes(place % width_blocks, size), product))
        for spot, product in found:
            total_ref[:, spot] += product

    over_owners(matrix, kept_ref, weight_refs, body)
    for index, out_ref in enumerate(out_refs):
        chunk, group = index // mem_count, index % mem_count
        span = out_ref.shape[1]
        out_ref[...] = total_ref[
            group * 2 * half : (group + 1) * 2 * half, chunk * span : (chunk + 1) * span
        ]


def gradient_kernel(matrix, width_blocks, mem_count, hid_count, kept_ref, place_ref, far_place_ref, *refs):
    row_ref, own_ref, pair_ref = refs[:3]
    late_refs = refs[3 : 3 + hid_count]
    keep_ref, send_ref, late_ref = refs[3 + hid_count :]
    cells, owned, size = keep_ref.shape[:3]
    tok_count = lax.axis_size(TOK)
    tok = lax.axis_index(TOK)
    rows = row_ref.shape[0] // mem_count
    part = rows // tok_count
    step = rows // hid_count
    turn = relative(tok_count)
    for block, source in enumerate(late_refs):
        start = block * step
        spot = ((start // part) ^ turn) * part + start % part
        for group in range(mem_count):
            late_ref[pl.ds(pl.multiple_of(spot + group * rows, step), step), :] = source[matrix, group]

    for cell in range(cells):
        places, values = ((place_ref, row_ref), (far_place_ref, late_ref))[cell]
        for side, out_ref in enumerate((keep_ref, send_ref)):
            first, count = owner_count(kept_ref, matrix, tok ^ (2 * cell), tok ^ side, owned)

            def body(slots):
                for slot in slots:
                    place = places[matrix, first + slot]
                    hidden = lanes(place // width_blocks, size)
                    width = lanes(place % width_blocks, size)
                    total = None
                    for group in range(mem_count):
                        wide = values[group * rows : (group + 1) * rows, width]
                        deep = jnp.concatenate(
                            [own_ref[group, :, hidden], pair_ref[group, :, hidden]], axis=0
                        )
                        left, right = (wide, deep) if matrix == 0 else (deep, wide)
                        term = dot(left, right, 0, 0).astype(jnp.bfloat16).astype(jnp.float32)
                        total = term if total is None else total + term
                    out_ref[cell, slot] = total

            over_slots(count, body)

            def clear(slot, carry):
                out_ref[cell, slot] = jnp.zeros((size, size), jnp.float32)
                return carry

            lax.fori_loop(count, owned, clear, 0)


def update_kernel(matrix, owned, kept_ref, keep_ref, swap_ref, weight_ref, moment_ref, variance_ref, *refs):
    out_refs = refs[-3:]
    turn = pl.program_id(0)
    tok = lax.axis_index(TOK)
    run = weight_ref.shape[3]
    _, count = owner_count(kept_ref, matrix, tok ^ turn, tok, owned)
    count = jnp.clip(count - pl.program_id(1) * run, 0, run)

    def update_from(grad_ref):
        def update(slot, carry):
            at = (0, 0, 0, slot)
            fresh = adam_step(weight_ref[at], moment_ref[at], variance_ref[at], grad_ref[0, slot])
            for out_ref, value in zip(out_refs, fresh):
                out_ref[at] = value
            return carry

        lax.fori_loop(0, count, update, 0)

    pl.when(turn % 2 == 0)(functools.partial(update_from, keep_ref))
    pl.when(turn % 2 == 1)(functools.partial(update_from, swap_ref))

    def keep(slot, carry):
        at = (0, 0, 0, slot)
        for out_ref, value_ref in zip(out_refs, (weight_ref, moment_ref, variance_ref)):
            out_ref[at] = value_ref[at]
        return carry

    lax.fori_loop(count, run, keep, 0)


def join_kernel(pair_major, keep_ref, swap_ref, *out_refs):
    part = out_refs[0].shape[1]
    for index, out_ref in enumerate(out_refs):
        for inner in range(out_ref.shape[0]):
            group, shift = (inner, index) if pair_major else (index, inner)
            at = slice(shift * part, (shift + 1) * part)
            out_ref[inner] = keep_ref[group, at] + swap_ref[group, at]


def split_kernel(*refs):
    inner = refs[0].shape[0]
    for index, out_ref in enumerate(refs[-inner:]):
        total = refs[0][index]
        for ref in refs[1:-inner]:
            total = total + ref[index]
        out_ref[...] = total


def total_of(refs):
    total = refs[0][...]
    for ref in refs[1:]:
        total = total + ref[...]
    return total


def activate_kernel(split, *refs):
    *part_refs, hidden_ref, preact_ref = refs
    span = preact_ref.shape[1] // 2
    for side, side_refs in enumerate((part_refs[:split], part_refs[split:])):
        at = slice(side * span, (side + 1) * span)
        preact = total_of(side_refs)
        preact_ref[:, at] = preact
        hidden_ref[:, at] = activate(preact).astype(jnp.bfloat16)


def slope_kernel(split, *refs):
    *part_refs, preact_ref, out_ref = refs
    span = preact_ref.shape[1] // 2
    for side, side_refs in enumerate((part_refs[:split], part_refs[split:])):
        at = slice(side * span, (side + 1) * span)
        slope = gelu_slope(preact_ref[:, at])
        out_ref[:, at] = (total_of(side_refs) * slope).astype(jnp.bfloat16)


def narrow_kernel(block_ref, *out_refs):
    for turn, out_ref in enumerate(out_refs):

        @pl.when(pl.program_id(0) == turn)
        def _():
            out_ref[...] = block_ref[0, 0, 0].astype(jnp.bfloat16)


SCALARS = pl.BlockSpec(memory_space=pltpu.SMEM)
WHOLE = pl.BlockSpec(memory_space=pltpu.VMEM)
ANYWHERE = pl.BlockSpec(memory_space=pl.ANY)


def call(kernel, outs, scalars, arrays, flops, scratch=(), scratch_sizes=()):
    moved = sum(math_size(a) for a in (*arrays, *outs))
    return pl.pallas_call(
        kernel,
        out_shape=outs,
        in_specs=[SCALARS] * len(scalars) + [WHOLE] * len(arrays),
        out_specs=[WHOLE] * len(outs),
        scratch_shapes=scratch,
        compiler_params=grant(moved + sum(scratch_sizes)),
        cost_estimate=pl.CostEstimate(flops=flops, bytes_accessed=moved, transcendentals=0),
    )(*scalars, *arrays)


def math_size(array):
    return math.prod(array.shape) * array.dtype.itemsize


def grant(needed):
    return pltpu.CompilerParams(vmem_limit_bytes=needed + VMEM_SPARE)


def on_device(inputs, cotangent, blocks, first_moment, second_moment, places, kept_counts):
    mem_count = lax.axis_size(MEM)
    tok_count = lax.axis_size(TOK)
    hid_count = lax.axis_size(HID)
    block_size = blocks.shape[-1]
    owned_slots = blocks.shape[3]
    local_slots = owned_slots * tok_count
    width_blocks = inputs.shape[1] // block_size
    hidden_span = FFW // hid_count
    rows = inputs.shape[0] * hid_count
    other = tok_count // 2
    half = rows // 2
    part = rows // tok_count
    chunks = CHUNKS
    kept = kept_counts[:, :, 0]
    place_ids = places[:, 0, 0]
    scalars = (kept, place_ids)
    f32, bf16 = jnp.float32, jnp.bfloat16

    def shift_hid(array, shift):
        return lax.ppermute(array, HID, [(i, (i + shift) % hid_count) for i in range(hid_count)])

    def shift_mem(array, shift):
        return lax.ppermute(array, MEM, [(i, (i + shift) % mem_count) for i in range(mem_count)])

    def flip_tok(array, bit):
        return lax.ppermute(array, TOK, [(i, i ^ bit) for i in range(tok_count)])

    def across(array, mem_shift, tok_shift):
        table = []
        for m in range(mem_count):
            for t in range(tok_count):
                to = ((m - mem_shift) % mem_count) * tok_count + (t ^ (2 * tok_shift))
                table.append((m * tok_count + t, to))
        return lax.ppermute(array, (MEM, TOK), table)

    peers = [(j, b) for j in range(mem_count) for b in range(other)][1:]

    def gather_rows(array):
        pieces = [array] + [shift_hid(array, k) for k in range(1, hid_count)]
        near = jnp.concatenate(pieces, axis=0)
        return [near] + [shift_mem(near, j) for j in range(1, mem_count)]

    def gather_late():
        both = flip_tok(jnp.stack([inputs, cotangent]), 2)
        found = [both] + [shift_mem(both, j) for j in range(1, mem_count)]
        moved = jnp.stack(found, axis=1)
        return [moved] + [shift_hid(moved, k) for k in range(1, hid_count)]

    def gather_weights(matrix):
        shape = (owned_slots, block_size, block_size)
        narrow = pl.pallas_call(
            narrow_kernel,
            grid=(tok_count,),
            out_shape=[jax.ShapeDtypeStruct(shape, bf16)] * tok_count,
            in_specs=[
                pl.BlockSpec(
                    (1, 1, 1) + blocks.shape[3:],
                    lambda i: (matrix, lax.axis_index(TOK) ^ i, 0, 0, 0, 0),
                )
            ],
            out_specs=[pl.BlockSpec(shape, lambda i: (0, 0, 0))] * tok_count,
            compiler_params=grant(owned_slots * block_size**2 * 4 * (2 + tok_count)),
        )(blocks)
        moved = [flip_tok(narrow[r], r) for r in range(1, tok_count)]
        return [narrow[0], *moved]

    def forward(matrix, transposed, row_groups, weights):
        kernel = functools.partial(
            forward_kernel, matrix, transposed, width_blocks, tok_count, hid_count, mem_count
        )
        width = row_groups[0].shape[1]
        outs = [
            jax.ShapeDtypeStruct((mem_count * rows, width), bf16),
            jax.ShapeDtypeStruct((mem_count, half, hidden_span), f32),
            jax.ShapeDtypeStruct((mem_count, half, hidden_span), f32),
        ]
        flops = 2 * mem_count * rows * local_slots * block_size * block_size
        return call(kernel, outs, scalars, [*row_groups, *weights], flops)

    def half_columns(kernel, outs, arrays, side, steps):
        span = hidden_span // 2 // steps

        def spec(shape, shift):
            lead = len(shape) - 1
            return pl.BlockSpec(tuple(shape[:-1]) + (span,), lambda i: (0,) * lead + (i + shift,))

        shift = side * steps
        needed = sum(math_size(a) for a in outs) // steps * 2
        needed += sum(math_size(a) for a in arrays) // steps
        return pl.pallas_call(
            kernel,
            grid=(steps,),
            out_shape=outs,
            in_specs=[spec(a.shape, shift) for a in arrays],
            out_specs=[spec(o.shape, 0) for o in outs],
            compiler_params=grant(needed),
            cost_estimate=pl.CostEstimate(
                flops=sum(math.prod(o.shape) for o in outs) * 2,
                bytes_accessed=needed * steps // 2,
                transcendentals=0,
            ),
        )(*arrays)

    def reduce_plane(keep, send):
        swap = flip_tok(send, 1)
        span = hidden_span // 2

        def array(*lead):
            return jax.ShapeDtypeStruct((*lead, span), f32)

        by_mem = half_columns(
            functools.partial(join_kernel, False),
            [array(other, part)] * mem_count,
            [keep, swap],
            0,
            2,
        )
        by_pair = half_columns(
            functools.partial(join_kernel, True),
            [array(mem_count, part)] * other,
            [keep, swap],
            1,
            2,
        )
        mem_terms = [by_mem[0]] + [shift_mem(by_mem[j], -j) for j in range(1, mem_count)]
        pair_terms = [by_pair[0]] + [flip_tok(by_pair[b], 2 * b) for b in range(1, other)]
        mine, *rest = call(split_kernel, [array(part)] * other, (), mem_terms, part)
        first = [mine] + [flip_tok(x, 2 * b) for b, x in enumerate(rest, 1)]
        mine, *rest = call(split_kernel, [array(part)] * mem_count, (), pair_terms, part)
        second = [mine] + [shift_mem(x, -j) for j, x in enumerate(rest, 1)]
        return first, second

    def gather_plane(piece):
        found = {(0, 0): piece}
        for j, b in peers:
            found[(-j) % mem_count, b] = across(piece, j, b)
        near = jnp.concatenate(
            [found[j, b] for j in range(mem_count) for b in range(other)], axis=0
        ).reshape(mem_count, half, hidden_span)
        return near, flip_tok(near, 1)

    def backward(matrix, transposed, near, far, weights):
        kernel = functools.partial(backward_kernel, matrix, transposed, width_blocks, mem_count)
        span = inputs.shape[1] // chunks
        outs = [jax.ShapeDtypeStruct((rows, span), f32)] * (mem_count * chunks)
        flops = 2 * mem_count * rows * local_slots * block_size * block_size
        scratch = [pltpu.VMEM((mem_count * rows, inputs.shape[1]), f32)]
        sizes = [mem_count * rows * inputs.shape[1] * 4]
        return call(kernel, outs, scalars, [near, far, *weights], flops, scratch, sizes)

    turn = relative(tok_count)
    step = inputs.shape[0]

    def reduce_rows(found):
        results = []
        for chunk in range(chunks):
            groups = found[chunk * mem_count : (chunk + 1) * mem_count]
            total = groups[0]
            for j in range(1, mem_count):
                total = total + shift_mem(groups[j], -j)
            result = None
            for k in range(hid_count):
                start = k * step
                spot = ((start // part) ^ turn) * part + start % part
                piece = lax.dynamic_slice_in_dim(total, spot, step, 0)
                if k:
                    piece = shift_hid(piece, -k)
                result = piece if result is None else result + piece
            results.append(result.astype(bf16))
        return jnp.concatenate(results, axis=1)

    def gradient(matrix, row_values, near, far, late):
        kernel = functools.partial(gradient_kernel, matrix, width_blocks, mem_count, hid_count)
        outs = [
            jax.ShapeDtypeStruct((other, owned_slots, block_size, block_size), f32),
            jax.ShapeDtypeStruct((other, owned_slots, block_size, block_size), f32),
        ]
        flops = 2 * mem_count * rows * local_slots * block_size * block_size
        keep, send = call(
            kernel,
            outs,
            (kept, place_ids, far_place_ids),
            [row_values, near, far, *late],
            flops,
            [pltpu.VMEM(row_values.shape, bf16)],
            [math_size(row_values)],
        )
        return keep, flip_tok(send, 1)

    def update(matrix, grads, held):
        splits = 2 if owned_slots % 2 == 0 else 1
        run = owned_slots // splits
        state_spec = pl.BlockSpec(
            (1, 1, 1, run, block_size, block_size),
            lambda i, j: (matrix, lax.axis_index(TOK) ^ i, 0, j, 0, 0),
        )
        grad_spec = pl.BlockSpec((1, run, block_size, block_size), lambda i, j: (i // 2, j, 0, 0))
        state = (blocks, first_moment, second_moment)
        size = local_slots * block_size * block_size
        return pl.pallas_call(
            functools.partial(update_kernel, matrix, owned_slots),
            grid=(tok_count, splits),
            out_shape=[jax.ShapeDtypeStruct(s.shape, f32) for s in state],
            in_specs=[SCALARS, grad_spec, grad_spec] + [state_spec] * 3 + [ANYWHERE] * len(held),
            out_specs=[state_spec] * 3,
            input_output_aliases={6 + i: i for i in range(len(held))},
            compiler_params=grant(16 * run * block_size**2 * 4),
            cost_estimate=pl.CostEstimate(
                flops=size * 12, bytes_accessed=size * 28, transcendentals=size
            ),
        )(kept, *grads, *state, *held)

    far_place_ids = flip_tok(place_ids, 2)
    input_groups = gather_rows(inputs)
    weights_first = gather_weights(0)
    cotangent_groups = gather_rows(cotangent)
    weights_second = gather_weights(1)
    late = gather_late()
    token_rows, *pre_part = forward(0, False, input_groups, weights_first)
    pre_terms = reduce_plane(*pre_part)
    grad_rows, *back_part = forward(1, True, cotangent_groups, weights_second)
    back_terms = reduce_plane(*back_part)
    piece = (part, hidden_span)
    outs = [jax.ShapeDtypeStruct(piece, bf16), jax.ShapeDtypeStruct(piece, f32)]
    kernel = functools.partial(activate_kernel, len(pre_terms[0]))
    hidden_piece, preact = call(kernel, outs, (), [*pre_terms[0], *pre_terms[1]], part)
    hidden = gather_plane(hidden_piece)
    kernel = functools.partial(slope_kernel, len(back_terms[0]))
    arrays = [*back_terms[0], *back_terms[1], preact]
    (grad_piece,) = call(kernel, outs[:1], (), arrays, part)
    pre_grad = gather_plane(grad_piece)
    layer_out = reduce_rows(backward(1, False, *hidden, weights_second))
    grad_in = reduce_rows(backward(0, True, *pre_grad, weights_first))
    second_grad = gradient(1, grad_rows, *hidden, late)
    first_grad = gradient(0, token_rows, *pre_grad, late)
    held = update(1, second_grad, ())
    return (layer_out, grad_in, *update(0, first_grad, held))


def solution(mesh):
    return jax.shard_map(
        on_device,
        mesh=mesh,
        in_specs=(
            P((MEM, HID), TOK),
            P((MEM, HID), TOK),
            P(None, None, HID, (MEM, TOK), None, None),
            P(None, None, HID, (MEM, TOK), None, None),
            P(None, None, HID, (MEM, TOK), None, None),
            P(None, TOK, HID, None),
            P(None, None, HID),
        ),
        out_specs=(
            P((MEM, HID), TOK),
            P((MEM, HID), TOK),
            P(None, None, HID, (MEM, TOK), None, None),
            P(None, None, HID, (MEM, TOK), None, None),
            P(None, None, HID, (MEM, TOK), None, None),
        ),
        check_vma=False,
    )
```

```python
import functools
import math

import jax
import jax.numpy as jnp
from jax import lax
from jax.experimental import pallas as pl
from jax.experimental.pallas import tpu as pltpu
from jax.sharding import PartitionSpec as P


FFW = 24576
STEP = 10


GELU_ROOT = 0.7978845608028654
GELU_CUBIC = 0.044715
BETA_FIRST = 0.9
BETA_SECOND = 0.95
LEARN_RATE = 0.001
WEIGHT_DECAY = 0.1
ADAM_EPSILON = 1e-08
VMEM_SPARE = 3 * 2**19
UNROLL = 4
CHUNKS = 2
MEM, HID, TOK = "mem", "hid", "tok"


def activate(values):
    tangent = jnp.tanh(GELU_ROOT * (values + GELU_CUBIC * values * values * values))
    return 0.5 * values * (1.0 + tangent)


def gelu_slope(values):
    tangent = jnp.tanh(GELU_ROOT * (values + GELU_CUBIC * values * values * values))
    return 0.5 * (1.0 + tangent) + 0.5 * values * (1.0 - tangent * tangent) * GELU_ROOT * (
        1.0 + 3.0 * GELU_CUBIC * values * values
    )


def adam_step(weight, moment, variance, gradient):
    new_moment = BETA_FIRST * moment + (1.0 - BETA_FIRST) * gradient
    new_variance = BETA_SECOND * variance + (1.0 - BETA_SECOND) * gradient * gradient
    scaled = (
        new_moment
        / (1.0 - BETA_FIRST**STEP)
        / (jnp.sqrt(new_variance / (1.0 - BETA_SECOND**STEP)) + ADAM_EPSILON)
    )
    new_weight = weight - LEARN_RATE * (scaled + WEIGHT_DECAY * weight)
    return new_weight, new_moment, new_variance


def dot(left, right, left_dim, right_dim):
    return lax.dot_general(
        left, right, (((left_dim,), (right_dim,)), ((), ())), preferred_element_type=jnp.float32
    )


def lanes(index, size):
    return pl.ds(pl.multiple_of(index * size, size), size)


def owner_count(kept_ref, matrix, cell, owner, owned):
    first = (lax.axis_index(MEM) * lax.axis_size(TOK) + owner) * owned
    return first, jnp.clip(kept_ref[matrix, cell] - first, 0, owned)


def over_slots(count, body):
    groups = count // UNROLL

    def run(group, carry):
        body([group * UNROLL + lane for lane in range(UNROLL)])
        return carry

    lax.fori_loop(0, groups, run, 0)

    def single(slot, carry):
        body([slot])
        return carry

    lax.fori_loop(groups * UNROLL, count, single, 0)


def over_owners(matrix, kept_ref, weight_refs, body):
    tok = lax.axis_index(TOK)
    for turn, weight_ref in enumerate(weight_refs):
        owned = weight_ref.shape[0]
        first, count = owner_count(kept_ref, matrix, tok, tok ^ turn, owned)
        over_slots(count, functools.partial(body, weight_ref, first))


def relative(tok_count):
    tok = lax.axis_index(TOK)
    return (tok % 2) * (tok_count // 2) + tok // 2


def forward_kernel(
    matrix, transposed, width_blocks, tok_count, hid_count, mem_count, kept_ref, place_ref, *refs
):
    sources = hid_count if matrix else mem_count
    own_refs, weight_refs, (row_ref, keep_ref, send_ref) = (
        refs[:sources],
        refs[sources:-3],
        refs[-3:],
    )
    half = keep_ref.shape[1]
    _, size = weight_refs[0].shape[:2]
    rows = row_ref.shape[0] // mem_count
    step = rows // hid_count
    part = rows // tok_count
    turn = relative(tok_count)
    for group in range(mem_count):
        for block in range(hid_count):
            start = block * step
            spot = ((start // part) ^ turn) * part + start % part + group * rows
            row_ref[pl.ds(pl.multiple_of(spot, step), step), :] = (
                own_refs[block][group] if matrix else own_refs[group][start : start + step, :]
            )
    keep_ref[...] = jnp.zeros(keep_ref.shape, jnp.float32)
    send_ref[...] = jnp.zeros(send_ref.shape, jnp.float32)

    def body(weight_ref, first, slots):
        found = []
        for slot in slots:
            place = place_ref[matrix, first + slot]
            left = row_ref[:, lanes(place % width_blocks, size)]
            product = dot(left, weight_ref[slot], 1, 1 if transposed else 0)
            found.append((lanes(place // width_blocks, size), product))
        for spot, product in found:
            for group in range(mem_count):
                start = group * rows
                keep_ref[group, :, spot] += product[start : start + half]
                send_ref[group, :, spot] += product[start + half : start + rows]

    over_owners(matrix, kept_ref, weight_refs, body)


def backward_kernel(
    matrix, transposed, width_blocks, mem_count, kept_ref, place_ref, own_ref, pair_ref, *refs
):
    tok_count = lax.axis_size(TOK)
    weight_refs, out_refs, total_ref = refs[:tok_count], refs[tok_count:-1], refs[-1]
    size = weight_refs[0].shape[-1]
    half = own_ref.shape[1]
    total_ref[...] = jnp.zeros(total_ref.shape, jnp.float32)

    def body(weight_ref, first, slots):
        found = []
        for slot in slots:
            place = place_ref[matrix, first + slot]
            spot = lanes(place // width_blocks, size)
            pieces = []
            for group in range(mem_count):
                pieces += [own_ref[group, :, spot], pair_ref[group, :, spot]]
            product = dot(
                jnp.concatenate(pieces, axis=0), weight_ref[slot], 1, 1 if transposed else 0
            )
            found.append((lanes(place % width_blocks, size), product))
        for spot, product in found:
            total_ref[:, spot] += product

    over_owners(matrix, kept_ref, weight_refs, body)
    for index, out_ref in enumerate(out_refs):
        chunk, group = index // mem_count, index % mem_count
        span = out_ref.shape[1]
        out_ref[...] = total_ref[
            group * 2 * half : (group + 1) * 2 * half, chunk * span : (chunk + 1) * span
        ]


def gradient_kernel(matrix, width_blocks, mem_count, hid_count, kept_ref, place_ref, far_place_ref, *refs):
    row_ref, own_ref, pair_ref = refs[:3]
    late_refs = refs[3 : 3 + hid_count]
    keep_ref, send_ref, late_ref = refs[3 + hid_count :]
    cells, owned, size = keep_ref.shape[:3]
    tok_count = lax.axis_size(TOK)
    tok = lax.axis_index(TOK)
    rows = row_ref.shape[0] // mem_count
    part = rows // tok_count
    step = rows // hid_count
    turn = relative(tok_count)
    for block, source in enumerate(late_refs):
        start = block * step
        spot = ((start // part) ^ turn) * part + start % part
        for group in range(mem_count):
            late_ref[pl.ds(pl.multiple_of(spot + group * rows, step), step), :] = source[matrix, group]

    for cell in range(cells):
        places, values = ((place_ref, row_ref), (far_place_ref, late_ref))[cell]
        for side, out_ref in enumerate((keep_ref, send_ref)):
            first, count = owner_count(kept_ref, matrix, tok ^ (2 * cell), tok ^ side, owned)

            def body(slots):
                for slot in slots:
                    place = places[matrix, first + slot]
                    hidden = lanes(place // width_blocks, size)
                    width = lanes(place % width_blocks, size)
                    total = None
                    for group in range(mem_count):
                        wide = values[group * rows : (group + 1) * rows, width]
                        deep = jnp.concatenate(
                            [own_ref[group, :, hidden], pair_ref[group, :, hidden]], axis=0
                        )
                        left, right = (wide, deep) if matrix == 0 else (deep, wide)
                        term = dot(left, right, 0, 0).astype(jnp.bfloat16).astype(jnp.float32)
                        total = term if total is None else total + term
                    out_ref[cell, slot] = total

            over_slots(count, body)

            def clear(slot, carry):
                out_ref[cell, slot] = jnp.zeros((size, size), jnp.float32)
                return carry

            lax.fori_loop(count, owned, clear, 0)


def update_kernel(matrix, owned, kept_ref, keep_ref, swap_ref, weight_ref, moment_ref, variance_ref, *refs):
    out_refs = refs[-3:]
    turn = pl.program_id(0)
    tok = lax.axis_index(TOK)
    run = weight_ref.shape[3]
    _, count = owner_count(kept_ref, matrix, tok ^ turn, tok, owned)
    count = jnp.clip(count - pl.program_id(1) * run, 0, run)

    def update_from(grad_ref):
        def update(slot, carry):
            at = (0, 0, 0, slot)
            fresh = adam_step(weight_ref[at], moment_ref[at], variance_ref[at], grad_ref[0, slot])
            for out_ref, value in zip(out_refs, fresh):
                out_ref[at] = value
            return carry

        lax.fori_loop(0, count, update, 0)

    pl.when(turn % 2 == 0)(functools.partial(update_from, keep_ref))
    pl.when(turn % 2 == 1)(functools.partial(update_from, swap_ref))

    def keep(slot, carry):
        at = (0, 0, 0, slot)
        for out_ref, value_ref in zip(out_refs, (weight_ref, moment_ref, variance_ref)):
            out_ref[at] = value_ref[at]
        return carry

    lax.fori_loop(count, run, keep, 0)


def join_kernel(pair_major, keep_ref, swap_ref, *out_refs):
    part = out_refs[0].shape[1]
    for index, out_ref in enumerate(out_refs):
        for inner in range(out_ref.shape[0]):
            group, shift = (inner, index) if pair_major else (index, inner)
            at = slice(shift * part, (shift + 1) * part)
            out_ref[inner] = keep_ref[group, at] + swap_ref[group, at]


def split_kernel(*refs):
    inner = refs[0].shape[0]
    for index, out_ref in enumerate(refs[-inner:]):
        total = refs[0][index]
        for ref in refs[1:-inner]:
            total = total + ref[index]
        out_ref[...] = total


def total_of(refs):
    total = refs[0][...]
    for ref in refs[1:]:
        total = total + ref[...]
    return total


def activate_kernel(split, *refs):
    *part_refs, hidden_ref, preact_ref = refs
    span = preact_ref.shape[1] // 2
    for side, side_refs in enumerate((part_refs[:split], part_refs[split:])):
        at = slice(side * span, (side + 1) * span)
        preact = total_of(side_refs)
        preact_ref[:, at] = preact
        hidden_ref[:, at] = activate(preact).astype(jnp.bfloat16)


def slope_kernel(split, *refs):
    *part_refs, preact_ref, out_ref = refs
    span = preact_ref.shape[1] // 2
    for side, side_refs in enumerate((part_refs[:split], part_refs[split:])):
        at = slice(side * span, (side + 1) * span)
        slope = gelu_slope(preact_ref[:, at])
        out_ref[:, at] = (total_of(side_refs) * slope).astype(jnp.bfloat16)


def narrow_kernel(block_ref, *out_refs):
    for turn, out_ref in enumerate(out_refs):

        @pl.when(pl.program_id(0) == turn)
        def _():
            out_ref[...] = block_ref[0, 0, 0].astype(jnp.bfloat16)


SCALARS = pl.BlockSpec(memory_space=pltpu.SMEM)
WHOLE = pl.BlockSpec(memory_space=pltpu.VMEM)
ANYWHERE = pl.BlockSpec(memory_space=pl.ANY)


def call(kernel, outs, scalars, arrays, flops, scratch=(), scratch_sizes=()):
    moved = sum(math_size(a) for a in (*arrays, *outs))
    return pl.pallas_call(
        kernel,
        out_shape=outs,
        in_specs=[SCALARS] * len(scalars) + [WHOLE] * len(arrays),
        out_specs=[WHOLE] * len(outs),
        scratch_shapes=scratch,
        compiler_params=grant(moved + sum(scratch_sizes)),
        cost_estimate=pl.CostEstimate(flops=flops, bytes_accessed=moved, transcendentals=0),
    )(*scalars, *arrays)


def math_size(array):
    return math.prod(array.shape) * array.dtype.itemsize


def grant(needed):
    return pltpu.CompilerParams(vmem_limit_bytes=needed + VMEM_SPARE)


def on_device(inputs, cotangent, blocks, first_moment, second_moment, places, kept_counts):
    mem_count = lax.axis_size(MEM)
    tok_count = lax.axis_size(TOK)
    hid_count = lax.axis_size(HID)
    block_size = blocks.shape[-1]
    owned_slots = blocks.shape[3]
    local_slots = owned_slots * tok_count
    width_blocks = inputs.shape[1] // block_size
    hidden_span = FFW // hid_count
    rows = inputs.shape[0] * hid_count
    other = tok_count // 2
    half = rows // 2
    part = rows // tok_count
    chunks = CHUNKS
    kept = kept_counts[:, :, 0]
    place_ids = places[:, 0, 0]
    scalars = (kept, place_ids)
    f32, bf16 = jnp.float32, jnp.bfloat16

    def shift_hid(array, shift):
        return lax.ppermute(array, HID, [(i, (i + shift) % hid_count) for i in range(hid_count)])

    def shift_mem(array, shift):
        return lax.ppermute(array, MEM, [(i, (i + shift) % mem_count) for i in range(mem_count)])

    def flip_tok(array, bit):
        return lax.ppermute(array, TOK, [(i, i ^ bit) for i in range(tok_count)])

    def across(array, mem_shift, tok_shift):
        table = []
        for m in range(mem_count):
            for t in range(tok_count):
                to = ((m - mem_shift) % mem_count) * tok_count + (t ^ (2 * tok_shift))
                table.append((m * tok_count + t, to))
        return lax.ppermute(array, (MEM, TOK), table)

    peers = [(j, b) for j in range(mem_count) for b in range(other)][1:]

    def gather_rows(array):
        pieces = [array] + [shift_hid(array, k) for k in range(1, hid_count)]
        near = jnp.concatenate(pieces, axis=0)
        return [near] + [shift_mem(near, j) for j in range(1, mem_count)]

    def gather_small(array):
        found = [array] + [shift_mem(array, j) for j in range(1, mem_count)]
        own = jnp.stack(found)
        return [own] + [shift_hid(own, k) for k in range(1, hid_count)]

    def gather_late():
        both = flip_tok(jnp.stack([inputs, cotangent]), 2)
        found = [both] + [shift_mem(both, j) for j in range(1, mem_count)]
        moved = jnp.stack(found, axis=1)
        return [moved] + [shift_hid(moved, k) for k in range(1, hid_count)]

    def gather_weights(matrix):
        shape = (owned_slots, block_size, block_size)
        narrow = pl.pallas_call(
            narrow_kernel,
            grid=(tok_count,),
            out_shape=[jax.ShapeDtypeStruct(shape, bf16)] * tok_count,
            in_specs=[
                pl.BlockSpec(
                    (1, 1, 1) + blocks.shape[3:],
                    lambda i: (matrix, lax.axis_index(TOK) ^ i, 0, 0, 0, 0),
                )
            ],
            out_specs=[pl.BlockSpec(shape, lambda i: (0, 0, 0))] * tok_count,
            compiler_params=grant(owned_slots * block_size**2 * 4 * (2 + tok_count)),
        )(blocks)
        moved = [flip_tok(narrow[r], r) for r in range(1, tok_count)]
        return [narrow[0], *moved]

    def forward(matrix, transposed, row_groups, weights):
        kernel = functools.partial(
            forward_kernel, matrix, transposed, width_blocks, tok_count, hid_count, mem_count
        )
        width = row_groups[0].shape[-1]
        outs = [
            jax.ShapeDtypeStruct((mem_count * rows, width), bf16),
            jax.ShapeDtypeStruct((mem_count, half, hidden_span), f32),
            jax.ShapeDtypeStruct((mem_count, half, hidden_span), f32),
        ]
        flops = 2 * mem_count * rows * local_slots * block_size * block_size
        return call(kernel, outs, scalars, [*row_groups, *weights], flops)

    def half_columns(kernel, outs, arrays, side, steps):
        span = hidden_span // 2 // steps

        def spec(shape, shift):
            lead = len(shape) - 1
            return pl.BlockSpec(tuple(shape[:-1]) + (span,), lambda i: (0,) * lead + (i + shift,))

        shift = side * steps
        needed = sum(math_size(a) for a in outs) // steps * 2
        needed += sum(math_size(a) for a in arrays) // steps
        return pl.pallas_call(
            kernel,
            grid=(steps,),
            out_shape=outs,
            in_specs=[spec(a.shape, shift) for a in arrays],
            out_specs=[spec(o.shape, 0) for o in outs],
            compiler_params=grant(needed),
            cost_estimate=pl.CostEstimate(
                flops=sum(math.prod(o.shape) for o in outs) * 2,
                bytes_accessed=needed * steps // 2,
                transcendentals=0,
            ),
        )(*arrays)

    def reduce_plane(keep, send):
        swap = flip_tok(send, 1)
        span = hidden_span // 2

        def array(*lead):
            return jax.ShapeDtypeStruct((*lead, span), f32)

        by_mem = half_columns(
            functools.partial(join_kernel, False),
            [array(other, part)] * mem_count,
            [keep, swap],
            0,
            2,
        )
        by_pair = half_columns(
            functools.partial(join_kernel, True),
            [array(mem_count, part)] * other,
            [keep, swap],
            1,
            2,
        )
        mem_terms = [by_mem[0]] + [shift_mem(by_mem[j], -j) for j in range(1, mem_count)]
        pair_terms = [by_pair[0]] + [flip_tok(by_pair[b], 2 * b) for b in range(1, other)]
        mine, *rest = call(split_kernel, [array(part)] * other, (), mem_terms, part)
        first = [mine] + [flip_tok(x, 2 * b) for b, x in enumerate(rest, 1)]
        mine, *rest = call(split_kernel, [array(part)] * mem_count, (), pair_terms, part)
        second = [mine] + [shift_mem(x, -j) for j, x in enumerate(rest, 1)]
        return first, second

    def gather_plane(piece):
        found = {(0, 0): piece}
        for j, b in peers:
            found[(-j) % mem_count, b] = across(piece, j, b)
        near = jnp.concatenate(
            [found[j, b] for j in range(mem_count) for b in range(other)], axis=0
        ).reshape(mem_count, half, hidden_span)
        return near, flip_tok(near, 1)

    def backward(matrix, transposed, near, far, weights):
        kernel = functools.partial(backward_kernel, matrix, transposed, width_blocks, mem_count)
        span = inputs.shape[1] // chunks
        outs = [jax.ShapeDtypeStruct((rows, span), f32)] * (mem_count * chunks)
        flops = 2 * mem_count * rows * local_slots * block_size * block_size
        scratch = [pltpu.VMEM((mem_count * rows, inputs.shape[1]), f32)]
        sizes = [mem_count * rows * inputs.shape[1] * 4]
        return call(kernel, outs, scalars, [near, far, *weights], flops, scratch, sizes)

    turn = relative(tok_count)
    step = inputs.shape[0]

    def reduce_rows(found):
        results = []
        for chunk in range(chunks):
            groups = found[chunk * mem_count : (chunk + 1) * mem_count]
            total = groups[0]
            for j in range(1, mem_count):
                total = total + shift_mem(groups[j], -j)
            result = None
            for k in range(hid_count):
                start = k * step
                spot = ((start // part) ^ turn) * part + start % part
                piece = lax.dynamic_slice_in_dim(total, spot, step, 0)
                if k:
                    piece = shift_hid(piece, -k)
                result = piece if result is None else result + piece
            results.append(result.astype(bf16))
        return jnp.concatenate(results, axis=1)

    def gradient(matrix, row_values, near, far, late):
        kernel = functools.partial(gradient_kernel, matrix, width_blocks, mem_count, hid_count)
        outs = [
            jax.ShapeDtypeStruct((other, owned_slots, block_size, block_size), f32),
            jax.ShapeDtypeStruct((other, owned_slots, block_size, block_size), f32),
        ]
        flops = 2 * mem_count * rows * local_slots * block_size * block_size
        keep, send = call(
            kernel,
            outs,
            (kept, place_ids, far_place_ids),
            [row_values, near, far, *late],
            flops,
            [pltpu.VMEM(row_values.shape, bf16)],
            [math_size(row_values)],
        )
        return keep, flip_tok(send, 1)

    def update(matrix, grads, held):
        splits = 2 if owned_slots % 2 == 0 else 1
        run = owned_slots // splits
        state_spec = pl.BlockSpec(
            (1, 1, 1, run, block_size, block_size),
            lambda i, j: (matrix, lax.axis_index(TOK) ^ i, 0, j, 0, 0),
        )
        grad_spec = pl.BlockSpec((1, run, block_size, block_size), lambda i, j: (i // 2, j, 0, 0))
        state = (blocks, first_moment, second_moment)
        size = local_slots * block_size * block_size
        return pl.pallas_call(
            functools.partial(update_kernel, matrix, owned_slots),
            grid=(tok_count, splits),
            out_shape=[jax.ShapeDtypeStruct(s.shape, f32) for s in state],
            in_specs=[SCALARS, grad_spec, grad_spec] + [state_spec] * 3 + [ANYWHERE] * len(held),
            out_specs=[state_spec] * 3,
            input_output_aliases={6 + i: i for i in range(len(held))},
            compiler_params=grant(44 * 2**20),
            cost_estimate=pl.CostEstimate(
                flops=size * 12, bytes_accessed=size * 28, transcendentals=size
            ),
        )(kept, *grads, *state, *held)

    far_place_ids = flip_tok(place_ids, 2)
    input_groups = gather_rows(inputs)
    weights_first = gather_weights(0)
    cotangent_groups = gather_small(cotangent)
    weights_second = gather_weights(1)
    late = gather_late()
    token_rows, *pre_part = forward(0, False, input_groups, weights_first)
    pre_terms = reduce_plane(*pre_part)
    grad_rows, *back_part = forward(1, True, cotangent_groups, weights_second)
    back_terms = reduce_plane(*back_part)
    piece = (part, hidden_span)
    outs = [jax.ShapeDtypeStruct(piece, bf16), jax.ShapeDtypeStruct(piece, f32)]
    kernel = functools.partial(activate_kernel, len(pre_terms[0]))
    hidden_piece, preact = call(kernel, outs, (), [*pre_terms[0], *pre_terms[1]], part)
    hidden = gather_plane(hidden_piece)
    kernel = functools.partial(slope_kernel, len(back_terms[0]))
    arrays = [*back_terms[0], *back_terms[1], preact]
    (grad_piece,) = call(kernel, outs[:1], (), arrays, part)
    pre_grad = gather_plane(grad_piece)
    layer_out = reduce_rows(backward(1, False, *hidden, weights_second))
    grad_in = reduce_rows(backward(0, True, *pre_grad, weights_first))
    second_grad = gradient(1, grad_rows, *hidden, late)
    first_grad = gradient(0, token_rows, *pre_grad, late)
    held = update(1, second_grad, ())
    return (layer_out, grad_in, *update(0, first_grad, held))


def solution(mesh):
    return jax.shard_map(
        on_device,
        mesh=mesh,
        in_specs=(
            P((MEM, HID), TOK),
            P((MEM, HID), TOK),
            P(None, None, HID, (MEM, TOK), None, None),
            P(None, None, HID, (MEM, TOK), None, None),
            P(None, None, HID, (MEM, TOK), None, None),
            P(None, TOK, HID, None),
            P(None, None, HID),
        ),
        out_specs=(
            P((MEM, HID), TOK),
            P((MEM, HID), TOK),
            P(None, None, HID, (MEM, TOK), None, None),
            P(None, None, HID, (MEM, TOK), None, None),
            P(None, None, HID, (MEM, TOK), None, None),
        ),
        check_vma=False,
    )
```

```python
import functools
import math

import jax
import jax.numpy as jnp
from jax import lax
from jax.experimental import pallas as pl
from jax.experimental.pallas import tpu as pltpu
from jax.sharding import PartitionSpec as P


FFW = 24576
STEP = 10


GELU_ROOT = 0.7978845608028654
GELU_CUBIC = 0.044715
BETA_FIRST = 0.9
BETA_SECOND = 0.95
LEARN_RATE = 0.001
WEIGHT_DECAY = 0.1
ADAM_EPSILON = 1e-08
VMEM_SPARE = 3 * 2**19
UNROLL = 4
CHUNKS = 2
MEM, HID, TOK = "mem", "hid", "tok"


def activate(values):
    tangent = jnp.tanh(GELU_ROOT * (values + GELU_CUBIC * values * values * values))
    return 0.5 * values * (1.0 + tangent)


def gelu_slope(values):
    tangent = jnp.tanh(GELU_ROOT * (values + GELU_CUBIC * values * values * values))
    return 0.5 * (1.0 + tangent) + 0.5 * values * (1.0 - tangent * tangent) * GELU_ROOT * (
        1.0 + 3.0 * GELU_CUBIC * values * values
    )


def adam_step(weight, moment, variance, gradient):
    new_moment = BETA_FIRST * moment + (1.0 - BETA_FIRST) * gradient
    new_variance = BETA_SECOND * variance + (1.0 - BETA_SECOND) * gradient * gradient
    scaled = (
        new_moment
        / (1.0 - BETA_FIRST**STEP)
        / (jnp.sqrt(new_variance / (1.0 - BETA_SECOND**STEP)) + ADAM_EPSILON)
    )
    new_weight = weight - LEARN_RATE * (scaled + WEIGHT_DECAY * weight)
    return new_weight, new_moment, new_variance


def dot(left, right, left_dim, right_dim):
    return lax.dot_general(
        left, right, (((left_dim,), (right_dim,)), ((), ())), preferred_element_type=jnp.float32
    )


def lanes(index, size):
    return pl.ds(pl.multiple_of(index * size, size), size)


def owner_count(kept_ref, matrix, cell, owner, owned):
    first = (lax.axis_index(MEM) * lax.axis_size(TOK) + owner) * owned
    return first, jnp.clip(kept_ref[matrix, cell] - first, 0, owned)


def over_slots(count, body):
    groups = count // UNROLL

    def run(group, carry):
        body([group * UNROLL + lane for lane in range(UNROLL)])
        return carry

    lax.fori_loop(0, groups, run, 0)

    def single(slot, carry):
        body([slot])
        return carry

    lax.fori_loop(groups * UNROLL, count, single, 0)


def over_owners(matrix, kept_ref, weight_refs, body):
    tok = lax.axis_index(TOK)
    for turn, weight_ref in enumerate(weight_refs):
        owned = weight_ref.shape[0]
        first, count = owner_count(kept_ref, matrix, tok, tok ^ turn, owned)
        over_slots(count, functools.partial(body, weight_ref, first))


def relative(tok_count):
    tok = lax.axis_index(TOK)
    return (tok % 2) * (tok_count // 2) + tok // 2


def forward_kernel(
    matrix, transposed, width_blocks, tok_count, hid_count, mem_count, kept_ref, place_ref, *refs
):
    sources = hid_count if matrix else mem_count
    own_refs, weight_refs, (row_ref, keep_ref, send_ref) = (
        refs[:sources],
        refs[sources:-3],
        refs[-3:],
    )
    half = keep_ref.shape[1]
    _, size = weight_refs[0].shape[:2]
    rows = row_ref.shape[0] // mem_count
    step = rows // hid_count
    part = rows // tok_count
    turn = relative(tok_count)
    for group in range(mem_count):
        for block in range(hid_count):
            start = block * step
            spot = ((start // part) ^ turn) * part + start % part + group * rows
            row_ref[pl.ds(pl.multiple_of(spot, step), step), :] = (
                own_refs[block][group] if matrix else own_refs[group][start : start + step, :]
            )
    keep_ref[...] = jnp.zeros(keep_ref.shape, jnp.float32)
    send_ref[...] = jnp.zeros(send_ref.shape, jnp.float32)

    def body(weight_ref, first, slots):
        found = []
        for slot in slots:
            place = place_ref[matrix, first + slot]
            left = row_ref[:, lanes(place % width_blocks, size)]
            product = dot(left, weight_ref[slot], 1, 1 if transposed else 0)
            found.append((lanes(place // width_blocks, size), product))
        for spot, product in found:
            for group in range(mem_count):
                start = group * rows
                keep_ref[group, :, spot] += product[start : start + half]
                send_ref[group, :, spot] += product[start + half : start + rows]

    over_owners(matrix, kept_ref, weight_refs, body)


def backward_kernel(
    matrix, transposed, width_blocks, mem_count, kept_ref, place_ref, own_ref, pair_ref, *refs
):
    tok_count = lax.axis_size(TOK)
    weight_refs, out_refs, total_ref = refs[:tok_count], refs[tok_count:-1], refs[-1]
    size = weight_refs[0].shape[-1]
    half = own_ref.shape[1]
    total_ref[...] = jnp.zeros(total_ref.shape, jnp.float32)

    def body(weight_ref, first, slots):
        found = []
        for slot in slots:
            place = place_ref[matrix, first + slot]
            spot = lanes(place // width_blocks, size)
            pieces = []
            for group in range(mem_count):
                pieces += [own_ref[group, :, spot], pair_ref[group, :, spot]]
            product = dot(
                jnp.concatenate(pieces, axis=0), weight_ref[slot], 1, 1 if transposed else 0
            )
            found.append((lanes(place % width_blocks, size), product))
        for spot, product in found:
            total_ref[:, spot] += product

    over_owners(matrix, kept_ref, weight_refs, body)
    for index, out_ref in enumerate(out_refs):
        chunk, group = index // mem_count, index % mem_count
        span = out_ref.shape[1]
        out_ref[...] = total_ref[
            group * 2 * half : (group + 1) * 2 * half, chunk * span : (chunk + 1) * span
        ]


def gradient_kernel(matrix, width_blocks, mem_count, hid_count, kept_ref, place_ref, far_place_ref, *refs):
    row_ref, own_ref, pair_ref = refs[:3]
    late_refs = refs[3 : 3 + hid_count]
    keep_ref, send_ref, late_ref = refs[3 + hid_count :]
    cells, owned, size = keep_ref.shape[:3]
    tok_count = lax.axis_size(TOK)
    tok = lax.axis_index(TOK)
    rows = row_ref.shape[0] // mem_count
    part = rows // tok_count
    step = rows // hid_count
    turn = relative(tok_count)
    for block, source in enumerate(late_refs):
        start = block * step
        spot = ((start // part) ^ turn) * part + start % part
        for group in range(mem_count):
            late_ref[pl.ds(pl.multiple_of(spot + group * rows, step), step), :] = source[matrix, group]

    for cell in range(cells):
        places, values = ((place_ref, row_ref), (far_place_ref, late_ref))[cell]
        for side, out_ref in enumerate((keep_ref, send_ref)):
            first, count = owner_count(kept_ref, matrix, tok ^ (2 * cell), tok ^ side, owned)

            def body(slots):
                for slot in slots:
                    place = places[matrix, first + slot]
                    hidden = lanes(place // width_blocks, size)
                    width = lanes(place % width_blocks, size)
                    total = None
                    for group in range(mem_count):
                        wide = values[group * rows : (group + 1) * rows, width]
                        deep = jnp.concatenate(
                            [own_ref[group, :, hidden], pair_ref[group, :, hidden]], axis=0
                        )
                        left, right = (wide, deep) if matrix == 0 else (deep, wide)
                        term = dot(left, right, 0, 0).astype(jnp.bfloat16).astype(jnp.float32)
                        total = term if total is None else total + term
                    out_ref[cell, slot] = total

            over_slots(count, body)

            def clear(slot, carry):
                out_ref[cell, slot] = jnp.zeros((size, size), jnp.float32)
                return carry

            lax.fori_loop(count, owned, clear, 0)


def update_kernel(matrix, owned, kept_ref, keep_ref, swap_ref, weight_ref, moment_ref, variance_ref, *refs):
    out_refs = refs[-3:]
    turn = pl.program_id(0)
    tok = lax.axis_index(TOK)
    run = weight_ref.shape[3]
    _, count = owner_count(kept_ref, matrix, tok ^ turn, tok, owned)
    count = jnp.clip(count - pl.program_id(1) * run, 0, run)

    def update_from(grad_ref):
        def update(slot, carry):
            at = (0, 0, 0, slot)
            fresh = adam_step(weight_ref[at], moment_ref[at], variance_ref[at], grad_ref[0, slot])
            for out_ref, value in zip(out_refs, fresh):
                out_ref[at] = value
            return carry

        lax.fori_loop(0, count, update, 0)

    pl.when(turn % 2 == 0)(functools.partial(update_from, keep_ref))
    pl.when(turn % 2 == 1)(functools.partial(update_from, swap_ref))

    def keep(slot, carry):
        at = (0, 0, 0, slot)
        for out_ref, value_ref in zip(out_refs, (weight_ref, moment_ref, variance_ref)):
            out_ref[at] = value_ref[at]
        return carry

    lax.fori_loop(count, run, keep, 0)


def join_kernel(pair_major, keep_ref, swap_ref, *out_refs):
    part = out_refs[0].shape[1]
    for index, out_ref in enumerate(out_refs):
        for inner in range(out_ref.shape[0]):
            group, shift = (inner, index) if pair_major else (index, inner)
            at = slice(shift * part, (shift + 1) * part)
            out_ref[inner] = keep_ref[group, at] + swap_ref[group, at]


def split_kernel(*refs):
    inner = refs[0].shape[0]
    for index, out_ref in enumerate(refs[-inner:]):
        total = refs[0][index]
        for ref in refs[1:-inner]:
            total = total + ref[index]
        out_ref[...] = total


def total_of(refs):
    total = refs[0][...]
    for ref in refs[1:]:
        total = total + ref[...]
    return total


def activate_kernel(split, *refs):
    *part_refs, hidden_ref, preact_ref = refs
    start = 0
    for side_refs in (part_refs[:split], part_refs[split:]):
        at = slice(start, start + side_refs[0].shape[1])
        start = at.stop
        preact = total_of(side_refs)
        preact_ref[:, at] = preact
        hidden_ref[:, at] = activate(preact).astype(jnp.bfloat16)


def slope_kernel(split, *refs):
    *part_refs, preact_ref, out_ref = refs
    start = 0
    for side_refs in (part_refs[:split], part_refs[split:]):
        at = slice(start, start + side_refs[0].shape[1])
        start = at.stop
        slope = gelu_slope(preact_ref[:, at])
        out_ref[:, at] = (total_of(side_refs) * slope).astype(jnp.bfloat16)


def narrow_kernel(block_ref, *out_refs):
    for turn, out_ref in enumerate(out_refs):

        @pl.when(pl.program_id(0) == turn)
        def _():
            out_ref[...] = block_ref[0, 0, 0].astype(jnp.bfloat16)


SCALARS = pl.BlockSpec(memory_space=pltpu.SMEM)
WHOLE = pl.BlockSpec(memory_space=pltpu.VMEM)
ANYWHERE = pl.BlockSpec(memory_space=pl.ANY)


def call(kernel, outs, scalars, arrays, flops, scratch=(), scratch_sizes=()):
    moved = sum(math_size(a) for a in (*arrays, *outs))
    return pl.pallas_call(
        kernel,
        out_shape=outs,
        in_specs=[SCALARS] * len(scalars) + [WHOLE] * len(arrays),
        out_specs=[WHOLE] * len(outs),
        scratch_shapes=scratch,
        compiler_params=grant(moved + sum(scratch_sizes)),
        cost_estimate=pl.CostEstimate(flops=flops, bytes_accessed=moved, transcendentals=0),
    )(*scalars, *arrays)


def math_size(array):
    return math.prod(array.shape) * array.dtype.itemsize


def grant(needed):
    return pltpu.CompilerParams(vmem_limit_bytes=needed + VMEM_SPARE)


def on_device(inputs, cotangent, blocks, first_moment, second_moment, places, kept_counts):
    mem_count = lax.axis_size(MEM)
    tok_count = lax.axis_size(TOK)
    hid_count = lax.axis_size(HID)
    block_size = blocks.shape[-1]
    owned_slots = blocks.shape[3]
    local_slots = owned_slots * tok_count
    width_blocks = inputs.shape[1] // block_size
    hidden_span = FFW // hid_count
    rows = inputs.shape[0] * hid_count
    other = tok_count // 2
    half = rows // 2
    part = rows // tok_count
    chunks = CHUNKS
    kept = kept_counts[:, :, 0]
    place_ids = places[:, 0, 0]
    scalars = (kept, place_ids)
    f32, bf16 = jnp.float32, jnp.bfloat16

    def shift_hid(array, shift):
        return lax.ppermute(array, HID, [(i, (i + shift) % hid_count) for i in range(hid_count)])

    def shift_mem(array, shift):
        return lax.ppermute(array, MEM, [(i, (i + shift) % mem_count) for i in range(mem_count)])

    def flip_tok(array, bit):
        return lax.ppermute(array, TOK, [(i, i ^ bit) for i in range(tok_count)])

    def across(array, mem_shift, tok_shift):
        table = []
        for m in range(mem_count):
            for t in range(tok_count):
                to = ((m - mem_shift) % mem_count) * tok_count + (t ^ (2 * tok_shift))
                table.append((m * tok_count + t, to))
        return lax.ppermute(array, (MEM, TOK), table)

    def gather_rows(array):
        pieces = [array] + [shift_hid(array, k) for k in range(1, hid_count)]
        near = jnp.concatenate(pieces, axis=0)
        return [near] + [shift_mem(near, j) for j in range(1, mem_count)]

    def gather_small(array):
        found = [array] + [shift_mem(array, j) for j in range(1, mem_count)]
        own = jnp.stack(found)
        return [own] + [shift_hid(own, k) for k in range(1, hid_count)]

    def gather_late():
        both = flip_tok(jnp.stack([inputs, cotangent]), 2)
        found = [both] + [shift_mem(both, j) for j in range(1, mem_count)]
        moved = jnp.stack(found, axis=1)
        return [moved] + [shift_hid(moved, k) for k in range(1, hid_count)]

    def gather_weights(matrix):
        shape = (owned_slots, block_size, block_size)
        narrow = pl.pallas_call(
            narrow_kernel,
            grid=(tok_count,),
            out_shape=[jax.ShapeDtypeStruct(shape, bf16)] * tok_count,
            in_specs=[
                pl.BlockSpec(
                    (1, 1, 1) + blocks.shape[3:],
                    lambda i: (matrix, lax.axis_index(TOK) ^ i, 0, 0, 0, 0),
                )
            ],
            out_specs=[pl.BlockSpec(shape, lambda i: (0, 0, 0))] * tok_count,
            compiler_params=grant(owned_slots * block_size**2 * 4 * (2 + tok_count)),
        )(blocks)
        moved = [flip_tok(narrow[r], r) for r in range(1, tok_count)]
        return [narrow[0], *moved]

    def forward(matrix, transposed, row_groups, weights):
        kernel = functools.partial(
            forward_kernel, matrix, transposed, width_blocks, tok_count, hid_count, mem_count
        )
        width = row_groups[0].shape[-1]
        outs = [
            jax.ShapeDtypeStruct((mem_count * rows, width), bf16),
            jax.ShapeDtypeStruct((mem_count, half, hidden_span), f32),
            jax.ShapeDtypeStruct((mem_count, half, hidden_span), f32),
        ]
        flops = 2 * mem_count * rows * local_slots * block_size * block_size
        return call(kernel, outs, scalars, [*row_groups, *weights], flops)

    mem_span = hidden_span * 5 // 8

    def side_columns(kernel, outs, arrays, side, steps=3):
        whole = hidden_span - mem_span if side else mem_span
        span = whole // steps

        def spec(shape, shift):
            lead = len(shape) - 1
            return pl.BlockSpec(tuple(shape[:-1]) + (span,), lambda i: (0,) * lead + (i + shift,))

        shift = side * mem_span // span
        needed = 2 * (sum(math_size(a) for a in outs) // steps)
        needed += 2 * (sum(math_size(a) // a.shape[-1] * span for a in arrays))
        return pl.pallas_call(
            kernel,
            grid=(steps,),
            out_shape=outs,
            in_specs=[spec(a.shape, shift) for a in arrays],
            out_specs=[spec(o.shape, 0) for o in outs],
            compiler_params=grant(needed),
            cost_estimate=pl.CostEstimate(
                flops=sum(math.prod(o.shape) for o in outs) * 2,
                bytes_accessed=needed * steps // 2,
                transcendentals=0,
            ),
        )(*arrays)

    def reduce_plane(keep, send):
        swap = flip_tok(send, 1)

        def array(side, *lead):
            return jax.ShapeDtypeStruct((*lead, hidden_span - mem_span if side else mem_span), f32)

        kernel = functools.partial(join_kernel, False)
        outs = [array(0, other, part)] * mem_count
        by_mem = side_columns(kernel, outs, [keep, swap], 0)
        kernel = functools.partial(join_kernel, True)
        outs = [array(1, mem_count, part)] * other
        by_pair = side_columns(kernel, outs, [keep, swap], 1)
        mem_terms = [by_mem[0]] + [shift_mem(by_mem[j], -j) for j in range(1, mem_count)]
        pair_terms = [by_pair[0]] + [flip_tok(by_pair[b], 2 * b) for b in range(1, other)]
        mine, *rest = call(split_kernel, [array(0, part)] * other, (), mem_terms, part)
        first = [mine] + [flip_tok(x, 2 * b) for b, x in enumerate(rest, 1)]
        mine, *rest = call(split_kernel, [array(1, part)] * mem_count, (), pair_terms, part)
        second = [mine] + [shift_mem(x, -j) for j, x in enumerate(rest, 1)]
        return first, second

    def gather_plane(piece):
        cut = part // 2
        found = {(0, 0): [piece]}
        for j in range(1, mem_count):
            found[(-j) % mem_count, 0] = [across(piece, j, 0)]
        for b in range(1, other):
            found[0, b] = [across(piece, 0, b)]
        for j in range(1, mem_count):
            for b in range(1, other):
                found[j, b] = [across(found[j, 0][0][:cut], 0, b)]
        for j in range(1, mem_count):
            for b in range(1, other):
                found[(-j) % mem_count, b].append(across(found[0, b][0][cut:], j, 0))
        near = jnp.concatenate(
            [x for j in range(mem_count) for b in range(other) for x in found[j, b]], axis=0
        ).reshape(mem_count, half, hidden_span)
        return near, flip_tok(near, 1)

    def backward(matrix, transposed, near, far, weights):
        kernel = functools.partial(backward_kernel, matrix, transposed, width_blocks, mem_count)
        span = inputs.shape[1] // chunks
        outs = [jax.ShapeDtypeStruct((rows, span), f32)] * (mem_count * chunks)
        flops = 2 * mem_count * rows * local_slots * block_size * block_size
        scratch = [pltpu.VMEM((mem_count * rows, inputs.shape[1]), f32)]
        sizes = [mem_count * rows * inputs.shape[1] * 4]
        return call(kernel, outs, scalars, [near, far, *weights], flops, scratch, sizes)

    turn = relative(tok_count)
    step = inputs.shape[0]

    def reduce_rows(found):
        results = []
        for chunk in range(chunks):
            groups = found[chunk * mem_count : (chunk + 1) * mem_count]
            total = groups[0]
            for j in range(1, mem_count):
                total = total + shift_mem(groups[j], -j)
            result = None
            for k in range(hid_count):
                start = k * step
                spot = ((start // part) ^ turn) * part + start % part
                piece = lax.dynamic_slice_in_dim(total, spot, step, 0)
                if k:
                    piece = shift_hid(piece, -k)
                result = piece if result is None else result + piece
            results.append(result.astype(bf16))
        return jnp.concatenate(results, axis=1)

    def gradient(matrix, row_values, near, far, late):
        kernel = functools.partial(gradient_kernel, matrix, width_blocks, mem_count, hid_count)
        outs = [
            jax.ShapeDtypeStruct((other, owned_slots, block_size, block_size), f32),
            jax.ShapeDtypeStruct((other, owned_slots, block_size, block_size), f32),
        ]
        flops = 2 * mem_count * rows * local_slots * block_size * block_size
        keep, send = call(
            kernel,
            outs,
            (kept, place_ids, far_place_ids),
            [row_values, near, far, *late],
            flops,
            [pltpu.VMEM(row_values.shape, bf16)],
            [math_size(row_values)],
        )
        return keep, flip_tok(send, 1)

    def update(matrix, grads, held):
        splits = 2 if owned_slots % 2 == 0 else 1
        run = owned_slots // splits
        state_spec = pl.BlockSpec(
            (1, 1, 1, run, block_size, block_size),
            lambda i, j: (matrix, lax.axis_index(TOK) ^ i, 0, j, 0, 0),
        )
        grad_spec = pl.BlockSpec((1, run, block_size, block_size), lambda i, j: (i // 2, j, 0, 0))
        state = (blocks, first_moment, second_moment)
        size = local_slots * block_size * block_size
        return pl.pallas_call(
            functools.partial(update_kernel, matrix, owned_slots),
            grid=(tok_count, splits),
            out_shape=[jax.ShapeDtypeStruct(s.shape, f32) for s in state],
            in_specs=[SCALARS, grad_spec, grad_spec] + [state_spec] * 3 + [ANYWHERE] * len(held),
            out_specs=[state_spec] * 3,
            input_output_aliases={6 + i: i for i in range(len(held))},
            compiler_params=grant(44 * 2**20),
            cost_estimate=pl.CostEstimate(
                flops=size * 12, bytes_accessed=size * 28, transcendentals=size
            ),
        )(kept, *grads, *state, *held)

    far_place_ids = flip_tok(place_ids, 2)
    input_groups = gather_rows(inputs)
    weights_first = gather_weights(0)
    cotangent_groups = gather_small(cotangent)
    weights_second = gather_weights(1)
    late = gather_late()
    token_rows, *pre_part = forward(0, False, input_groups, weights_first)
    pre_terms = reduce_plane(*pre_part)
    grad_rows, *back_part = forward(1, True, cotangent_groups, weights_second)
    back_terms = reduce_plane(*back_part)
    piece = (part, hidden_span)
    outs = [jax.ShapeDtypeStruct(piece, bf16), jax.ShapeDtypeStruct(piece, f32)]
    kernel = functools.partial(activate_kernel, len(pre_terms[0]))
    hidden_piece, preact = call(kernel, outs, (), [*pre_terms[0], *pre_terms[1]], part)
    hidden = gather_plane(hidden_piece)
    kernel = functools.partial(slope_kernel, len(back_terms[0]))
    arrays = [*back_terms[0], *back_terms[1], preact]
    (grad_piece,) = call(kernel, outs[:1], (), arrays, part)
    pre_grad = gather_plane(grad_piece)
    layer_out = reduce_rows(backward(1, False, *hidden, weights_second))
    grad_in = reduce_rows(backward(0, True, *pre_grad, weights_first))
    second_grad = gradient(1, grad_rows, *hidden, late)
    first_grad = gradient(0, token_rows, *pre_grad, late)
    held = update(1, second_grad, ())
    return (layer_out, grad_in, *update(0, first_grad, held))


def solution(mesh):
    return jax.shard_map(
        on_device,
        mesh=mesh,
        in_specs=(
            P((MEM, HID), TOK),
            P((MEM, HID), TOK),
            P(None, None, HID, (MEM, TOK), None, None),
            P(None, None, HID, (MEM, TOK), None, None),
            P(None, None, HID, (MEM, TOK), None, None),
            P(None, TOK, HID, None),
            P(None, None, HID),
        ),
        out_specs=(
            P((MEM, HID), TOK),
            P((MEM, HID), TOK),
            P(None, None, HID, (MEM, TOK), None, None),
            P(None, None, HID, (MEM, TOK), None, None),
            P(None, None, HID, (MEM, TOK), None, None),
        ),
        check_vma=False,
    )
```

```python
import functools
import math

import jax
import jax.numpy as jnp
from jax import lax
from jax.experimental import pallas as pl
from jax.experimental.pallas import tpu as pltpu
from jax.sharding import PartitionSpec as P


FFW = 24576
STEP = 10


GELU_ROOT = 0.7978845608028654
GELU_CUBIC = 0.044715
BETA_FIRST = 0.9
BETA_SECOND = 0.95
LEARN_RATE = 0.001
WEIGHT_DECAY = 0.1
ADAM_EPSILON = 1e-08
VMEM_SPARE = 3 * 2**19
UNROLL = 4
CHUNKS = 2
MEM, HID, TOK = "mem", "hid", "tok"


def activate(values):
    tangent = jnp.tanh(GELU_ROOT * (values + GELU_CUBIC * values * values * values))
    return 0.5 * values * (1.0 + tangent)


def gelu_slope(values):
    tangent = jnp.tanh(GELU_ROOT * (values + GELU_CUBIC * values * values * values))
    return 0.5 * (1.0 + tangent) + 0.5 * values * (1.0 - tangent * tangent) * GELU_ROOT * (
        1.0 + 3.0 * GELU_CUBIC * values * values
    )


def adam_step(weight, moment, variance, gradient):
    new_moment = BETA_FIRST * moment + (1.0 - BETA_FIRST) * gradient
    new_variance = BETA_SECOND * variance + (1.0 - BETA_SECOND) * gradient * gradient
    scaled = (
        new_moment
        / (1.0 - BETA_FIRST**STEP)
        / (jnp.sqrt(new_variance / (1.0 - BETA_SECOND**STEP)) + ADAM_EPSILON)
    )
    new_weight = weight - LEARN_RATE * (scaled + WEIGHT_DECAY * weight)
    return new_weight, new_moment, new_variance


def dot(left, right, left_dim, right_dim):
    return lax.dot_general(
        left, right, (((left_dim,), (right_dim,)), ((), ())), preferred_element_type=jnp.float32
    )


def lanes(index, size):
    return pl.ds(pl.multiple_of(index * size, size), size)


def owner_count(kept_ref, matrix, cell, owner, owned):
    first = (lax.axis_index(MEM) * lax.axis_size(TOK) + owner) * owned
    return first, jnp.clip(kept_ref[matrix, cell] - first, 0, owned)


def over_slots(count, body):
    groups = count // UNROLL

    def run(group, carry):
        body([group * UNROLL + lane for lane in range(UNROLL)])
        return carry

    lax.fori_loop(0, groups, run, 0)

    def single(slot, carry):
        body([slot])
        return carry

    lax.fori_loop(groups * UNROLL, count, single, 0)


def start_weights(sources, held_ref, sems):
    copies = [
        pltpu.make_async_copy(source, held_ref.at[index], sems.at[index])
        for index, source in enumerate(sources)
    ]
    for copy in copies:
        copy.start()

    def finish():
        for copy in copies:
            copy.wait()

    return [held_ref.at[index] for index in range(len(sources))], finish


def over_owners(matrix, kept_ref, weight_refs, body):
    tok = lax.axis_index(TOK)
    for turn, weight_ref in enumerate(weight_refs):
        owned = weight_ref.shape[0]
        first, count = owner_count(kept_ref, matrix, tok, tok ^ turn, owned)
        over_slots(count, functools.partial(body, weight_ref, first))


def relative(tok_count):
    tok = lax.axis_index(TOK)
    return (tok % 2) * (tok_count // 2) + tok // 2


def forward_kernel(
    matrix, transposed, width_blocks, tok_count, hid_count, mem_count, kept_ref, place_ref, *refs
):
    sources = hid_count if matrix else mem_count
    own_refs, weight_refs, (row_ref, keep_ref, send_ref) = (
        refs[:sources],
        refs[sources : sources + tok_count],
        refs[sources + tok_count : -2],
    )
    weight_refs, finish = start_weights(weight_refs, *refs[-2:])
    half = keep_ref.shape[1]
    _, size = weight_refs[0].shape[:2]
    rows = row_ref.shape[0] // mem_count
    step = rows // hid_count
    part = rows // tok_count
    turn = relative(tok_count)
    for group in range(mem_count):
        for block in range(hid_count):
            start = block * step
            spot = ((start // part) ^ turn) * part + start % part + group * rows
            row_ref[pl.ds(pl.multiple_of(spot, step), step), :] = (
                own_refs[block][group] if matrix else own_refs[group][start : start + step, :]
            )
    keep_ref[...] = jnp.zeros(keep_ref.shape, jnp.float32)
    send_ref[...] = jnp.zeros(send_ref.shape, jnp.float32)

    def body(weight_ref, first, slots):
        found = []
        for slot in slots:
            place = place_ref[matrix, first + slot]
            left = row_ref[:, lanes(place % width_blocks, size)]
            product = dot(left, weight_ref[slot], 1, 1 if transposed else 0)
            found.append((lanes(place // width_blocks, size), product))
        for spot, product in found:
            for group in range(mem_count):
                start = group * rows
                keep_ref[group, :, spot] += product[start : start + half]
                send_ref[group, :, spot] += product[start + half : start + rows]

    finish()
    over_owners(matrix, kept_ref, weight_refs, body)


def backward_kernel(
    matrix, transposed, width_blocks, mem_count, kept_ref, place_ref, own_ref, pair_ref, *refs
):
    tok_count = lax.axis_size(TOK)
    out_refs, total_ref = refs[tok_count:-3], refs[-1]
    weight_refs, finish = start_weights(refs[:tok_count], *refs[-3:-1])
    size = weight_refs[0].shape[-1]
    half = own_ref.shape[1]
    total_ref[...] = jnp.zeros(total_ref.shape, jnp.float32)

    def body(weight_ref, first, slots):
        found = []
        for slot in slots:
            place = place_ref[matrix, first + slot]
            spot = lanes(place // width_blocks, size)
            pieces = []
            for group in range(mem_count):
                pieces += [own_ref[group, :, spot], pair_ref[group, :, spot]]
            product = dot(
                jnp.concatenate(pieces, axis=0), weight_ref[slot], 1, 1 if transposed else 0
            )
            found.append((lanes(place % width_blocks, size), product))
        for spot, product in found:
            total_ref[:, spot] += product

    finish()
    over_owners(matrix, kept_ref, weight_refs, body)
    for index, out_ref in enumerate(out_refs):
        chunk, group = index // mem_count, index % mem_count
        span = out_ref.shape[1]
        out_ref[...] = total_ref[
            group * 2 * half : (group + 1) * 2 * half, chunk * span : (chunk + 1) * span
        ]


def gradient_kernel(
    matrix, cell, width_blocks, mem_count, kept_ref, place_ref, row_ref, own_ref, pair_ref, *out_refs
):
    owned, size = out_refs[0].shape[:2]
    tok_count = lax.axis_size(TOK)
    tok = lax.axis_index(TOK)
    rows = row_ref.shape[0] // mem_count
    part = rows // tok_count

    def wide_rows(group, width):
        if cell == 0:
            return row_ref[group * rows : (group + 1) * rows, width]
        starts = [group * rows + (p ^ cell) * part for p in range(tok_count)]
        return jnp.concatenate([row_ref[start : start + part, width] for start in starts], axis=0)

    for side, out_ref in enumerate(out_refs):
        first, count = owner_count(kept_ref, matrix, tok ^ (2 * cell), tok ^ side, owned)

        def body(slots):
            for slot in slots:
                place = place_ref[matrix, first + slot]
                hidden = lanes(place // width_blocks, size)
                width = lanes(place % width_blocks, size)
                total = None
                for group in range(mem_count):
                    wide = wide_rows(group, width)
                    deep = jnp.concatenate(
                        [own_ref[group, :, hidden], pair_ref[group, :, hidden]], axis=0
                    )
                    left, right = (wide, deep) if matrix == 0 else (deep, wide)
                    term = dot(left, right, 0, 0).astype(jnp.bfloat16).astype(jnp.float32)
                    total = term if total is None else total + term
                out_ref[slot] = total

        over_slots(count, body)

        def clear(slot, carry):
            out_ref[slot] = jnp.zeros((size, size), jnp.float32)
            return carry

        lax.fori_loop(count, owned, clear, 0)


def update_kernel(matrix, owned, kept_ref, *refs):
    tok_count = lax.axis_size(TOK)
    grad_refs = refs[:tok_count]
    weight_ref, moment_ref, variance_ref = refs[tok_count : tok_count + 3]
    out_refs = refs[-3:]
    turn = pl.program_id(0)
    tok = lax.axis_index(TOK)
    run = weight_ref.shape[3]
    _, count = owner_count(kept_ref, matrix, tok ^ turn, tok, owned)
    count = jnp.clip(count - pl.program_id(1) * run, 0, run)

    def update_from(grad_ref):
        def update(slot, carry):
            at = (0, 0, 0, slot)
            fresh = adam_step(weight_ref[at], moment_ref[at], variance_ref[at], grad_ref[slot])
            for out_ref, value in zip(out_refs, fresh):
                out_ref[at] = value
            return carry

        lax.fori_loop(0, count, update, 0)

    for index, grad_ref in enumerate(grad_refs):
        pl.when(turn == index)(functools.partial(update_from, grad_ref))

    def keep(slot, carry):
        at = (0, 0, 0, slot)
        for out_ref, value_ref in zip(out_refs, (weight_ref, moment_ref, variance_ref)):
            out_ref[at] = value_ref[at]
        return carry

    lax.fori_loop(count, run, keep, 0)


def join_kernel(pair_major, keep_ref, swap_ref, *out_refs):
    part = out_refs[0].shape[1]
    for index, out_ref in enumerate(out_refs):
        for inner in range(out_ref.shape[0]):
            group, shift = (inner, index) if pair_major else (index, inner)
            at = slice(shift * part, (shift + 1) * part)
            out_ref[inner] = keep_ref[group, at] + swap_ref[group, at]


def split_kernel(*refs):
    inner = refs[0].shape[0]
    for index, out_ref in enumerate(refs[-inner:]):
        total = refs[0][index]
        for ref in refs[1:-inner]:
            total = total + ref[index]
        out_ref[...] = total


def total_of(refs):
    total = refs[0][...]
    for ref in refs[1:]:
        total = total + ref[...]
    return total


def activate_kernel(split, *refs):
    *part_refs, hidden_ref, preact_ref = refs
    start = 0
    for side_refs in (part_refs[:split], part_refs[split:]):
        at = slice(start, start + side_refs[0].shape[1])
        start = at.stop
        preact = total_of(side_refs)
        preact_ref[:, at] = preact
        hidden_ref[:, at] = activate(preact).astype(jnp.bfloat16)


def slope_kernel(split, *refs):
    *part_refs, preact_ref, out_ref = refs
    start = 0
    for side_refs in (part_refs[:split], part_refs[split:]):
        at = slice(start, start + side_refs[0].shape[1])
        start = at.stop
        slope = gelu_slope(preact_ref[:, at])
        out_ref[:, at] = (total_of(side_refs) * slope).astype(jnp.bfloat16)


def narrow_kernel(block_ref, *out_refs):
    for turn, out_ref in enumerate(out_refs):

        @pl.when(pl.program_id(0) == turn)
        def _():
            out_ref[...] = block_ref[0, 0, 0].astype(jnp.bfloat16)


SCALARS = pl.BlockSpec(memory_space=pltpu.SMEM)
WHOLE = pl.BlockSpec(memory_space=pltpu.VMEM)
OUTSIDE = pl.BlockSpec(memory_space=pltpu.HBM)
ANYWHERE = pl.BlockSpec(memory_space=pl.ANY)


def call(kernel, outs, scalars, arrays, flops, outside=(), scratch=()):
    if outside:
        scratch = [
            pltpu.VMEM((len(outside), *outside[0].shape), outside[0].dtype),
            pltpu.SemaphoreType.DMA((len(outside),)),
            *scratch,
        ]
    moved = sum(math_size(a) for a in (*arrays, *outs, *outside))
    needed = moved + sum(math_size(x) for x in scratch[2:])
    return pl.pallas_call(
        kernel,
        out_shape=outs,
        in_specs=[SCALARS] * len(scalars) + [WHOLE] * len(arrays) + [OUTSIDE] * len(outside),
        out_specs=[WHOLE] * len(outs),
        scratch_shapes=scratch,
        compiler_params=grant(needed),
        cost_estimate=pl.CostEstimate(flops=flops, bytes_accessed=moved, transcendentals=0),
    )(*scalars, *arrays, *outside)


def math_size(array):
    return math.prod(array.shape) * array.dtype.itemsize


def grant(needed):
    return pltpu.CompilerParams(vmem_limit_bytes=needed + VMEM_SPARE)


def on_device(inputs, cotangent, blocks, first_moment, second_moment, places, kept_counts):
    mem_count = lax.axis_size(MEM)
    tok_count = lax.axis_size(TOK)
    hid_count = lax.axis_size(HID)
    block_size = blocks.shape[-1]
    owned_slots = blocks.shape[3]
    local_slots = owned_slots * tok_count
    width_blocks = inputs.shape[1] // block_size
    hidden_span = FFW // hid_count
    rows = inputs.shape[0] * hid_count
    other = tok_count // 2
    half = rows // 2
    part = rows // tok_count
    chunks = CHUNKS
    kept = kept_counts[:, :, 0]
    place_ids = places[:, 0, 0]
    scalars = (kept, place_ids)
    f32, bf16 = jnp.float32, jnp.bfloat16

    def shift_hid(array, shift):
        return lax.ppermute(array, HID, [(i, (i + shift) % hid_count) for i in range(hid_count)])

    def shift_mem(array, shift):
        return lax.ppermute(array, MEM, [(i, (i + shift) % mem_count) for i in range(mem_count)])

    def flip_tok(array, bit):
        return lax.ppermute(array, TOK, [(i, i ^ bit) for i in range(tok_count)])

    def across(array, mem_shift, tok_shift):
        table = []
        for m in range(mem_count):
            for t in range(tok_count):
                to = ((m - mem_shift) % mem_count) * tok_count + (t ^ (2 * tok_shift))
                table.append((m * tok_count + t, to))
        return lax.ppermute(array, (MEM, TOK), table)

    def gather_rows(array):
        pieces = [array] + [shift_hid(array, k) for k in range(1, hid_count)]
        near = jnp.concatenate(pieces, axis=0)
        return [near] + [shift_mem(near, j) for j in range(1, mem_count)]

    def gather_small(array):
        found = [array] + [shift_mem(array, j) for j in range(1, mem_count)]
        own = jnp.stack(found)
        return [own] + [shift_hid(own, k) for k in range(1, hid_count)]

    def gather_weights(matrix):
        shape = (owned_slots, block_size, block_size)
        narrow = pl.pallas_call(
            narrow_kernel,
            grid=(tok_count,),
            out_shape=[jax.ShapeDtypeStruct(shape, bf16)] * tok_count,
            in_specs=[
                pl.BlockSpec(
                    (1, 1, 1) + blocks.shape[3:],
                    lambda i: (matrix, lax.axis_index(TOK) ^ i, 0, 0, 0, 0),
                )
            ],
            out_specs=[pl.BlockSpec(shape, lambda i: (0, 0, 0))] * tok_count,
            compiler_params=grant(owned_slots * block_size**2 * 4 * (2 + tok_count)),
        )(blocks)
        moved = [flip_tok(narrow[r], r) for r in range(1, tok_count)]
        return [narrow[0], *moved]

    def forward(matrix, transposed, row_groups, weights):
        kernel = functools.partial(
            forward_kernel, matrix, transposed, width_blocks, tok_count, hid_count, mem_count
        )
        width = row_groups[0].shape[-1]
        outs = [
            jax.ShapeDtypeStruct((mem_count * rows, width), bf16),
            jax.ShapeDtypeStruct((mem_count, half, hidden_span), f32),
            jax.ShapeDtypeStruct((mem_count, half, hidden_span), f32),
        ]
        flops = 2 * mem_count * rows * local_slots * block_size * block_size
        return call(kernel, outs, scalars, row_groups, flops, weights)

    mem_span = hidden_span // 2

    def side_columns(kernel, outs, arrays, side, steps=3):
        whole = hidden_span - mem_span if side else mem_span
        span = whole // steps

        def spec(shape, shift):
            lead = len(shape) - 1
            return pl.BlockSpec(tuple(shape[:-1]) + (span,), lambda i: (0,) * lead + (i + shift,))

        shift = side * mem_span // span
        needed = 2 * (sum(math_size(a) for a in outs) // steps)
        needed += 2 * (sum(math_size(a) // a.shape[-1] * span for a in arrays))
        return pl.pallas_call(
            kernel,
            grid=(steps,),
            out_shape=outs,
            in_specs=[spec(a.shape, shift) for a in arrays],
            out_specs=[spec(o.shape, 0) for o in outs],
            compiler_params=grant(needed),
            cost_estimate=pl.CostEstimate(
                flops=sum(math.prod(o.shape) for o in outs) * 2,
                bytes_accessed=needed * steps // 2,
                transcendentals=0,
            ),
        )(*arrays)

    def reduce_plane(keep, send):
        swap = flip_tok(send, 1)

        def array(side, *lead):
            return jax.ShapeDtypeStruct((*lead, hidden_span - mem_span if side else mem_span), f32)

        kernel = functools.partial(join_kernel, False)
        outs = [array(0, other, part)] * mem_count
        by_mem = side_columns(kernel, outs, [keep, swap], 0)
        kernel = functools.partial(join_kernel, True)
        outs = [array(1, mem_count, part)] * other
        by_pair = side_columns(kernel, outs, [keep, swap], 1)
        mem_terms = [by_mem[0]] + [shift_mem(by_mem[j], -j) for j in range(1, mem_count)]
        pair_terms = [by_pair[0]] + [flip_tok(by_pair[b], 2 * b) for b in range(1, other)]
        mine, *rest = call(split_kernel, [array(0, part)] * other, (), mem_terms, part)
        first = [mine] + [flip_tok(x, 2 * b) for b, x in enumerate(rest, 1)]
        mine, *rest = call(split_kernel, [array(1, part)] * mem_count, (), pair_terms, part)
        second = [mine] + [shift_mem(x, -j) for j, x in enumerate(rest, 1)]
        return first, second

    peers = [(j, b) for j in range(mem_count) for b in range(other)][1:]

    def gather_plane(piece):
        found = {(0, 0): piece}
        for j, b in peers:
            found[(-j) % mem_count, b] = across(piece, j, b)
        near = jnp.concatenate(
            [found[j, b] for j in range(mem_count) for b in range(other)], axis=0
        ).reshape(mem_count, half, hidden_span)
        return near, flip_tok(near, 1)

    def backward(matrix, transposed, near, far, weights):
        kernel = functools.partial(backward_kernel, matrix, transposed, width_blocks, mem_count)
        span = inputs.shape[1] // chunks
        outs = [jax.ShapeDtypeStruct((rows, span), f32)] * (mem_count * chunks)
        flops = 2 * mem_count * rows * local_slots * block_size * block_size
        scratch = [pltpu.VMEM((mem_count * rows, inputs.shape[1]), f32)]
        return call(kernel, outs, scalars, [near, far], flops, weights, scratch)

    turn = relative(tok_count)
    step = inputs.shape[0]

    def reduce_rows(found):
        results = []
        for chunk in range(chunks):
            groups = found[chunk * mem_count : (chunk + 1) * mem_count]
            total = groups[0]
            for j in range(1, mem_count):
                total = total + shift_mem(groups[j], -j)
            result = None
            for k in range(hid_count):
                start = k * step
                spot = ((start // part) ^ turn) * part + start % part
                piece = lax.dynamic_slice_in_dim(total, spot, step, 0)
                if k:
                    piece = shift_hid(piece, -k)
                result = piece if result is None else result + piece
            results.append(result.astype(bf16))
        return jnp.concatenate(results, axis=1)

    def gradient(matrix, cell, ids, row_values, near, far):
        kernel = functools.partial(gradient_kernel, matrix, cell, width_blocks, mem_count)
        outs = [jax.ShapeDtypeStruct((owned_slots, block_size, block_size), f32)] * 2
        flops = 2 * mem_count * rows * owned_slots * 2 * block_size * block_size
        keep, send = call(kernel, outs, (kept, ids), [row_values, near, far], flops)
        return keep, flip_tok(send, 1)

    def update(matrix, grads, held):
        splits = 2 if owned_slots % 2 == 0 else 1
        run = owned_slots // splits
        state_spec = pl.BlockSpec(
            (1, 1, 1, run, block_size, block_size),
            lambda i, j: (matrix, lax.axis_index(TOK) ^ i, 0, j, 0, 0),
        )

        def grad_spec(turn):
            return pl.BlockSpec(
                (run, block_size, block_size),
                lambda i, j: (jnp.where(i < turn, 0, jnp.where(i > turn, splits - 1, j)), 0, 0),
            )

        state = (blocks, first_moment, second_moment)
        size = local_slots * block_size * block_size
        return pl.pallas_call(
            functools.partial(update_kernel, matrix, owned_slots),
            grid=(tok_count, splits),
            out_shape=[jax.ShapeDtypeStruct(s.shape, f32) for s in state],
            in_specs=[SCALARS]
            + [grad_spec(turn) for turn in range(tok_count)]
            + [state_spec] * 3
            + [ANYWHERE] * len(held),
            out_specs=[state_spec] * 3,
            input_output_aliases={4 + tok_count + i: i for i in range(len(held))},
            compiler_params=grant(44 * 2**20),
            cost_estimate=pl.CostEstimate(
                flops=size * 12, bytes_accessed=size * 28, transcendentals=size
            ),
        )(kept, *grads, *state, *held)

    far_place_ids = flip_tok(place_ids, 2)
    input_groups = gather_rows(inputs)
    weights_first = gather_weights(0)
    cotangent_groups = gather_small(cotangent)
    weights_second = gather_weights(1)
    token_rows, *pre_part = forward(0, False, input_groups, weights_first)
    pre_terms = reduce_plane(*pre_part)
    grad_rows, *back_part = forward(1, True, cotangent_groups, weights_second)
    back_terms = reduce_plane(*back_part)
    piece = (part, hidden_span)
    outs = [jax.ShapeDtypeStruct(piece, bf16), jax.ShapeDtypeStruct(piece, f32)]
    kernel = functools.partial(activate_kernel, len(pre_terms[0]))
    hidden_piece, preact = call(kernel, outs, (), [*pre_terms[0], *pre_terms[1]], part)
    hidden = gather_plane(hidden_piece)
    kernel = functools.partial(slope_kernel, len(back_terms[0]))
    arrays = [*back_terms[0], *back_terms[1], preact]
    (grad_piece,) = call(kernel, outs[:1], (), arrays, part)
    pre_grad = gather_plane(grad_piece)
    layer_out = reduce_rows(backward(1, False, *hidden, weights_second))
    grad_in = reduce_rows(backward(0, True, *pre_grad, weights_first))
    far_grad_rows = flip_tok(grad_rows, 2)
    far_token_rows = flip_tok(token_rows, 2)
    second_grad = [
        *gradient(1, 0, place_ids, grad_rows, *hidden),
        *gradient(1, 1, far_place_ids, far_grad_rows, *hidden),
    ]
    first_grad = [
        *gradient(0, 0, place_ids, token_rows, *pre_grad),
        *gradient(0, 1, far_place_ids, far_token_rows, *pre_grad),
    ]
    held = update(1, second_grad, ())
    return (layer_out, grad_in, *update(0, first_grad, held))


def solution(mesh):
    return jax.shard_map(
        on_device,
        mesh=mesh,
        in_specs=(
            P((MEM, HID), TOK),
            P((MEM, HID), TOK),
            P(None, None, HID, (MEM, TOK), None, None),
            P(None, None, HID, (MEM, TOK), None, None),
            P(None, None, HID, (MEM, TOK), None, None),
            P(None, TOK, HID, None),
            P(None, None, HID),
        ),
        out_specs=(
            P((MEM, HID), TOK),
            P((MEM, HID), TOK),
            P(None, None, HID, (MEM, TOK), None, None),
            P(None, None, HID, (MEM, TOK), None, None),
            P(None, None, HID, (MEM, TOK), None, None),
        ),
        check_vma=False,
    )
```

```python
import functools
import math

import jax
import jax.numpy as jnp
from jax import lax
from jax.experimental import pallas as pl
from jax.experimental.pallas import tpu as pltpu
from jax.sharding import PartitionSpec as P


FFW = 24576
STEP = 10


GELU_ROOT = 0.7978845608028654
GELU_CUBIC = 0.044715
BETA_FIRST = 0.9
BETA_SECOND = 0.95
LEARN_RATE = 0.001
WEIGHT_DECAY = 0.1
ADAM_EPSILON = 1e-08
VMEM_SPARE = 3 * 2**19
UNROLL = 4
CHUNKS = 2
MEM, HID, TOK = "mem", "hid", "tok"


def activate(values):
    tangent = jnp.tanh(GELU_ROOT * (values + GELU_CUBIC * values * values * values))
    return 0.5 * values * (1.0 + tangent)


def gelu_slope(values):
    tangent = jnp.tanh(GELU_ROOT * (values + GELU_CUBIC * values * values * values))
    return 0.5 * (1.0 + tangent) + 0.5 * values * (1.0 - tangent * tangent) * GELU_ROOT * (
        1.0 + 3.0 * GELU_CUBIC * values * values
    )


def adam_step(weight, moment, variance, gradient):
    new_moment = BETA_FIRST * moment + (1.0 - BETA_FIRST) * gradient
    new_variance = BETA_SECOND * variance + (1.0 - BETA_SECOND) * gradient * gradient
    scaled = (
        new_moment
        / (1.0 - BETA_FIRST**STEP)
        / (jnp.sqrt(new_variance / (1.0 - BETA_SECOND**STEP)) + ADAM_EPSILON)
    )
    new_weight = weight - LEARN_RATE * (scaled + WEIGHT_DECAY * weight)
    return new_weight, new_moment, new_variance


def dot(left, right, left_dim, right_dim):
    return lax.dot_general(
        left, right, (((left_dim,), (right_dim,)), ((), ())), preferred_element_type=jnp.float32
    )


def lanes(index, size):
    return pl.ds(pl.multiple_of(index * size, size), size)


def owner_count(kept_ref, matrix, cell, owner, owned):
    first = (lax.axis_index(MEM) * lax.axis_size(TOK) + owner) * owned
    return first, jnp.clip(kept_ref[matrix, cell] - first, 0, owned)


def over_slots(count, body):
    groups = count // UNROLL

    def run(group, carry):
        body([group * UNROLL + lane for lane in range(UNROLL)])
        return carry

    lax.fori_loop(0, groups, run, 0)

    def single(slot, carry):
        body([slot])
        return carry

    lax.fori_loop(groups * UNROLL, count, single, 0)


def start_weights(sources, held_ref, sems):
    copies = [
        pltpu.make_async_copy(source, held_ref.at[index], sems.at[index])
        for index, source in enumerate(sources)
    ]
    for copy in copies:
        copy.start()

    def finish():
        for copy in copies:
            copy.wait()

    return [held_ref.at[index] for index in range(len(sources))], finish


def over_owners(matrix, kept_ref, weight_refs, body):
    tok = lax.axis_index(TOK)
    for turn, weight_ref in enumerate(weight_refs):
        owned = weight_ref.shape[0]
        first, count = owner_count(kept_ref, matrix, tok, tok ^ turn, owned)
        over_slots(count, functools.partial(body, weight_ref, first))


def relative(tok_count):
    tok = lax.axis_index(TOK)
    return (tok % 2) * (tok_count // 2) + tok // 2


def forward_kernel(
    matrix, transposed, width_blocks, tok_count, hid_count, mem_count, kept_ref, place_ref, *refs
):
    sources = hid_count if matrix else mem_count
    own_refs = refs[:sources]
    row_ref, keep_ref, send_ref, held_ref, sems = refs[sources + tok_count :]
    weight_refs, finish = start_weights(refs[sources : sources + tok_count], held_ref, sems)
    half = keep_ref.shape[1]
    _, size = weight_refs[0].shape[:2]
    rows = row_ref.shape[0] // mem_count
    step = rows // hid_count
    part = rows // tok_count
    turn = relative(tok_count)
    for group in range(mem_count):
        for block in range(hid_count):
            start = block * step
            spot = ((start // part) ^ turn) * part + start % part + group * rows
            row_ref[pl.ds(pl.multiple_of(spot, step), step), :] = (
                own_refs[block][group] if matrix else own_refs[group][start : start + step, :]
            )
    keep_ref[...] = jnp.zeros(keep_ref.shape, jnp.float32)
    send_ref[...] = jnp.zeros(send_ref.shape, jnp.float32)

    def body(weight_ref, first, slots):
        found = []
        for slot in slots:
            place = place_ref[matrix, first + slot]
            left = row_ref[:, lanes(place % width_blocks, size)]
            product = dot(left, weight_ref[slot], 1, 1 if transposed else 0)
            found.append((lanes(place // width_blocks, size), product))
        for spot, product in found:
            for group in range(mem_count):
                start = group * rows
                keep_ref[group, :, spot] += product[start : start + half]
                send_ref[group, :, spot] += product[start + half : start + rows]

    finish()
    over_owners(matrix, kept_ref, weight_refs, body)


def backward_kernel(
    matrix, transposed, width_blocks, mem_count, kept_ref, place_ref, own_ref, pair_ref, *refs
):
    tok_count = lax.axis_size(TOK)
    held_ref, out_refs, total_ref = refs[0], refs[1:-1], refs[-1]
    weight_refs = [held_ref.at[turn] for turn in range(tok_count)]
    size = held_ref.shape[-1]
    half = own_ref.shape[1]
    total_ref[...] = jnp.zeros(total_ref.shape, jnp.float32)

    def body(weight_ref, first, slots):
        found = []
        for slot in slots:
            place = place_ref[matrix, first + slot]
            spot = lanes(place // width_blocks, size)
            pieces = []
            for group in range(mem_count):
                pieces += [own_ref[group, :, spot], pair_ref[group, :, spot]]
            product = dot(
                jnp.concatenate(pieces, axis=0), weight_ref[slot], 1, 1 if transposed else 0
            )
            found.append((lanes(place % width_blocks, size), product))
        for spot, product in found:
            total_ref[:, spot] += product

    over_owners(matrix, kept_ref, weight_refs, body)
    for index, out_ref in enumerate(out_refs):
        chunk, group = index // mem_count, index % mem_count
        span = out_ref.shape[1]
        out_ref[...] = total_ref[
            group * 2 * half : (group + 1) * 2 * half, chunk * span : (chunk + 1) * span
        ]


def gradient_kernel(
    matrix, cell, width_blocks, mem_count, kept_ref, place_ref, row_ref, own_ref, pair_ref, *out_refs
):
    owned, size = out_refs[0].shape[:2]
    tok_count = lax.axis_size(TOK)
    tok = lax.axis_index(TOK)
    rows = row_ref.shape[0] // mem_count
    part = rows // tok_count

    def wide_rows(group, width):
        if cell == 0:
            return row_ref[group * rows : (group + 1) * rows, width]
        starts = [group * rows + (p ^ cell) * part for p in range(tok_count)]
        return jnp.concatenate([row_ref[start : start + part, width] for start in starts], axis=0)

    for side, out_ref in enumerate(out_refs):
        first, count = owner_count(kept_ref, matrix, tok ^ (2 * cell), tok ^ side, owned)

        def body(slots):
            for slot in slots:
                place = place_ref[matrix, first + slot]
                hidden = lanes(place // width_blocks, size)
                width = lanes(place % width_blocks, size)
                total = None
                for group in range(mem_count):
                    wide = wide_rows(group, width)
                    deep = jnp.concatenate(
                        [own_ref[group, :, hidden], pair_ref[group, :, hidden]], axis=0
                    )
                    left, right = (wide, deep) if matrix == 0 else (deep, wide)
                    term = dot(left, right, 0, 0).astype(jnp.bfloat16).astype(jnp.float32)
                    total = term if total is None else total + term
                out_ref[slot] = total

        over_slots(count, body)

        def clear(slot, carry):
            out_ref[slot] = jnp.zeros((size, size), jnp.float32)
            return carry

        lax.fori_loop(count, owned, clear, 0)


def update_kernel(matrix, cell, owned, kept_ref, own_ref, pair_ref, *refs):
    weight_ref, moment_ref, variance_ref = refs[:3]
    out_refs = refs[-3:]
    turn = pl.program_id(0)
    tok = lax.axis_index(TOK)
    run = weight_ref.shape[3]
    _, count = owner_count(kept_ref, matrix, tok ^ (2 * cell + turn), tok, owned)
    count = jnp.clip(count - pl.program_id(1) * run, 0, run)

    def update_from(grad_ref):
        def update(slot, carry):
            at = (0, 0, 0, slot)
            fresh = adam_step(weight_ref[at], moment_ref[at], variance_ref[at], grad_ref[slot])
            for out_ref, value in zip(out_refs, fresh):
                out_ref[at] = value
            return carry

        lax.fori_loop(0, count, update, 0)

    pl.when(turn == 0)(functools.partial(update_from, own_ref))
    pl.when(turn == 1)(functools.partial(update_from, pair_ref))

    def keep(slot, carry):
        at = (0, 0, 0, slot)
        for out_ref, value_ref in zip(out_refs, (weight_ref, moment_ref, variance_ref)):
            out_ref[at] = value_ref[at]
        return carry

    lax.fori_loop(count, run, keep, 0)


def join_kernel(pair_major, keep_ref, swap_ref, *out_refs):
    part = out_refs[0].shape[1]
    for index, out_ref in enumerate(out_refs):
        for inner in range(out_ref.shape[0]):
            group, shift = (inner, index) if pair_major else (index, inner)
            at = slice(shift * part, (shift + 1) * part)
            out_ref[inner] = keep_ref[group, at] + swap_ref[group, at]


def split_kernel(*refs):
    inner = refs[0].shape[0]
    for index, out_ref in enumerate(refs[-inner:]):
        total = refs[0][index]
        for ref in refs[1:-inner]:
            total = total + ref[index]
        out_ref[...] = total


def total_of(refs):
    total = refs[0][...]
    for ref in refs[1:]:
        total = total + ref[...]
    return total


def activate_kernel(split, *refs):
    *part_refs, hidden_ref, preact_ref = refs
    start = 0
    for side_refs in (part_refs[:split], part_refs[split:]):
        at = slice(start, start + side_refs[0].shape[1])
        start = at.stop
        preact = total_of(side_refs)
        preact_ref[:, at] = preact
        hidden_ref[:, at] = activate(preact).astype(jnp.bfloat16)


def slope_kernel(split, *refs):
    *part_refs, preact_ref, out_ref = refs
    start = 0
    for side_refs in (part_refs[:split], part_refs[split:]):
        at = slice(start, start + side_refs[0].shape[1])
        start = at.stop
        slope = gelu_slope(preact_ref[:, at])
        out_ref[:, at] = (total_of(side_refs) * slope).astype(jnp.bfloat16)


def narrow_kernel(block_ref, *out_refs):
    for turn, out_ref in enumerate(out_refs):

        @pl.when(pl.program_id(0) == turn)
        def _():
            out_ref[...] = block_ref[0, 0, 0].astype(jnp.bfloat16)


SCALARS = pl.BlockSpec(memory_space=pltpu.SMEM)
WHOLE = pl.BlockSpec(memory_space=pltpu.VMEM)
OUTSIDE = pl.BlockSpec(memory_space=pltpu.HBM)
ANYWHERE = pl.BlockSpec(memory_space=pl.ANY)


def call(kernel, outs, scalars, arrays, flops, outside=(), scratch=()):
    moved = sum(math_size(a) for a in (*arrays, *outs))
    needed = moved
    if outside:
        scratch = [pltpu.SemaphoreType.DMA((len(outside),))]
    else:
        needed += sum(math_size(x) for x in scratch)
    return pl.pallas_call(
        kernel,
        out_shape=outs,
        in_specs=[SCALARS] * len(scalars) + [WHOLE] * len(arrays) + [OUTSIDE] * len(outside),
        out_specs=[WHOLE] * len(outs),
        scratch_shapes=scratch,
        compiler_params=grant(needed),
        cost_estimate=pl.CostEstimate(flops=flops, bytes_accessed=moved, transcendentals=0),
    )(*scalars, *arrays, *outside)


def math_size(array):
    return math.prod(array.shape) * array.dtype.itemsize


def grant(needed):
    return pltpu.CompilerParams(vmem_limit_bytes=needed + VMEM_SPARE)


def on_device(inputs, cotangent, blocks, first_moment, second_moment, places, kept_counts):
    mem_count = lax.axis_size(MEM)
    tok_count = lax.axis_size(TOK)
    hid_count = lax.axis_size(HID)
    block_size = blocks.shape[-1]
    owned_slots = blocks.shape[3]
    local_slots = owned_slots * tok_count
    width_blocks = inputs.shape[1] // block_size
    hidden_span = FFW // hid_count
    rows = inputs.shape[0] * hid_count
    other = tok_count // 2
    half = rows // 2
    part = rows // tok_count
    chunks = CHUNKS
    kept = kept_counts[:, :, 0]
    place_ids = places[:, 0, 0]
    scalars = (kept, place_ids)
    f32, bf16 = jnp.float32, jnp.bfloat16

    def shift_hid(array, shift):
        return lax.ppermute(array, HID, [(i, (i + shift) % hid_count) for i in range(hid_count)])

    def shift_mem(array, shift):
        return lax.ppermute(array, MEM, [(i, (i + shift) % mem_count) for i in range(mem_count)])

    def flip_tok(array, bit):
        return lax.ppermute(array, TOK, [(i, i ^ bit) for i in range(tok_count)])

    def across(array, mem_shift, tok_shift):
        table = []
        for m in range(mem_count):
            for t in range(tok_count):
                to = ((m - mem_shift) % mem_count) * tok_count + (t ^ (2 * tok_shift))
                table.append((m * tok_count + t, to))
        return lax.ppermute(array, (MEM, TOK), table)

    def gather_rows(array):
        pieces = [array] + [shift_hid(array, k) for k in range(1, hid_count)]
        near = jnp.concatenate(pieces, axis=0)
        return [near] + [shift_mem(near, j) for j in range(1, mem_count)]

    def gather_small(array):
        found = [array] + [shift_mem(array, j) for j in range(1, mem_count)]
        own = jnp.stack(found)
        return [own] + [shift_hid(own, k) for k in range(1, hid_count)]

    def gather_weights(matrix):
        shape = (owned_slots, block_size, block_size)
        narrow = pl.pallas_call(
            narrow_kernel,
            grid=(tok_count,),
            out_shape=[jax.ShapeDtypeStruct(shape, bf16)] * tok_count,
            in_specs=[
                pl.BlockSpec(
                    (1, 1, 1) + blocks.shape[3:],
                    lambda i: (matrix, lax.axis_index(TOK) ^ i, 0, 0, 0, 0),
                )
            ],
            out_specs=[pl.BlockSpec(shape, lambda i: (0, 0, 0))] * tok_count,
            compiler_params=grant(owned_slots * block_size**2 * 4 * (2 + tok_count)),
        )(blocks)
        moved = [flip_tok(narrow[r], r) for r in range(1, tok_count)]
        return [narrow[0], *moved]

    def forward(matrix, transposed, row_groups, weights):
        kernel = functools.partial(
            forward_kernel, matrix, transposed, width_blocks, tok_count, hid_count, mem_count
        )
        width = row_groups[0].shape[-1]
        outs = [
            jax.ShapeDtypeStruct((mem_count * rows, width), bf16),
            jax.ShapeDtypeStruct((mem_count, half, hidden_span), f32),
            jax.ShapeDtypeStruct((mem_count, half, hidden_span), f32),
            jax.ShapeDtypeStruct((tok_count, owned_slots, block_size, block_size), bf16),
        ]
        flops = 2 * mem_count * rows * local_slots * block_size * block_size
        return call(kernel, outs, scalars, row_groups, flops, weights)

    mem_span = hidden_span // 2

    def side_columns(kernel, outs, arrays, side, steps=3):
        whole = hidden_span - mem_span if side else mem_span
        span = whole // steps

        def spec(shape, shift):
            lead = len(shape) - 1
            return pl.BlockSpec(tuple(shape[:-1]) + (span,), lambda i: (0,) * lead + (i + shift,))

        shift = side * mem_span // span
        needed = 2 * (sum(math_size(a) for a in outs) // steps)
        needed += 2 * (sum(math_size(a) // a.shape[-1] * span for a in arrays))
        return pl.pallas_call(
            kernel,
            grid=(steps,),
            out_shape=outs,
            in_specs=[spec(a.shape, shift) for a in arrays],
            out_specs=[spec(o.shape, 0) for o in outs],
            compiler_params=grant(needed),
            cost_estimate=pl.CostEstimate(
                flops=sum(math.prod(o.shape) for o in outs) * 2,
                bytes_accessed=needed * steps // 2,
                transcendentals=0,
            ),
        )(*arrays)

    def reduce_plane(keep, send):
        swap = flip_tok(send, 1)

        def array(side, *lead):
            return jax.ShapeDtypeStruct((*lead, hidden_span - mem_span if side else mem_span), f32)

        kernel = functools.partial(join_kernel, False)
        outs = [array(0, other, part)] * mem_count
        by_mem = side_columns(kernel, outs, [keep, swap], 0)
        kernel = functools.partial(join_kernel, True)
        outs = [array(1, mem_count, part)] * other
        by_pair = side_columns(kernel, outs, [keep, swap], 1)
        mem_terms = [by_mem[0]] + [shift_mem(by_mem[j], -j) for j in range(1, mem_count)]
        pair_terms = [by_pair[0]] + [flip_tok(by_pair[b], 2 * b) for b in range(1, other)]
        mine, *rest = call(split_kernel, [array(0, part)] * other, (), mem_terms, part)
        first = [mine] + [flip_tok(x, 2 * b) for b, x in enumerate(rest, 1)]
        mine, *rest = call(split_kernel, [array(1, part)] * mem_count, (), pair_terms, part)
        second = [mine] + [shift_mem(x, -j) for j, x in enumerate(rest, 1)]
        return first, second

    peers = [(j, b) for j in range(mem_count) for b in range(other)][1:]

    def gather_plane(piece):
        found = {(0, 0): piece}
        for j, b in peers:
            found[(-j) % mem_count, b] = across(piece, j, b)
        near = jnp.concatenate(
            [found[j, b] for j in range(mem_count) for b in range(other)], axis=0
        ).reshape(mem_count, half, hidden_span)
        return near, flip_tok(near, 1)

    def backward(matrix, transposed, near, far, weights):
        kernel = functools.partial(backward_kernel, matrix, transposed, width_blocks, mem_count)
        span = inputs.shape[1] // chunks
        outs = [jax.ShapeDtypeStruct((rows, span), f32)] * (mem_count * chunks)
        flops = 2 * mem_count * rows * local_slots * block_size * block_size
        scratch = [pltpu.VMEM((mem_count * rows, inputs.shape[1]), f32)]
        arrays = [near, far, weights]
        return call(kernel, outs, scalars, arrays, flops, (), scratch)

    turn = relative(tok_count)
    step = inputs.shape[0]

    def reduce_rows(found):
        results = []
        for chunk in range(chunks):
            groups = found[chunk * mem_count : (chunk + 1) * mem_count]
            total = groups[0]
            for j in range(1, mem_count):
                total = total + shift_mem(groups[j], -j)
            result = None
            for k in range(hid_count):
                start = k * step
                spot = ((start // part) ^ turn) * part + start % part
                piece = lax.dynamic_slice_in_dim(total, spot, step, 0)
                if k:
                    piece = shift_hid(piece, -k)
                result = piece if result is None else result + piece
            results.append(result.astype(bf16))
        return jnp.concatenate(results, axis=1)

    def gradient(matrix, cell, ids, row_values, near, far):
        kernel = functools.partial(gradient_kernel, matrix, cell, width_blocks, mem_count)
        outs = [jax.ShapeDtypeStruct((owned_slots, block_size, block_size), f32)] * 2
        flops = 2 * mem_count * rows * owned_slots * 2 * block_size * block_size
        keep, send = call(kernel, outs, (kept, ids), [row_values, near, far], flops)
        return keep, flip_tok(send, 1)

    def update(matrix, cell, grads, held):
        splits = 2 if owned_slots % 2 == 0 else 1
        run = owned_slots // splits
        state_spec = pl.BlockSpec(
            (1, 1, 1, run, block_size, block_size),
            lambda i, j: (matrix, lax.axis_index(TOK) ^ (2 * cell + i), 0, j, 0, 0),
        )
        own_spec = pl.BlockSpec(
            (run, block_size, block_size), lambda i, j: (jnp.where(i == 0, j, splits - 1), 0, 0)
        )
        pair_spec = pl.BlockSpec(
            (run, block_size, block_size), lambda i, j: (jnp.where(i == 0, 0, j), 0, 0)
        )
        state = (blocks, first_moment, second_moment)
        size = 2 * owned_slots * block_size * block_size
        return pl.pallas_call(
            functools.partial(update_kernel, matrix, cell, owned_slots),
            grid=(2, splits),
            out_shape=[jax.ShapeDtypeStruct(s.shape, f32) for s in state],
            in_specs=[SCALARS, own_spec, pair_spec] + [state_spec] * 3 + [ANYWHERE] * len(held),
            out_specs=[state_spec] * 3,
            input_output_aliases={6 + i: i for i in range(len(held))},
            compiler_params=grant(44 * 2**20),
            cost_estimate=pl.CostEstimate(
                flops=size * 12, bytes_accessed=size * 28, transcendentals=size
            ),
        )(kept, *grads, *state, *held)

    far_place_ids = flip_tok(place_ids, 2)
    input_groups = gather_rows(inputs)
    weights_first = gather_weights(0)
    cotangent_groups = gather_small(cotangent)
    weights_second = gather_weights(1)
    token_rows, *pre_part, weights_first = forward(0, False, input_groups, weights_first)
    pre_terms = reduce_plane(*pre_part)
    grad_rows, *back_part, weights_second = forward(1, True, cotangent_groups, weights_second)
    back_terms = reduce_plane(*back_part)
    piece = (part, hidden_span)
    outs = [jax.ShapeDtypeStruct(piece, bf16), jax.ShapeDtypeStruct(piece, f32)]
    kernel = functools.partial(activate_kernel, len(pre_terms[0]))
    hidden_piece, preact = call(kernel, outs, (), [*pre_terms[0], *pre_terms[1]], part)
    hidden = gather_plane(hidden_piece)
    kernel = functools.partial(slope_kernel, len(back_terms[0]))
    arrays = [*back_terms[0], *back_terms[1], preact]
    (grad_piece,) = call(kernel, outs[:1], (), arrays, part)
    pre_grad = gather_plane(grad_piece)
    layer_out = reduce_rows(backward(1, False, *hidden, weights_second))
    grad_in = reduce_rows(backward(0, True, *pre_grad, weights_first))
    far_grad_rows = flip_tok(grad_rows, 2)
    far_token_rows = flip_tok(token_rows, 2)
    grads = gradient(1, 0, place_ids, grad_rows, *hidden)
    state = update(1, 0, grads, ())
    grads = gradient(0, 0, place_ids, token_rows, *pre_grad)
    state = update(0, 0, grads, state)
    grads = gradient(1, 1, far_place_ids, far_grad_rows, *hidden)
    state = update(1, 1, grads, state)
    grads = gradient(0, 1, far_place_ids, far_token_rows, *pre_grad)
    return (layer_out, grad_in, *update(0, 1, grads, state))


def solution(mesh):
    return jax.shard_map(
        on_device,
        mesh=mesh,
        in_specs=(
            P((MEM, HID), TOK),
            P((MEM, HID), TOK),
            P(None, None, HID, (MEM, TOK), None, None),
            P(None, None, HID, (MEM, TOK), None, None),
            P(None, None, HID, (MEM, TOK), None, None),
            P(None, TOK, HID, None),
            P(None, None, HID),
        ),
        out_specs=(
            P((MEM, HID), TOK),
            P((MEM, HID), TOK),
            P(None, None, HID, (MEM, TOK), None, None),
            P(None, None, HID, (MEM, TOK), None, None),
            P(None, None, HID, (MEM, TOK), None, None),
        ),
        check_vma=False,
    )
```

```python
import functools
import math

import jax
import jax.numpy as jnp
from jax import lax
from jax.experimental import pallas as pl
from jax.experimental.pallas import tpu as pltpu
from jax.sharding import PartitionSpec as P


FFW = 24576
STEP = 10


GELU_ROOT = 0.7978845608028654
GELU_CUBIC = 0.044715
BETA_FIRST = 0.9
BETA_SECOND = 0.95
LEARN_RATE = 0.001
WEIGHT_DECAY = 0.1
ADAM_EPSILON = 1e-08
VMEM_SPARE = 3 * 2**19
UNROLL = 4
CHUNKS = 2
MEM, HID, TOK = "mem", "hid", "tok"


def activate(values):
    tangent = jnp.tanh(GELU_ROOT * (values + GELU_CUBIC * values * values * values))
    return 0.5 * values * (1.0 + tangent)


def gelu_slope(values):
    tangent = jnp.tanh(GELU_ROOT * (values + GELU_CUBIC * values * values * values))
    return 0.5 * (1.0 + tangent) + 0.5 * values * (1.0 - tangent * tangent) * GELU_ROOT * (
        1.0 + 3.0 * GELU_CUBIC * values * values
    )


def adam_step(weight, moment, variance, gradient):
    new_moment = BETA_FIRST * moment + (1.0 - BETA_FIRST) * gradient
    new_variance = BETA_SECOND * variance + (1.0 - BETA_SECOND) * (gradient * gradient)
    scaled = new_variance * (1.0 / (1.0 - BETA_SECOND**STEP))
    root = scaled * lax.rsqrt(scaled)
    step = new_moment * (LEARN_RATE / (1.0 - BETA_FIRST**STEP)) / (root + ADAM_EPSILON)
    new_weight = weight * (1.0 - LEARN_RATE * WEIGHT_DECAY) - step
    return new_weight, new_moment, new_variance


def dot(left, right, left_dim, right_dim):
    return lax.dot_general(
        left, right, (((left_dim,), (right_dim,)), ((), ())), preferred_element_type=jnp.float32
    )


def lanes(index, size):
    return pl.ds(pl.multiple_of(index * size, size), size)


def owner_count(kept_ref, matrix, cell, owner, owned):
    first = (lax.axis_index(MEM) * lax.axis_size(TOK) + owner) * owned
    return first, jnp.clip(kept_ref[matrix, cell] - first, 0, owned)


def over_slots(count, body):
    groups = count // UNROLL

    def run(group, carry):
        body([group * UNROLL + lane for lane in range(UNROLL)])
        return carry

    lax.fori_loop(0, groups, run, 0)

    def single(slot, carry):
        body([slot])
        return carry

    lax.fori_loop(groups * UNROLL, count, single, 0)


def start_weights(sources, held_ref, sems):
    copies = [
        pltpu.make_async_copy(source, held_ref.at[index], sems.at[index])
        for index, source in enumerate(sources)
    ]
    for copy in copies:
        copy.start()

    def finish():
        for copy in copies:
            copy.wait()

    return [held_ref.at[index] for index in range(len(sources))], finish


def over_owners(matrix, kept_ref, weight_refs, body):
    tok = lax.axis_index(TOK)
    for turn, weight_ref in enumerate(weight_refs):
        owned = weight_ref.shape[0]
        first, count = owner_count(kept_ref, matrix, tok, tok ^ turn, owned)
        over_slots(count, functools.partial(body, weight_ref, first))


def relative(tok_count):
    tok = lax.axis_index(TOK)
    return (tok % 2) * (tok_count // 2) + tok // 2


def forward_kernel(
    matrix, transposed, width_blocks, tok_count, hid_count, mem_count, kept_ref, place_ref, *refs
):
    sources = hid_count if matrix else mem_count
    own_refs = refs[:sources]
    row_ref, keep_ref, send_ref, held_ref, sems = refs[sources + tok_count :]
    weight_refs, finish = start_weights(refs[sources : sources + tok_count], held_ref, sems)
    half = keep_ref.shape[1]
    _, size = weight_refs[0].shape[:2]
    rows = row_ref.shape[0] // mem_count
    step = rows // hid_count
    part = rows // tok_count
    turn = relative(tok_count)
    for group in range(mem_count):
        for block in range(hid_count):
            start = block * step
            spot = ((start // part) ^ turn) * part + start % part + group * rows
            row_ref[pl.ds(pl.multiple_of(spot, step), step), :] = (
                own_refs[block][group] if matrix else own_refs[group][start : start + step, :]
            )
    keep_ref[...] = jnp.zeros(keep_ref.shape, jnp.float32)
    send_ref[...] = jnp.zeros(send_ref.shape, jnp.float32)

    def body(weight_ref, first, slots):
        found = []
        for slot in slots:
            place = place_ref[matrix, first + slot]
            left = row_ref[:, lanes(place % width_blocks, size)]
            product = dot(left, weight_ref[slot], 1, 1 if transposed else 0)
            found.append((lanes(place // width_blocks, size), product))
        for spot, product in found:
            for group in range(mem_count):
                start = group * rows
                keep_ref[group, :, spot] += product[start : start + half]
                send_ref[group, :, spot] += product[start + half : start + rows]

    finish()
    over_owners(matrix, kept_ref, weight_refs, body)


def backward_kernel(
    matrix, transposed, width_blocks, mem_count, kept_ref, place_ref, own_ref, pair_ref, *refs
):
    tok_count = lax.axis_size(TOK)
    held_ref, out_refs, total_ref = refs[0], refs[1:-1], refs[-1]
    weight_refs = [held_ref.at[turn] for turn in range(tok_count)]
    size = held_ref.shape[-1]
    half = own_ref.shape[1]
    total_ref[...] = jnp.zeros(total_ref.shape, jnp.float32)

    def body(weight_ref, first, slots):
        found = []
        for slot in slots:
            place = place_ref[matrix, first + slot]
            spot = lanes(place // width_blocks, size)
            pieces = []
            for group in range(mem_count):
                pieces += [own_ref[group, :, spot], pair_ref[group, :, spot]]
            product = dot(
                jnp.concatenate(pieces, axis=0), weight_ref[slot], 1, 1 if transposed else 0
            )
            found.append((lanes(place % width_blocks, size), product))
        for spot, product in found:
            total_ref[:, spot] += product

    over_owners(matrix, kept_ref, weight_refs, body)
    for index, out_ref in enumerate(out_refs):
        chunk, group = index // mem_count, index % mem_count
        span = out_ref.shape[1]
        out_ref[...] = total_ref[
            group * 2 * half : (group + 1) * 2 * half, chunk * span : (chunk + 1) * span
        ]


def gradient_kernel(
    matrix, cell, width_blocks, mem_count, kept_ref, place_ref, row_ref, own_ref, pair_ref, *out_refs
):
    owned, size = out_refs[0].shape[:2]
    tok_count = lax.axis_size(TOK)
    tok = lax.axis_index(TOK)
    rows = row_ref.shape[0] // mem_count
    part = rows // tok_count

    def wide_rows(group, width):
        if cell == 0:
            return row_ref[group * rows : (group + 1) * rows, width]
        starts = [group * rows + (p ^ cell) * part for p in range(tok_count)]
        return jnp.concatenate([row_ref[start : start + part, width] for start in starts], axis=0)

    for side, out_ref in enumerate(out_refs):
        first, count = owner_count(kept_ref, matrix, tok ^ (2 * cell), tok ^ side, owned)

        def body(slots):
            for slot in slots:
                place = place_ref[matrix, first + slot]
                hidden = lanes(place // width_blocks, size)
                width = lanes(place % width_blocks, size)
                total = None
                for group in range(mem_count):
                    wide = wide_rows(group, width)
                    deep = jnp.concatenate(
                        [own_ref[group, :, hidden], pair_ref[group, :, hidden]], axis=0
                    )
                    left, right = (wide, deep) if matrix == 0 else (deep, wide)
                    term = dot(left, right, 0, 0).astype(jnp.bfloat16).astype(jnp.float32)
                    total = term if total is None else total + term
                out_ref[slot] = total

        over_slots(count, body)

        def clear(slot, carry):
            out_ref[slot] = jnp.zeros((size, size), jnp.float32)
            return carry

        lax.fori_loop(count, owned, clear, 0)


def update_kernel(matrix, cell, owned, kept_ref, own_ref, pair_ref, *refs):
    weight_ref, moment_ref, variance_ref = refs[:3]
    out_refs = refs[-3:]
    turn = pl.program_id(0)
    tok = lax.axis_index(TOK)
    run = weight_ref.shape[3]
    _, count = owner_count(kept_ref, matrix, tok ^ (2 * cell + turn), tok, owned)
    count = jnp.clip(count - pl.program_id(1) * run, 0, run)

    def update_from(grad_ref):
        def update(slot, carry):
            at = (0, 0, 0, slot)
            fresh = adam_step(weight_ref[at], moment_ref[at], variance_ref[at], grad_ref[slot])
            for out_ref, value in zip(out_refs, fresh):
                out_ref[at] = value
            return carry

        lax.fori_loop(0, count, update, 0)

    pl.when(turn == 0)(functools.partial(update_from, own_ref))
    pl.when(turn == 1)(functools.partial(update_from, pair_ref))

    def keep(slot, carry):
        at = (0, 0, 0, slot)
        for out_ref, value_ref in zip(out_refs, (weight_ref, moment_ref, variance_ref)):
            out_ref[at] = value_ref[at]
        return carry

    lax.fori_loop(count, run, keep, 0)


def join_kernel(pair_major, keep_ref, swap_ref, *out_refs):
    part = out_refs[0].shape[1]
    for index, out_ref in enumerate(out_refs):
        for inner in range(out_ref.shape[0]):
            group, shift = (inner, index) if pair_major else (index, inner)
            at = slice(shift * part, (shift + 1) * part)
            out_ref[inner] = keep_ref[group, at] + swap_ref[group, at]


def split_kernel(*refs):
    inner = refs[0].shape[0]
    for index, out_ref in enumerate(refs[-inner:]):
        total = refs[0][index]
        for ref in refs[1:-inner]:
            total = total + ref[index]
        out_ref[...] = total


def total_of(refs):
    total = refs[0][...]
    for ref in refs[1:]:
        total = total + ref[...]
    return total


def activate_kernel(split, *refs):
    *part_refs, hidden_ref, preact_ref = refs
    start = 0
    for side_refs in (part_refs[:split], part_refs[split:]):
        at = slice(start, start + side_refs[0].shape[1])
        start = at.stop
        preact = total_of(side_refs)
        preact_ref[:, at] = preact
        hidden_ref[:, at] = activate(preact).astype(jnp.bfloat16)


def slope_kernel(split, *refs):
    *part_refs, preact_ref, out_ref = refs
    start = 0
    for side_refs in (part_refs[:split], part_refs[split:]):
        at = slice(start, start + side_refs[0].shape[1])
        start = at.stop
        slope = gelu_slope(preact_ref[:, at])
        out_ref[:, at] = (total_of(side_refs) * slope).astype(jnp.bfloat16)


def narrow_kernel(block_ref, *out_refs):
    for turn, out_ref in enumerate(out_refs):

        @pl.when(pl.program_id(0) == turn)
        def _():
            out_ref[...] = block_ref[0, 0, 0].astype(jnp.bfloat16)


SCALARS = pl.BlockSpec(memory_space=pltpu.SMEM)
WHOLE = pl.BlockSpec(memory_space=pltpu.VMEM)
OUTSIDE = pl.BlockSpec(memory_space=pltpu.HBM)
ANYWHERE = pl.BlockSpec(memory_space=pl.ANY)


def call(kernel, outs, scalars, arrays, flops, outside=(), scratch=()):
    moved = sum(math_size(a) for a in (*arrays, *outs))
    needed = moved
    if outside:
        scratch = [pltpu.SemaphoreType.DMA((len(outside),))]
    else:
        needed += sum(math_size(x) for x in scratch)
    return pl.pallas_call(
        kernel,
        out_shape=outs,
        in_specs=[SCALARS] * len(scalars) + [WHOLE] * len(arrays) + [OUTSIDE] * len(outside),
        out_specs=[WHOLE] * len(outs),
        scratch_shapes=scratch,
        compiler_params=grant(needed),
        cost_estimate=pl.CostEstimate(flops=flops, bytes_accessed=moved, transcendentals=0),
    )(*scalars, *arrays, *outside)


def math_size(array):
    return math.prod(array.shape) * array.dtype.itemsize


def grant(needed):
    return pltpu.CompilerParams(vmem_limit_bytes=needed + VMEM_SPARE)


def on_device(inputs, cotangent, blocks, first_moment, second_moment, places, kept_counts):
    mem_count = lax.axis_size(MEM)
    tok_count = lax.axis_size(TOK)
    hid_count = lax.axis_size(HID)
    block_size = blocks.shape[-1]
    owned_slots = blocks.shape[3]
    local_slots = owned_slots * tok_count
    width_blocks = inputs.shape[1] // block_size
    hidden_span = FFW // hid_count
    rows = inputs.shape[0] * hid_count
    other = tok_count // 2
    half = rows // 2
    part = rows // tok_count
    chunks = CHUNKS
    kept = kept_counts[:, :, 0]
    place_ids = places[:, 0, 0]
    scalars = (kept, place_ids)
    f32, bf16 = jnp.float32, jnp.bfloat16

    def shift_hid(array, shift):
        return lax.ppermute(array, HID, [(i, (i + shift) % hid_count) for i in range(hid_count)])

    def shift_mem(array, shift):
        return lax.ppermute(array, MEM, [(i, (i + shift) % mem_count) for i in range(mem_count)])

    def flip_tok(array, bit):
        return lax.ppermute(array, TOK, [(i, i ^ bit) for i in range(tok_count)])

    def across(array, mem_shift, tok_shift):
        table = []
        for m in range(mem_count):
            for t in range(tok_count):
                to = ((m - mem_shift) % mem_count) * tok_count + (t ^ (2 * tok_shift))
                table.append((m * tok_count + t, to))
        return lax.ppermute(array, (MEM, TOK), table)

    def gather_rows(array):
        pieces = [array] + [shift_hid(array, k) for k in range(1, hid_count)]
        near = jnp.concatenate(pieces, axis=0)
        return [near] + [shift_mem(near, j) for j in range(1, mem_count)]

    def gather_small(array):
        found = [array] + [shift_mem(array, j) for j in range(1, mem_count)]
        own = jnp.stack(found)
        return [own] + [shift_hid(own, k) for k in range(1, hid_count)]

    def gather_weights(matrix):
        shape = (owned_slots, block_size, block_size)
        narrow = pl.pallas_call(
            narrow_kernel,
            grid=(tok_count,),
            out_shape=[jax.ShapeDtypeStruct(shape, bf16)] * tok_count,
            in_specs=[
                pl.BlockSpec(
                    (1, 1, 1) + blocks.shape[3:],
                    lambda i: (matrix, lax.axis_index(TOK) ^ i, 0, 0, 0, 0),
                )
            ],
            out_specs=[pl.BlockSpec(shape, lambda i: (0, 0, 0))] * tok_count,
            compiler_params=grant(owned_slots * block_size**2 * 4 * (2 + tok_count)),
        )(blocks)
        moved = [flip_tok(narrow[r], r) for r in range(1, tok_count)]
        return [narrow[0], *moved]

    def forward(matrix, transposed, row_groups, weights):
        kernel = functools.partial(
            forward_kernel, matrix, transposed, width_blocks, tok_count, hid_count, mem_count
        )
        width = row_groups[0].shape[-1]
        outs = [
            jax.ShapeDtypeStruct((mem_count * rows, width), bf16),
            jax.ShapeDtypeStruct((mem_count, half, hidden_span), f32),
            jax.ShapeDtypeStruct((mem_count, half, hidden_span), f32),
            jax.ShapeDtypeStruct((tok_count, owned_slots, block_size, block_size), bf16),
        ]
        flops = 2 * mem_count * rows * local_slots * block_size * block_size
        return call(kernel, outs, scalars, row_groups, flops, weights)

    mem_span = hidden_span * 5 // 8

    def side_columns(kernel, outs, arrays, side, steps=3):
        whole = hidden_span - mem_span if side else mem_span
        span = whole // steps

        def spec(shape, shift):
            lead = len(shape) - 1
            return pl.BlockSpec(tuple(shape[:-1]) + (span,), lambda i: (0,) * lead + (i + shift,))

        shift = side * mem_span // span
        needed = 2 * (sum(math_size(a) for a in outs) // steps)
        needed += 2 * (sum(math_size(a) // a.shape[-1] * span for a in arrays))
        return pl.pallas_call(
            kernel,
            grid=(steps,),
            out_shape=outs,
            in_specs=[spec(a.shape, shift) for a in arrays],
            out_specs=[spec(o.shape, 0) for o in outs],
            compiler_params=grant(needed),
            cost_estimate=pl.CostEstimate(
                flops=sum(math.prod(o.shape) for o in outs) * 2,
                bytes_accessed=needed * steps // 2,
                transcendentals=0,
            ),
        )(*arrays)

    def reduce_plane(keep, send):
        swap = flip_tok(send, 1)

        def array(side, *lead):
            return jax.ShapeDtypeStruct((*lead, hidden_span - mem_span if side else mem_span), f32)

        kernel = functools.partial(join_kernel, False)
        outs = [array(0, other, part)] * mem_count
        by_mem = side_columns(kernel, outs, [keep, swap], 0)
        kernel = functools.partial(join_kernel, True)
        outs = [array(1, mem_count, part)] * other
        by_pair = side_columns(kernel, outs, [keep, swap], 1)
        mem_terms = [by_mem[0]] + [shift_mem(by_mem[j], -j) for j in range(1, mem_count)]
        pair_terms = [by_pair[0]] + [flip_tok(by_pair[b], 2 * b) for b in range(1, other)]
        mine, *rest = call(split_kernel, [array(0, part)] * other, (), mem_terms, part)
        first = [mine] + [flip_tok(x, 2 * b) for b, x in enumerate(rest, 1)]
        mine, *rest = call(split_kernel, [array(1, part)] * mem_count, (), pair_terms, part)
        second = [mine] + [shift_mem(x, -j) for j, x in enumerate(rest, 1)]
        return first, second

    peers = [(j, b) for j in range(mem_count) for b in range(other)][1:]

    def gather_plane(piece):
        found = {(0, 0): piece}
        for j, b in peers:
            found[(-j) % mem_count, b] = across(piece, j, b)
        near = jnp.concatenate(
            [found[j, b] for j in range(mem_count) for b in range(other)], axis=0
        ).reshape(mem_count, half, hidden_span)
        return near, flip_tok(near, 1)

    def backward(matrix, transposed, near, far, weights):
        kernel = functools.partial(backward_kernel, matrix, transposed, width_blocks, mem_count)
        span = inputs.shape[1] // chunks
        outs = [jax.ShapeDtypeStruct((rows, span), f32)] * (mem_count * chunks)
        flops = 2 * mem_count * rows * local_slots * block_size * block_size
        scratch = [pltpu.VMEM((mem_count * rows, inputs.shape[1]), f32)]
        arrays = [near, far, weights]
        return call(kernel, outs, scalars, arrays, flops, (), scratch)

    turn = relative(tok_count)
    step = inputs.shape[0]

    def spot_of(k):
        start = k * step
        return ((start // part) ^ turn) * part + start % part

    def mem_first(groups):
        total = groups[0]
        for j in range(1, mem_count):
            total = total + shift_mem(groups[j], -j)
        result = lax.dynamic_slice_in_dim(total, spot_of(0), step, 0)
        for k in range(1, hid_count):
            piece = lax.dynamic_slice_in_dim(total, spot_of(k), step, 0)
            result = result + shift_hid(piece, -k)
        return result.astype(bf16)

    def hid_first(groups):
        def rows_of(k):
            return jnp.stack([lax.dynamic_slice_in_dim(g, spot_of(k), step, 0) for g in groups])

        total = rows_of(0)
        for k in range(1, hid_count):
            total = total + shift_hid(rows_of(k), -k)
        result = total[0]
        for j in range(1, mem_count):
            result = result + shift_mem(total[j], -j)
        return result.astype(bf16)

    def reduce_rows(found, hid_chunks=0):
        results = []
        for chunk in range(chunks):
            groups = found[chunk * mem_count : (chunk + 1) * mem_count]
            if chunk < chunks - hid_chunks:
                results.append(mem_first(groups))
            else:
                results.append(hid_first(groups))
        return jnp.concatenate(results, axis=1)

    def gradient(matrix, cell, ids, row_values, near, far):
        kernel = functools.partial(gradient_kernel, matrix, cell, width_blocks, mem_count)
        outs = [jax.ShapeDtypeStruct((owned_slots, block_size, block_size), f32)] * 2
        flops = 2 * mem_count * rows * owned_slots * 2 * block_size * block_size
        keep, send = call(kernel, outs, (kept, ids), [row_values, near, far], flops)
        return keep, flip_tok(send, 1)

    def update(matrix, cell, grads, held):
        splits = 2 if owned_slots % 2 == 0 else 1
        run = owned_slots // splits
        state_spec = pl.BlockSpec(
            (1, 1, 1, run, block_size, block_size),
            lambda i, j: (matrix, lax.axis_index(TOK) ^ (2 * cell + i), 0, j, 0, 0),
        )
        own_spec = pl.BlockSpec(
            (run, block_size, block_size), lambda i, j: (jnp.where(i == 0, j, splits - 1), 0, 0)
        )
        pair_spec = pl.BlockSpec(
            (run, block_size, block_size), lambda i, j: (jnp.where(i == 0, 0, j), 0, 0)
        )
        state = (blocks, first_moment, second_moment)
        size = 2 * owned_slots * block_size * block_size
        return pl.pallas_call(
            functools.partial(update_kernel, matrix, cell, owned_slots),
            grid=(2, splits),
            out_shape=[jax.ShapeDtypeStruct(s.shape, f32) for s in state],
            in_specs=[SCALARS, own_spec, pair_spec] + [state_spec] * 3 + [ANYWHERE] * len(held),
            out_specs=[state_spec] * 3,
            input_output_aliases={6 + i: i for i in range(len(held))},
            compiler_params=grant(44 * 2**20),
            cost_estimate=pl.CostEstimate(
                flops=size * 12, bytes_accessed=size * 28, transcendentals=size
            ),
        )(kept, *grads, *state, *held)

    far_place_ids = flip_tok(place_ids, 2)
    input_groups = gather_rows(inputs)
    weights_first = gather_weights(0)
    cotangent_groups = gather_small(cotangent)
    weights_second = gather_weights(1)
    token_rows, *pre_part, weights_first = forward(0, False, input_groups, weights_first)
    pre_terms = reduce_plane(*pre_part)
    grad_rows, *back_part, weights_second = forward(1, True, cotangent_groups, weights_second)
    back_terms = reduce_plane(*back_part)
    piece = (part, hidden_span)
    outs = [jax.ShapeDtypeStruct(piece, bf16), jax.ShapeDtypeStruct(piece, f32)]
    kernel = functools.partial(activate_kernel, len(pre_terms[0]))
    hidden_piece, preact = call(kernel, outs, (), [*pre_terms[0], *pre_terms[1]], part)
    hidden = gather_plane(hidden_piece)
    kernel = functools.partial(slope_kernel, len(back_terms[0]))
    arrays = [*back_terms[0], *back_terms[1], preact]
    (grad_piece,) = call(kernel, outs[:1], (), arrays, part)
    pre_grad = gather_plane(grad_piece)
    layer_out = reduce_rows(backward(1, False, *hidden, weights_second), 1)
    grad_in = reduce_rows(backward(0, True, *pre_grad, weights_first))
    far_grad_rows = flip_tok(grad_rows, 2)
    far_token_rows = flip_tok(token_rows, 2)
    grads = gradient(1, 0, place_ids, grad_rows, *hidden)
    state = update(1, 0, grads, ())
    grads = gradient(0, 0, place_ids, token_rows, *pre_grad)
    state = update(0, 0, grads, state)
    grads = gradient(1, 1, far_place_ids, far_grad_rows, *hidden)
    state = update(1, 1, grads, state)
    grads = gradient(0, 1, far_place_ids, far_token_rows, *pre_grad)
    return (layer_out, grad_in, *update(0, 1, grads, state))


def solution(mesh):
    return jax.shard_map(
        on_device,
        mesh=mesh,
        in_specs=(
            P((MEM, HID), TOK),
            P((MEM, HID), TOK),
            P(None, None, HID, (MEM, TOK), None, None),
            P(None, None, HID, (MEM, TOK), None, None),
            P(None, None, HID, (MEM, TOK), None, None),
            P(None, TOK, HID, None),
            P(None, None, HID),
        ),
        out_specs=(
            P((MEM, HID), TOK),
            P((MEM, HID), TOK),
            P(None, None, HID, (MEM, TOK), None, None),
            P(None, None, HID, (MEM, TOK), None, None),
            P(None, None, HID, (MEM, TOK), None, None),
        ),
        check_vma=False,
    )
```

```python
import functools
import math

import jax
import jax.numpy as jnp
from jax import lax
from jax.experimental import pallas as pl
from jax.experimental.pallas import tpu as pltpu
from jax.sharding import PartitionSpec as P


FFW = 24576
STEP = 10


GELU_ROOT = 0.7978845608028654
GELU_CUBIC = 0.044715
BETA_FIRST = 0.9
BETA_SECOND = 0.95
LEARN_RATE = 0.001
WEIGHT_DECAY = 0.1
ADAM_EPSILON = 1e-08
VMEM_SPARE = 3 * 2**19
UNROLL = 6
CHUNKS = 2
MEM, HID, TOK = "mem", "hid", "tok"


def activate(values):
    tangent = jnp.tanh(GELU_ROOT * (values + GELU_CUBIC * values * values * values))
    return 0.5 * values * (1.0 + tangent)


def gelu_slope(values):
    tangent = jnp.tanh(GELU_ROOT * (values + GELU_CUBIC * values * values * values))
    return 0.5 * (1.0 + tangent) + 0.5 * values * (1.0 - tangent * tangent) * GELU_ROOT * (
        1.0 + 3.0 * GELU_CUBIC * values * values
    )


def adam_step(weight, moment, variance, gradient):
    new_moment = BETA_FIRST * moment + (1.0 - BETA_FIRST) * gradient
    new_variance = BETA_SECOND * variance + (1.0 - BETA_SECOND) * (gradient * gradient)
    scaled = new_variance * (1.0 / (1.0 - BETA_SECOND**STEP))
    root = scaled * lax.rsqrt(scaled)
    step = new_moment * (LEARN_RATE / (1.0 - BETA_FIRST**STEP)) / (root + ADAM_EPSILON)
    new_weight = weight * (1.0 - LEARN_RATE * WEIGHT_DECAY) - step
    return new_weight, new_moment, new_variance


def dot(left, right, left_dim, right_dim):
    return lax.dot_general(
        left, right, (((left_dim,), (right_dim,)), ((), ())), preferred_element_type=jnp.float32
    )


def lanes(index, size):
    return pl.ds(pl.multiple_of(index * size, size), size)


def owner_count(kept_ref, matrix, cell, owner, owned):
    first = (lax.axis_index(MEM) * lax.axis_size(TOK) + owner) * owned
    return first, jnp.clip(kept_ref[matrix, cell] - first, 0, owned)


def over_slots(count, body):
    groups = count // UNROLL

    def run(group, carry):
        body([group * UNROLL + lane for lane in range(UNROLL)])
        return carry

    lax.fori_loop(0, groups, run, 0)

    def single(slot, carry):
        body([slot])
        return carry

    lax.fori_loop(groups * UNROLL, count, single, 0)


def start_weights(sources, held_ref, sems):
    copies = [
        pltpu.make_async_copy(source, held_ref.at[index], sems.at[index])
        for index, source in enumerate(sources)
    ]
    for copy in copies:
        copy.start()

    def finish():
        for copy in copies:
            copy.wait()

    return [held_ref.at[index] for index in range(len(sources))], finish


def over_owners(matrix, kept_ref, weight_refs, body):
    tok = lax.axis_index(TOK)
    for turn, weight_ref in enumerate(weight_refs):
        owned = weight_ref.shape[0]
        first, count = owner_count(kept_ref, matrix, tok, tok ^ turn, owned)
        over_slots(count, functools.partial(body, weight_ref, first))


def relative(tok_count):
    tok = lax.axis_index(TOK)
    return (tok % 2) * (tok_count // 2) + tok // 2


def forward_kernel(
    matrix, transposed, width_blocks, tok_count, hid_count, mem_count, kept_ref, place_ref, *refs
):
    sources = hid_count if matrix else mem_count
    own_refs = refs[:sources]
    row_ref, keep_ref, send_ref, held_ref, sems = refs[sources + tok_count :]
    weight_refs, finish = start_weights(refs[sources : sources + tok_count], held_ref, sems)
    half = keep_ref.shape[1]
    _, size = weight_refs[0].shape[:2]
    rows = row_ref.shape[0] // mem_count
    step = rows // hid_count
    part = rows // tok_count
    turn = relative(tok_count)
    for group in range(mem_count):
        for block in range(hid_count):
            start = block * step
            spot = ((start // part) ^ turn) * part + start % part + group * rows
            row_ref[pl.ds(pl.multiple_of(spot, step), step), :] = (
                own_refs[block][group] if matrix else own_refs[group][start : start + step, :]
            )
    keep_ref[...] = jnp.zeros(keep_ref.shape, jnp.float32)
    send_ref[...] = jnp.zeros(send_ref.shape, jnp.float32)

    def body(weight_ref, first, slots):
        found = []
        for slot in slots:
            place = place_ref[matrix, first + slot]
            left = row_ref[:, lanes(place % width_blocks, size)]
            product = dot(left, weight_ref[slot], 1, 1 if transposed else 0)
            found.append((lanes(place // width_blocks, size), product))
        for spot, product in found:
            for group in range(mem_count):
                start = group * rows
                keep_ref[group, :, spot] += product[start : start + half]
                send_ref[group, :, spot] += product[start + half : start + rows]

    finish()
    over_owners(matrix, kept_ref, weight_refs, body)


def backward_kernel(
    matrix, transposed, width_blocks, mem_count, kept_ref, place_ref, own_ref, pair_ref, *refs
):
    tok_count = lax.axis_size(TOK)
    held_ref, out_refs, total_ref = refs[0], refs[1:-1], refs[-1]
    weight_refs = [held_ref.at[turn] for turn in range(tok_count)]
    size = held_ref.shape[-1]
    half = own_ref.shape[1]
    total_ref[...] = jnp.zeros(total_ref.shape, jnp.float32)

    def body(weight_ref, first, slots):
        found = []
        for slot in slots:
            place = place_ref[matrix, first + slot]
            spot = lanes(place // width_blocks, size)
            pieces = []
            for group in range(mem_count):
                pieces += [own_ref[group, :, spot], pair_ref[group, :, spot]]
            product = dot(
                jnp.concatenate(pieces, axis=0), weight_ref[slot], 1, 1 if transposed else 0
            )
            found.append((lanes(place % width_blocks, size), product))
        for spot, product in found:
            total_ref[:, spot] += product

    over_owners(matrix, kept_ref, weight_refs, body)
    for index, out_ref in enumerate(out_refs):
        chunk, group = index // mem_count, index % mem_count
        span = out_ref.shape[1]
        out_ref[...] = total_ref[
            group * 2 * half : (group + 1) * 2 * half, chunk * span : (chunk + 1) * span
        ]


def gradient_kernel(
    matrix, cell, width_blocks, mem_count, kept_ref, place_ref, row_ref, own_ref, pair_ref, *out_refs
):
    owned, size = out_refs[0].shape[:2]
    tok_count = lax.axis_size(TOK)
    tok = lax.axis_index(TOK)
    rows = row_ref.shape[0] // mem_count
    part = rows // tok_count

    def wide_rows(group, width):
        if cell == 0:
            return row_ref[group * rows : (group + 1) * rows, width]
        starts = [group * rows + (p ^ cell) * part for p in range(tok_count)]
        return jnp.concatenate([row_ref[start : start + part, width] for start in starts], axis=0)

    for side, out_ref in enumerate(out_refs):
        first, count = owner_count(kept_ref, matrix, tok ^ (2 * cell), tok ^ side, owned)

        def body(slots):
            for slot in slots:
                place = place_ref[matrix, first + slot]
                hidden = lanes(place // width_blocks, size)
                width = lanes(place % width_blocks, size)
                total = None
                for group in range(mem_count):
                    wide = wide_rows(group, width)
                    deep = jnp.concatenate(
                        [own_ref[group, :, hidden], pair_ref[group, :, hidden]], axis=0
                    )
                    left, right = (wide, deep) if matrix == 0 else (deep, wide)
                    term = dot(left, right, 0, 0).astype(jnp.bfloat16).astype(jnp.float32)
                    total = term if total is None else total + term
                out_ref[slot] = total

        over_slots(count, body)

        def clear(slot, carry):
            out_ref[slot] = jnp.zeros((size, size), jnp.float32)
            return carry

        lax.fori_loop(count, owned, clear, 0)


def update_kernel(matrix, cell, owned, kept_ref, own_ref, pair_ref, *refs):
    weight_ref, moment_ref, variance_ref = refs[:3]
    out_refs = refs[-3:]
    turn = pl.program_id(0)
    tok = lax.axis_index(TOK)
    run = weight_ref.shape[3]
    _, count = owner_count(kept_ref, matrix, tok ^ (2 * cell + turn), tok, owned)
    count = jnp.clip(count - pl.program_id(1) * run, 0, run)

    def update_from(grad_ref):
        def update(slot, carry):
            at = (0, 0, 0, slot)
            fresh = adam_step(weight_ref[at], moment_ref[at], variance_ref[at], grad_ref[slot])
            for out_ref, value in zip(out_refs, fresh):
                out_ref[at] = value
            return carry

        lax.fori_loop(0, count, update, 0)

    pl.when(turn == 0)(functools.partial(update_from, own_ref))
    pl.when(turn == 1)(functools.partial(update_from, pair_ref))

    def keep(slot, carry):
        at = (0, 0, 0, slot)
        for out_ref, value_ref in zip(out_refs, (weight_ref, moment_ref, variance_ref)):
            out_ref[at] = value_ref[at]
        return carry

    lax.fori_loop(count, run, keep, 0)


def join_kernel(pair_major, keep_ref, swap_ref, *out_refs):
    part = out_refs[0].shape[1]
    for index, out_ref in enumerate(out_refs):
        for inner in range(out_ref.shape[0]):
            group, shift = (inner, index) if pair_major else (index, inner)
            at = slice(shift * part, (shift + 1) * part)
            out_ref[inner] = keep_ref[group, at] + swap_ref[group, at]


def split_kernel(*refs):
    inner = refs[0].shape[0]
    for index, out_ref in enumerate(refs[-inner:]):
        total = refs[0][index]
        for ref in refs[1:-inner]:
            total = total + ref[index]
        out_ref[...] = total


def total_of(refs):
    total = refs[0][...]
    for ref in refs[1:]:
        total = total + ref[...]
    return total


def activate_kernel(split, *refs):
    *part_refs, hidden_ref, preact_ref = refs
    start = 0
    for side_refs in (part_refs[:split], part_refs[split:]):
        at = slice(start, start + side_refs[0].shape[1])
        start = at.stop
        preact = total_of(side_refs)
        preact_ref[:, at] = preact
        hidden_ref[:, at] = activate(preact).astype(jnp.bfloat16)


def slope_kernel(split, *refs):
    *part_refs, preact_ref, out_ref = refs
    start = 0
    for side_refs in (part_refs[:split], part_refs[split:]):
        at = slice(start, start + side_refs[0].shape[1])
        start = at.stop
        slope = gelu_slope(preact_ref[:, at])
        out_ref[:, at] = (total_of(side_refs) * slope).astype(jnp.bfloat16)


def narrow_kernel(block_ref, *out_refs):
    for turn, out_ref in enumerate(out_refs):

        @pl.when(pl.program_id(0) == turn)
        def _():
            out_ref[...] = block_ref[0, 0, 0].astype(jnp.bfloat16)


SCALARS = pl.BlockSpec(memory_space=pltpu.SMEM)
WHOLE = pl.BlockSpec(memory_space=pltpu.VMEM)
OUTSIDE = pl.BlockSpec(memory_space=pltpu.HBM)
ANYWHERE = pl.BlockSpec(memory_space=pl.ANY)


def call(kernel, outs, scalars, arrays, flops, outside=(), scratch=()):
    moved = sum(math_size(a) for a in (*arrays, *outs))
    needed = moved
    if outside:
        scratch = [pltpu.SemaphoreType.DMA((len(outside),))]
    else:
        needed += sum(math_size(x) for x in scratch)
    return pl.pallas_call(
        kernel,
        out_shape=outs,
        in_specs=[SCALARS] * len(scalars) + [WHOLE] * len(arrays) + [OUTSIDE] * len(outside),
        out_specs=[WHOLE] * len(outs),
        scratch_shapes=scratch,
        compiler_params=grant(needed),
        cost_estimate=pl.CostEstimate(flops=flops, bytes_accessed=moved, transcendentals=0),
    )(*scalars, *arrays, *outside)


def math_size(array):
    return math.prod(array.shape) * array.dtype.itemsize


def grant(needed):
    return pltpu.CompilerParams(vmem_limit_bytes=needed + VMEM_SPARE)


def on_device(inputs, cotangent, blocks, first_moment, second_moment, places, kept_counts):
    mem_count = lax.axis_size(MEM)
    tok_count = lax.axis_size(TOK)
    hid_count = lax.axis_size(HID)
    block_size = blocks.shape[-1]
    owned_slots = blocks.shape[3]
    local_slots = owned_slots * tok_count
    width_blocks = inputs.shape[1] // block_size
    hidden_span = FFW // hid_count
    rows = inputs.shape[0] * hid_count
    other = tok_count // 2
    half = rows // 2
    part = rows // tok_count
    chunks = CHUNKS
    kept = kept_counts[:, :, 0]
    place_ids = places[:, 0, 0]
    scalars = (kept, place_ids)
    f32, bf16 = jnp.float32, jnp.bfloat16

    def shift_hid(array, shift):
        return lax.ppermute(array, HID, [(i, (i + shift) % hid_count) for i in range(hid_count)])

    def shift_mem(array, shift):
        return lax.ppermute(array, MEM, [(i, (i + shift) % mem_count) for i in range(mem_count)])

    def flip_tok(array, bit):
        return lax.ppermute(array, TOK, [(i, i ^ bit) for i in range(tok_count)])

    def across(array, mem_shift, tok_shift):
        table = []
        for m in range(mem_count):
            for t in range(tok_count):
                to = ((m - mem_shift) % mem_count) * tok_count + (t ^ (2 * tok_shift))
                table.append((m * tok_count + t, to))
        return lax.ppermute(array, (MEM, TOK), table)

    def gather_rows(array):
        pieces = [array] + [shift_hid(array, k) for k in range(1, hid_count)]
        near = jnp.concatenate(pieces, axis=0)
        return [near] + [shift_mem(near, j) for j in range(1, mem_count)]

    def gather_small(array):
        found = [array] + [shift_mem(array, j) for j in range(1, mem_count)]
        own = jnp.stack(found)
        return [own] + [shift_hid(own, k) for k in range(1, hid_count)]

    def narrow(matrix, turns):
        shape = (owned_slots, block_size, block_size)
        return pl.pallas_call(
            narrow_kernel,
            grid=(len(turns),),
            out_shape=[jax.ShapeDtypeStruct(shape, bf16)] * len(turns),
            in_specs=[
                pl.BlockSpec(
                    (1, 1, 1) + blocks.shape[3:],
                    lambda i: (matrix, lax.axis_index(TOK) ^ (turns[0] + i), 0, 0, 0, 0),
                )
            ],
            out_specs=[pl.BlockSpec(shape, lambda i: (0, 0, 0))] * len(turns),
            compiler_params=grant(44 * 2**20),
        )(blocks)

    def gather_weights(matrix):
        near, far = range(2), range(2, tok_count)
        sent = [flip_tok(x, r) for r, x in zip(far, narrow(matrix, far))]
        own, pair = narrow(matrix, near)
        return [own, flip_tok(pair, 1), *sent]

    def forward(matrix, transposed, row_groups, weights):
        kernel = functools.partial(
            forward_kernel, matrix, transposed, width_blocks, tok_count, hid_count, mem_count
        )
        width = row_groups[0].shape[-1]
        outs = [
            jax.ShapeDtypeStruct((mem_count * rows, width), bf16),
            jax.ShapeDtypeStruct((mem_count, half, hidden_span), f32),
            jax.ShapeDtypeStruct((mem_count, half, hidden_span), f32),
            jax.ShapeDtypeStruct((tok_count, owned_slots, block_size, block_size), bf16),
        ]
        flops = 2 * mem_count * rows * local_slots * block_size * block_size
        return call(kernel, outs, scalars, row_groups, flops, weights)

    mem_span = hidden_span * 5 // 8

    def side_columns(kernel, outs, arrays, side, steps=3):
        whole = hidden_span - mem_span if side else mem_span
        span = whole // steps

        def spec(shape, shift):
            lead = len(shape) - 1
            return pl.BlockSpec(tuple(shape[:-1]) + (span,), lambda i: (0,) * lead + (i + shift,))

        shift = side * mem_span // span
        needed = 2 * (sum(math_size(a) for a in outs) // steps)
        needed += 2 * (sum(math_size(a) // a.shape[-1] * span for a in arrays))
        return pl.pallas_call(
            kernel,
            grid=(steps,),
            out_shape=outs,
            in_specs=[spec(a.shape, shift) for a in arrays],
            out_specs=[spec(o.shape, 0) for o in outs],
            compiler_params=grant(needed),
            cost_estimate=pl.CostEstimate(
                flops=sum(math.prod(o.shape) for o in outs) * 2,
                bytes_accessed=needed * steps // 2,
                transcendentals=0,
            ),
        )(*arrays)

    def reduce_plane(keep, send):
        swap = flip_tok(send, 1)

        def array(side, *lead):
            return jax.ShapeDtypeStruct((*lead, hidden_span - mem_span if side else mem_span), f32)

        kernel = functools.partial(join_kernel, False)
        outs = [array(0, other, part)] * mem_count
        by_mem = side_columns(kernel, outs, [keep, swap], 0)
        kernel = functools.partial(join_kernel, True)
        outs = [array(1, mem_count, part)] * other
        by_pair = side_columns(kernel, outs, [keep, swap], 1)
        mem_terms = [by_mem[0]] + [shift_mem(by_mem[j], -j) for j in range(1, mem_count)]
        pair_terms = [by_pair[0]] + [flip_tok(by_pair[b], 2 * b) for b in range(1, other)]
        mine, *rest = call(split_kernel, [array(0, part)] * other, (), mem_terms, part)
        first = [mine] + [flip_tok(x, 2 * b) for b, x in enumerate(rest, 1)]
        mine, *rest = call(split_kernel, [array(1, part)] * mem_count, (), pair_terms, part)
        second = [mine] + [shift_mem(x, -j) for j, x in enumerate(rest, 1)]
        return first, second

    peers = [(j, b) for j in range(mem_count) for b in range(other)][1:]

    def gather_plane(piece):
        found = {(0, 0): piece}
        for j, b in peers:
            found[(-j) % mem_count, b] = across(piece, j, b)
        near = jnp.concatenate(
            [found[j, b] for j in range(mem_count) for b in range(other)], axis=0
        ).reshape(mem_count, half, hidden_span)
        return near, flip_tok(near, 1)

    def backward(matrix, transposed, near, far, weights):
        kernel = functools.partial(backward_kernel, matrix, transposed, width_blocks, mem_count)
        span = inputs.shape[1] // chunks
        outs = [jax.ShapeDtypeStruct((rows, span), f32)] * (mem_count * chunks)
        flops = 2 * mem_count * rows * local_slots * block_size * block_size
        scratch = [pltpu.VMEM((mem_count * rows, inputs.shape[1]), f32)]
        arrays = [near, far, weights]
        return call(kernel, outs, scalars, arrays, flops, (), scratch)

    turn = relative(tok_count)
    step = inputs.shape[0]

    def spot_of(k):
        start = k * step
        return ((start // part) ^ turn) * part + start % part

    def mem_first(groups):
        total = groups[0]
        for j in range(1, mem_count):
            total = total + shift_mem(groups[j], -j)
        result = lax.dynamic_slice_in_dim(total, spot_of(0), step, 0)
        for k in range(1, hid_count):
            piece = lax.dynamic_slice_in_dim(total, spot_of(k), step, 0)
            result = result + shift_hid(piece, -k)
        return result.astype(bf16)

    def hid_first(groups):
        def rows_of(k):
            return jnp.stack([lax.dynamic_slice_in_dim(g, spot_of(k), step, 0) for g in groups])

        total = rows_of(0)
        for k in range(1, hid_count):
            total = total + shift_hid(rows_of(k), -k)
        result = total[0]
        for j in range(1, mem_count):
            result = result + shift_mem(total[j], -j)
        return result.astype(bf16)

    def reduce_rows(found, hid_chunks=0):
        results = []
        for chunk in range(chunks):
            groups = found[chunk * mem_count : (chunk + 1) * mem_count]
            if chunk < chunks - hid_chunks:
                results.append(mem_first(groups))
            else:
                results.append(hid_first(groups))
        return jnp.concatenate(results, axis=1)

    def gradient(matrix, cell, ids, row_values, near, far):
        kernel = functools.partial(gradient_kernel, matrix, cell, width_blocks, mem_count)
        outs = [jax.ShapeDtypeStruct((owned_slots, block_size, block_size), f32)] * 2
        flops = 2 * mem_count * rows * owned_slots * 2 * block_size * block_size
        keep, send = call(kernel, outs, (kept, ids), [row_values, near, far], flops)
        return keep, flip_tok(send, 1)

    def update(matrix, cell, grads, held):
        splits = 1
        run = owned_slots // splits
        state_spec = pl.BlockSpec(
            (1, 1, 1, run, block_size, block_size),
            lambda i, j: (matrix, lax.axis_index(TOK) ^ (2 * cell + i), 0, j, 0, 0),
        )
        own_spec = pl.BlockSpec(
            (run, block_size, block_size), lambda i, j: (jnp.where(i == 0, j, splits - 1), 0, 0)
        )
        pair_spec = pl.BlockSpec(
            (run, block_size, block_size), lambda i, j: (jnp.where(i == 0, 0, j), 0, 0)
        )
        state = (blocks, first_moment, second_moment)
        size = 2 * owned_slots * block_size * block_size
        return pl.pallas_call(
            functools.partial(update_kernel, matrix, cell, owned_slots),
            grid=(2, splits),
            out_shape=[jax.ShapeDtypeStruct(s.shape, f32) for s in state],
            in_specs=[SCALARS, own_spec, pair_spec] + [state_spec] * 3 + [ANYWHERE] * len(held),
            out_specs=[state_spec] * 3,
            input_output_aliases={6 + i: i for i in range(len(held))},
            compiler_params=grant(44 * 2**20),
            cost_estimate=pl.CostEstimate(
                flops=size * 12, bytes_accessed=size * 28, transcendentals=size
            ),
        )(kept, *grads, *state, *held)

    far_place_ids = flip_tok(place_ids, 2)
    input_groups = gather_rows(inputs)
    weights_first = gather_weights(0)
    cotangent_groups = gather_small(cotangent)
    weights_second = gather_weights(1)
    token_rows, *pre_part, weights_first = forward(0, False, input_groups, weights_first)
    pre_terms = reduce_plane(*pre_part)
    grad_rows, *back_part, weights_second = forward(1, True, cotangent_groups, weights_second)
    back_terms = reduce_plane(*back_part)
    piece = (part, hidden_span)
    outs = [jax.ShapeDtypeStruct(piece, bf16), jax.ShapeDtypeStruct(piece, f32)]
    kernel = functools.partial(activate_kernel, len(pre_terms[0]))
    hidden_piece, preact = call(kernel, outs, (), [*pre_terms[0], *pre_terms[1]], part)
    hidden = gather_plane(hidden_piece)
    kernel = functools.partial(slope_kernel, len(back_terms[0]))
    arrays = [*back_terms[0], *back_terms[1], preact]
    (grad_piece,) = call(kernel, outs[:1], (), arrays, part)
    pre_grad = gather_plane(grad_piece)
    layer_out = reduce_rows(backward(1, False, *hidden, weights_second), 1)
    grad_in = reduce_rows(backward(0, True, *pre_grad, weights_first))
    far_grad_rows = flip_tok(grad_rows, 2)
    far_token_rows = flip_tok(token_rows, 2)
    grads = gradient(1, 0, place_ids, grad_rows, *hidden)
    state = update(1, 0, grads, ())
    grads = gradient(0, 0, place_ids, token_rows, *pre_grad)
    state = update(0, 0, grads, state)
    grads = gradient(1, 1, far_place_ids, far_grad_rows, *hidden)
    state = update(1, 1, grads, state)
    grads = gradient(0, 1, far_place_ids, far_token_rows, *pre_grad)
    return (layer_out, grad_in, *update(0, 1, grads, state))


def solution(mesh):
    return jax.shard_map(
        on_device,
        mesh=mesh,
        in_specs=(
            P((MEM, HID), TOK),
            P((MEM, HID), TOK),
            P(None, None, HID, (MEM, TOK), None, None),
            P(None, None, HID, (MEM, TOK), None, None),
            P(None, None, HID, (MEM, TOK), None, None),
            P(None, TOK, HID, None),
            P(None, None, HID),
        ),
        out_specs=(
            P((MEM, HID), TOK),
            P((MEM, HID), TOK),
            P(None, None, HID, (MEM, TOK), None, None),
            P(None, None, HID, (MEM, TOK), None, None),
            P(None, None, HID, (MEM, TOK), None, None),
        ),
        check_vma=False,
    )
```
